256 devices in a mesh: seq: 64 (over z, y, core), tp: 4 (over x).
Axes of the slice: x: 4, y: 4, z: 8, core: 2. Of those that a mesh axis runs over, the one named last changes fastest.
Arguments:
- patches: bfloat16 [64, 256, 1408], P('seq'), may hold values from -6 to 6
- picture_grid: int32 [64, 2], P('seq'), may hold values from 4 to 8, as said below
- vision_qkv: bfloat16 [1408, 3, 1408], P(None, None, 'tp')
- vision_out: bfloat16 [1408, 1408], P('tp'), may hold values from -0.15625 to 0.15625
- merge_weight: bfloat16 [4, 1408, 1408], P('tp'), may hold values from -0.078125 to 0.078125
- picture_block: int32 [64], P('seq'), may hold values from 0 to 63, as said below
- picture_offset: int32 [64], P('seq'), may hold values from 0 to 112, as said below
- tokens: bfloat16 [8192, 1408], P('seq', 'tp'), may hold values from -6 to 6
- prompt_lengths: int32 [16], replicated, may hold values from 1 to 2048, 8192 in all
- text_qkv: bfloat16 [1408, 3, 1408], P(None, None, 'tp')
- text_out: bfloat16 [1408, 1408], P('tp'), may hold values from -0.15625 to 0.15625
Outputs:
- hidden_out: bfloat16 [8192, 1408], P('seq')
The draws below stay inside these ranges and needn't reach their ends.
Inputs may be any that keep to these rules, and one draw needn't show every extreme that they name: `picture_grid`: some picture has both entries equal to 8, another both equal to 4. `picture_block`: the blocks of different pictures differ. picture_offset plus the product of the picture's two picture_grid entries is at most 128. `prompt_lengths`: the lengths sum to 8192.
All inputs are finite; a program needn't handle non-finite values.
Results may differ from the reference program's by a relative error of at most 0.018.
Values may be sent and summed in bfloat16 or wider, within the bound.
No kernel may reach another device: no remote copies, remote signals or barrier semaphores. Data moves between devices by JAX's collectives and lax.ppermute only.
A program may use at most 64 MiB of HBM per device.

```python
import math
import jax
import jax.numpy as jnp
import numpy as np
from jax import lax

D = 1408
HEADS = 16
HEAD = 88
MAXGRID = 16
BLOCK = 128
PROMPTS = 16
PATCHES = 256
MERGED = 64
PICTURES = 64
TOKENS = 8192
NBLOCKS = 64


def chosen_pictures(key):
    fullest = jax.random.randint(jax.random.fold_in(key, 12), (), 0, PICTURES)
    step = jax.random.randint(jax.random.fold_in(key, 15), (), 1, PICTURES)
    smallest = (fullest + step) % PICTURES
    return (fullest, smallest)


def grid_sides(key):
    halves = MAXGRID // 2
    lowest = MAXGRID // 4
    sides = jax.random.randint(jax.random.fold_in(key, 11), (PICTURES, 2), lowest, halves + 1)
    fullest, smallest = chosen_pictures(key)
    indices = jnp.arange(PICTURES)
    sides = jnp.where((indices == fullest)[:, None], halves, sides)
    return jnp.where((indices == smallest)[:, None], lowest, sides)


def draw_picture_grid(key, part):
    return grid_sides(key).astype(jnp.int32)


def draw_picture_block(key, part):
    order = jax.random.permutation(jax.random.fold_in(key, 13), NBLOCKS)
    return order[:PICTURES].astype(jnp.int32)


def draw_picture_offset(key, part):
    sides = grid_sides(key)
    room = BLOCK - sides[:, 0] * sides[:, 1] + 1
    offsets = jax.random.randint(jax.random.fold_in(key, 14), (PICTURES,), 0, room)
    fullest, smallest = chosen_pictures(key)
    indices = jnp.arange(PICTURES)
    offsets = jnp.where(indices == fullest, 0, offsets)
    offsets = jnp.where(indices == smallest, room - 1, offsets)
    return offsets.astype(jnp.int32)


def projection_draw(key):
    values = jax.random.normal(key, (D, 3, D), jnp.float32) * D ** (-0.5)
    return values.astype(jnp.bfloat16)


def draw_vision_qkv(key, part):
    return projection_draw(jax.random.fold_in(key, 21))


def draw_text_qkv(key, part):
    return projection_draw(jax.random.fold_in(key, 22))


def shard_levels(own_key, dims, cuts, low, high):
    def one(position, shards_of):
        steps = jax.random.uniform(jax.random.fold_in(jax.random.fold_in(own_key, 6), position), (shards_of,), jnp.float32, low / len(cuts), high / len(cuts))
        return jnp.repeat(jnp.exp(steps), dims[position] // shards_of).reshape((-1,) + (1,) * (len(dims) - position - 1))

    level = one(*cuts[0])
    for cut in cuts[1:]:
        level = level * one(*cut)
    return level


def length_profile(number_of, total, limit, slope):
    weights = [(1 << 20) // math.isqrt(standing ** slope) + 1 for standing in range(2, number_of + 1)]
    rest, given = total - limit - (number_of - 1), [1] * (number_of - 1)
    while rest > 0:
        free = [i for i in range(number_of - 1) if given[i] < limit]
        whole, budget = sum([weights[i] for i in free]), rest
        for i in free:
            addition = min(limit - given[i], max(1, budget * weights[i] // whole), rest)
            given[i] = given[i] + addition
            rest = rest - addition
    return np.array([limit] + given)


def uneven_parts(own_key, number_of, total, bound, slope):
    if number_of == 2:
        one = jax.random.randint(own_key, (), max(1, total - bound), min(bound, total - 1) + 1)
        return jnp.stack([one, total - one])
    sizes = jnp.asarray(length_profile(number_of, total, bound, slope), jnp.int32)
    twos = (number_of - 1) // 2
    donor, sink = sizes[1:1 + 2 * twos:2], sizes[2:2 + 2 * twos:2]
    room = jnp.minimum(donor - 1, bound - sink)
    moved = jax.random.randint(jax.random.fold_in(own_key, 1), (twos,), 0, 1 << 20) % (room + 1)
    sizes = sizes.at[1:1 + 2 * twos:2].set(donor - moved).at[2:2 + 2 * twos:2].set(sink + moved)
    return sizes[jax.random.permutation(jax.random.fold_in(own_key, 2), number_of)]


def bell_draw(stream_key, shape, scale, most, pieces=(), kind=jnp.bfloat16):
    result = scale * jax.random.normal(stream_key, shape, jnp.float32)
    if pieces:
        result = result * shard_levels(stream_key, shape, pieces, -0.22, 0.18)
    return jnp.clip(result, -most, most).astype(kind)


def setup_inputs(seed: int = 0) -> dict:
    keys = jax.random.split(jax.random.key(seed), 12)
    patches = bell_draw(keys[0], (PICTURES, PATCHES, D), 1.0, 6.0, ((0, 64),))
    picture_grid = draw_picture_grid(jax.random.fold_in(keys[11], 71), 0)
    vision_qkv = draw_vision_qkv(jax.random.fold_in(keys[11], 71), 0)
    vision_out = bell_draw(keys[3], (D, D), D ** -0.5, 0.15625, ((0, 4),))
    merge_weight = bell_draw(keys[4], (4, D, D), (4 * D) ** -0.5, 0.078125, ((0, 4),))
    picture_block = draw_picture_block(jax.random.fold_in(keys[11], 71), 0)
    picture_offset = draw_picture_offset(jax.random.fold_in(keys[11], 71), 0)
    tokens = bell_draw(keys[7], (TOKENS, D), 1.0, 6.0, ((0, 64), (1, 4)))
    prompt_lengths = uneven_parts(keys[8], PROMPTS, TOKENS, TOKENS // 4, 2).astype(jnp.int32)
    text_qkv = draw_text_qkv(jax.random.fold_in(keys[11], 71), 0)
    text_out = bell_draw(keys[10], (D, D), D ** -0.5, 0.15625, ((0, 4),))
    return {"patches": patches, "picture_grid": picture_grid, "vision_qkv": vision_qkv, "vision_out": vision_out, "merge_weight": merge_weight, "picture_block": picture_block, "picture_offset": picture_offset, "tokens": tokens, "prompt_lengths": prompt_lengths, "text_qkv": text_qkv, "text_out": text_out}


EPSILON = 1e-06
MASKED = -1e+30

def normalize(values):
    values = values.astype(jnp.float32)
    centre = lax.optimization_barrier(jnp.mean(values, axis=-1, keepdims=True))
    shifted = values - centre
    spread = lax.optimization_barrier(jnp.mean(shifted * shifted, axis=-1, keepdims=True))
    return (shifted * lax.rsqrt(spread + EPSILON)).astype(jnp.bfloat16)

def softmax_context(scores, allowed, value_rows):
    scores = jnp.where(allowed, scores, MASKED)
    row_max = lax.optimization_barrier(jnp.max(scores, axis=-1, keepdims=True))
    expons = jnp.where(allowed, jnp.exp(scores - row_max), 0.0)
    row_total = lax.optimization_barrier(jnp.sum(expons, axis=-1))
    weights = expons.astype(jnp.bfloat16)
    summed = jnp.einsum('hqk,khe->qhe', weights.astype(jnp.float32), value_rows.astype(jnp.float32))
    context = summed / jnp.transpose(row_total)[:, :, None]
    return context.astype(jnp.bfloat16).reshape(context.shape[0], -1)

def merge_cells(normed):
    halves = MAXGRID // 2
    shaped = normed.reshape(halves, 2, halves, 2, normed.shape[-1])
    return shaped.transpose(0, 2, 1, 3, 4).reshape(halves * halves, 4, normed.shape[-1])

def merged_positions(half_grid, block_index, offset):
    halves = MAXGRID // 2
    cells = jnp.arange(MERGED, dtype=jnp.int32)
    row_cell = cells // halves
    col_cell = cells % halves
    usable = (row_cell < half_grid[0]) & (col_cell < half_grid[1])
    target = block_index * BLOCK + offset + row_cell * half_grid[1] + col_cell
    return jnp.where(usable, target, -1).astype(jnp.int32)

def prompt_starts(prompt_lengths, positions):
    ends = jnp.cumsum(prompt_lengths).astype(jnp.int32)
    picked = jnp.where(ends[None, :] <= positions[:, None], prompt_lengths[None, :], 0)
    return lax.optimization_barrier(jnp.sum(picked, axis=1)).astype(jnp.int32)

def picture_layer(picture, half_grid, vision_qkv, vision_out, merge_weight):
    normed = normalize(picture)
    projected = jnp.dot(normed, vision_qkv.reshape(D, 3 * D), preferred_element_type=jnp.float32)
    projected = projected.astype(jnp.bfloat16).reshape(PATCHES, 3, HEADS, HEAD)
    scores = jnp.einsum('qhe,khe->hqk', projected[:, 0].astype(jnp.float32), projected[:, 1].astype(jnp.float32)) * HEAD ** (-0.5)
    cells = jnp.arange(PATCHES, dtype=jnp.int32)
    usable = (cells // MAXGRID < 2 * half_grid[0]) & (cells % MAXGRID < 2 * half_grid[1])
    context = softmax_context(scores, usable[None, None, :], projected[:, 2])
    hidden = picture.astype(jnp.float32) + jnp.dot(context, vision_out, preferred_element_type=jnp.float32)
    merged_in = merge_cells(normalize(hidden))
    merged = jnp.dot(merged_in.reshape(MERGED, 4 * D), merge_weight.reshape(4 * D, D), preferred_element_type=jnp.float32)
    return merged.astype(jnp.bfloat16)

def reference(patches, picture_grid, vision_qkv, vision_out, merge_weight, picture_block, picture_offset, tokens, prompt_lengths, text_qkv, text_out):

    def one_picture(index):
        return picture_layer(patches[index], picture_grid[index], vision_qkv, vision_out, merge_weight)
    merged = lax.map(one_picture, jnp.arange(PICTURES, dtype=jnp.int32))
    targets = jax.vmap(merged_positions)(picture_grid, picture_block, picture_offset).reshape(-1)
    targets = jnp.where(targets >= 0, targets, TOKENS)
    prompt_in = tokens.at[targets].set(merged.reshape(-1, D), mode='drop')
    normed = normalize(prompt_in)
    projected = jnp.dot(normed, text_qkv.reshape(D, 3 * D), preferred_element_type=jnp.float32)
    projected = projected.astype(jnp.bfloat16).reshape(TOKENS, 3, HEADS, HEAD)
    starts = prompt_starts(prompt_lengths, jnp.arange(TOKENS, dtype=jnp.int32))
    key_rows = projected[:, 1].astype(jnp.float32)
    value_rows = projected[:, 2]
    key_pos = jnp.arange(TOKENS, dtype=jnp.int32)

    def block_context(index):
        first = (index * BLOCK).astype(jnp.int32)
        query_rows = lax.dynamic_slice_in_dim(projected[:, 0], first, BLOCK, 0).astype(jnp.float32)
        query_pos = first + jnp.arange(BLOCK, dtype=jnp.int32)
        query_start = lax.dynamic_slice_in_dim(starts, first, BLOCK, 0)
        allowed = (key_pos[None, :] <= query_pos[:, None]) & (key_pos[None, :] >= query_start[:, None])
        scores = jnp.einsum('qhe,khe->hqk', query_rows, key_rows) * HEAD ** (-0.5)
        return softmax_context(scores, allowed[None], value_rows)
    contexts = lax.map(block_context, jnp.arange(TOKENS // BLOCK, dtype=jnp.int32))
    context = contexts.reshape(TOKENS, D)
    output = prompt_in.astype(jnp.float32) + jnp.dot(context, text_out, preferred_element_type=jnp.float32)
    return output.astype(jnp.bfloat16)
```

```python
import jax
import jax.numpy as jnp
import numpy as np
from jax import lax
from jax.sharding import Mesh
from jax.sharding import PartitionSpec as P

HEAD = 88
MAXGRID = 16
BLOCK = 128
MERGED = 64
EPSILON = 1e-06
MASKED = -1e30
SCALE = HEAD ** (-0.5)
BF = jnp.bfloat16
F32 = jnp.float32


def ahead(x, axis, by):
    count = lax.axis_size(axis)
    return lax.ppermute(x, axis, [(i, i + by) for i in range(count - by)])


def around(x, axis, by):
    count = lax.axis_size(axis)
    return lax.ppermute(x, axis, [(i, (i + by) % count) for i in range(count)])


def gather_ring(x, axis):
    count = lax.axis_size(axis)
    me = lax.axis_index(axis)
    out = jnp.zeros((count,) + x.shape, x.dtype)
    out = lax.dynamic_update_index_in_dim(out, x, me, 0)
    for by in range(1, count):
        got = around(x, axis, by)
        out = lax.dynamic_update_index_in_dim(out, got, (me - by) % count, 0)
    return out


def normalize(values, axis=-1):
    values = values.astype(F32)
    centre = jnp.mean(values, axis=axis, keepdims=True)
    shifted = values - centre
    spread = jnp.mean(shifted * shifted, axis=axis, keepdims=True)
    return (shifted * lax.rsqrt(spread + EPSILON)).astype(BF)


def vision_share(picture, half_grid, vision_qkv, vision_out):
    width, _, local_width = vision_qkv.shape
    heads = local_width // HEAD
    count = picture.shape[0]
    normed = normalize(picture)
    projected = jnp.dot(
        normed, vision_qkv.reshape(width, 3 * local_width), preferred_element_type=F32
    )
    projected = projected.astype(BF).reshape(count, 3, heads, HEAD)
    scores = (
        jnp.einsum("qhe,khe->hqk", projected[:, 0], projected[:, 1], preferred_element_type=F32)
        * SCALE
    )
    cells = jnp.arange(count, dtype=jnp.int32)
    usable = (cells // MAXGRID < 2 * half_grid[0]) & (cells % MAXGRID < 2 * half_grid[1])
    allowed = usable[None, None, :]
    scores = jnp.where(allowed, scores, MASKED)
    row_max = jnp.max(scores, axis=-1, keepdims=True)
    expons = jnp.where(allowed, jnp.exp(scores - row_max), 0.0)
    row_total = jnp.sum(expons, axis=-1)
    summed = jnp.einsum(
        "hqk,khe->qhe", expons.astype(BF), projected[:, 2], preferred_element_type=F32
    )
    context = (summed / jnp.transpose(row_total)[:, :, None]).astype(BF)
    context = context.reshape(8, 2, 8, 2, local_width).transpose(1, 3, 0, 2, 4)
    context = context.reshape(count, local_width)
    share = jnp.dot(context, vision_out, preferred_element_type=F32).astype(BF)
    return share.reshape(4, MERGED, width)


def local(
    patches,
    picture_grid,
    vision_qkv,
    vision_out,
    merge_weight,
    picture_block,
    picture_offset,
    tokens,
    prompt_lengths,
    text_qkv,
    text_out,
):
    width = patches.shape[2]
    local_width = vision_qkv.shape[2]
    heads = local_width // HEAD
    z = lax.axis_index("z")
    c = lax.axis_index("c")
    t = lax.axis_index("t")
    half_grid = picture_grid[0]
    block = picture_block[0]
    offset = picture_offset[0]
    picture = patches[0]

    token_parts = gather_ring(tokens, "t")
    out_full = gather_ring(text_out, "t")

    shares = vision_share(picture, half_grid, vision_qkv, vision_out)
    shares = lax.all_to_all(shares, "t", 0, 0, tiled=True)
    own = picture.reshape(8, 2, 8, 2, width).transpose(1, 3, 0, 2, 4).reshape(4, MERGED, width)
    own = lax.dynamic_index_in_dim(own, t, 0, keepdims=False)
    hidden = own.astype(F32) + jnp.sum(shares.astype(F32), axis=0)
    merged = jnp.dot(normalize(hidden), merge_weight[0], preferred_element_type=F32).astype(BF)

    facts = jnp.stack([block, offset, half_grid[0], half_grid[1], jnp.int32(1)])
    facts = jnp.where(t == 0, facts, 0).astype(BF)
    facts = jnp.pad(facts, (0, 123))
    rows = jnp.concatenate([merged, jnp.broadcast_to(facts, (MERGED, 128))], axis=1)
    wide = width + 128
    rows = rows.reshape(1, 4, 16, wide)
    to_y = (block % 8) // 2
    routed = jnp.where(jnp.arange(4)[:, None, None, None] == to_y, rows, jnp.zeros((), BF))
    got = lax.all_to_all(routed.reshape(16, 16, wide), ("y", "t"), 0, 0, tiled=True)
    got = jnp.sum(got.reshape(4, 4, 16, wide).astype(F32), axis=1).astype(BF)
    got = lax.all_gather(got, "c", axis=0, tiled=True)
    to = got[:, 0, width].astype(F32).astype(jnp.int32)
    there = got[:, 0, width + 4] > 0
    pick = there & (to % 2 == c)
    pick = pick[None, :] & (to[None, :] // 8 == jnp.arange(8)[:, None])
    routed = jnp.einsum("zk,krd->zrd", pick.astype(BF), got, preferred_element_type=F32).astype(BF)
    got = lax.all_to_all(routed, "z", 0, 0, tiled=True)
    got = jnp.sum(got.astype(F32), axis=0).astype(BF)
    got = gather_ring(got, "t").reshape(MERGED, wide)

    facts = got[0, width:].astype(F32).astype(jnp.int32)
    cells = jnp.arange(MERGED, dtype=jnp.int32)
    target = facts[1] + (cells // 8) * facts[3] + cells % 8
    usable = (cells // 8 < facts[2]) & (cells % 8 < facts[3]) & (facts[4] > 0)
    target = jnp.where(usable, target, -1)
    table = jnp.arange(BLOCK, dtype=jnp.int32)[:, None] == target[None, :]
    placed = jnp.dot(table.astype(BF), got[:, :width], preferred_element_type=F32).astype(BF)
    covered = jnp.any(table, axis=1)
    own_tokens = token_parts.transpose(1, 0, 2).reshape(BLOCK, width)
    prompt_in = jnp.where(covered[:, None], placed, own_tokens)

    normed = normalize(prompt_in)
    projected = jnp.einsum("td,dce->cet", normed, text_qkv, preferred_element_type=F32).astype(BF)
    projected = projected.reshape(3, heads, HEAD, BLOCK).transpose(1, 0, 2, 3)
    projected = lax.all_to_all(projected, "y", 0, 0, tiled=True)
    queries = projected[:, 0]
    pairs = projected[:, 1:]
    pairs = jnp.stack([pairs, ahead(pairs, "z", 1), ahead(pairs, "z", 2)])
    pairs = lax.all_gather(pairs, "c", axis=0, tiled=False)
    keys = pairs[:, :, :, 0].transpose(3, 0, 1, 2, 4).reshape(HEAD, -1)
    values = pairs[:, :, :, 1].transpose(3, 0, 1, 2, 4).reshape(HEAD, -1)
    lanes = jnp.arange(BLOCK, dtype=jnp.int32)
    planes = jnp.arange(3, dtype=jnp.int32)[None, :, None, None]
    rows_y = jnp.arange(4, dtype=jnp.int32)
    cores = jnp.arange(2, dtype=jnp.int32)[:, None, None, None]
    key_pos = (z - planes) * 1024 + rows_y[None, None, :, None] * 256 + cores * 128 + lanes
    key_pos = key_pos.reshape(-1)
    query_pos = (z * 1024 + rows_y[:, None] * 256 + c * 128 + lanes[None, :]).reshape(-1)
    ends = jnp.cumsum(prompt_lengths)
    starts = jnp.max(jnp.where(ends[None, :] <= query_pos[:, None], ends[None, :], 0), axis=1)
    visible = (key_pos[None, :] <= query_pos[:, None]) & (key_pos[None, :] >= starts[:, None])
    queries = queries.transpose(0, 2, 1).reshape(4 * BLOCK, HEAD)
    scores = jnp.dot(queries, keys, preferred_element_type=F32) * SCALE
    scores = jnp.where(visible, scores, MASKED)
    top = jnp.max(scores, axis=1, keepdims=True)
    expons = jnp.where(visible, jnp.exp(scores - top), 0.0)
    total = jnp.sum(expons, axis=1, keepdims=True)
    summed = lax.dot_general(
        expons.astype(BF), values, (((1,), (1,)), ((), ())), preferred_element_type=F32
    )
    context = (summed / total).astype(BF).reshape(4, BLOCK, HEAD).transpose(0, 2, 1)
    sent = jnp.broadcast_to(context[None], (4, 4, HEAD, BLOCK)).reshape(16, HEAD, BLOCK)
    context = lax.all_to_all(sent, ("t", "y"), 0, 0, tiled=True).reshape(width, BLOCK)
    gained = lax.dot_general(
        context, out_full.reshape(width, width), (((0,), (0,)), ((), ())), preferred_element_type=F32
    )
    return (prompt_in.astype(F32) + gained).astype(BF)


def solution(mesh):
    split = Mesh(np.asarray(mesh.devices).reshape(8, 4, 2, 4), ("z", "y", "c", "t"))
    seq = ("z", "y", "c")
    placed = (
        P(seq, None, None),
        P(seq, None),
        P(None, None, "t"),
        P("t", None),
        P("t", None, None),
        P(seq),
        P(seq),
        P(seq, "t"),
        P(),
        P(None, None, "t"),
        P("t", None),
    )
    return jax.shard_map(
        local, mesh=split, in_specs=placed, out_specs=P(seq, None), check_vma=False
    )
```

```python
import jax
import jax.numpy as jnp
import numpy as np
from jax import lax
from jax.experimental import pallas as pl
from jax.experimental.pallas import tpu as pltpu
from jax.sharding import Mesh
from jax.sharding import PartitionSpec as P

HEAD = 88
MAXGRID = 16
BLOCK = 128
MERGED = 64
EPSILON = 1e-06
SCALE = HEAD ** (-0.5)
BF = jnp.bfloat16
F32 = jnp.float32
I32 = jnp.int32
VMEM = pltpu.VMEM
SMEM = pltpu.SMEM
FACTS = 128
WINDOW = 18 * BLOCK


def ahead(x, axis, by):
    count = lax.axis_size(axis)
    return lax.ppermute(x, axis, [(i, i + by) for i in range(count - by)])


def around(x, axis, by):
    count = lax.axis_size(axis)
    return lax.ppermute(x, axis, [(i, (i + by) % count) for i in range(count)])


def call(kernel, out_shape, spaces, scratch=()):
    single = not isinstance(out_shape, (list, tuple))
    outs = pl.BlockSpec(memory_space=VMEM)
    return pl.pallas_call(
        kernel,
        out_shape=out_shape,
        in_specs=[pl.BlockSpec(memory_space=s) for s in spaces],
        out_specs=outs if single else [outs] * len(out_shape),
        scratch_shapes=scratch,
        compiler_params=pltpu.CompilerParams(vmem_limit_bytes=48 << 20),
    )


def shape(dims, dtype=BF):
    return jax.ShapeDtypeStruct(dims, dtype)


def iota(dims, axis):
    return lax.broadcasted_iota(I32, dims, axis)


def dot(a, b, over):
    return lax.dot_general(
        a, b, (((over[0],), (over[1],)), ((), ())), preferred_element_type=F32
    )


def normalize(values):
    centre = jnp.mean(values, axis=-1, keepdims=True)
    shifted = values - centre
    spread = jnp.mean(shifted * shifted, axis=-1, keepdims=True)
    return (shifted * lax.rsqrt(spread + EPSILON)).astype(BF)


def slot_of(row):
    i, j = row // 128, (row // 64) % 2
    a, b = (row // 8) % 8, row % 8
    return (2 * a + i) * MAXGRID + 2 * b + j


def vision_kernel(grid_ref, picture_ref, qkv_ref, out_ref, share_ref):
    count = picture_ref.shape[0]
    local_width = qkv_ref.shape[1]
    normed = normalize(picture_ref[...].astype(F32))
    queries = dot(qkv_ref[0], normed, (1, 1))
    keys = dot(qkv_ref[1], normed, (1, 1))
    values = dot(qkv_ref[2], normed, (1, 1))
    slots = iota((count, 1), 0)
    usable = (slots // MAXGRID < 2 * grid_ref[0, 0]) & (slots % MAXGRID < 2 * grid_ref[0, 1])
    contexts = []
    for first in range(0, local_width, HEAD):
        q, k, v = (x[first : first + HEAD].astype(BF) for x in (queries, keys, values))
        scores = dot(k, q, (0, 0)) * SCALE
        scores = jnp.where(usable, scores, -jnp.inf)
        expons = jnp.exp(scores - jnp.max(scores, axis=0, keepdims=True))
        total = jnp.sum(expons, axis=0, keepdims=True)
        contexts.append(dot(v, expons.astype(BF), (1, 0)) / total)
    context = jnp.concatenate(contexts, axis=0).astype(BF)
    order = slot_of(iota((count, count), 0)) == iota((count, count), 1)
    context = dot(order.astype(BF), context, (1, 1)).astype(BF)
    share_ref[...] = dot(context, out_ref[...], (1, 0)).astype(BF)


def merge_kernel(facts_ref, own_ref, shares_ref, weight_ref, rows_ref):
    width = own_ref.shape[1]
    hidden = own_ref[...].astype(F32)
    gained = shares_ref[0].astype(F32)
    for other in range(1, 4):
        gained = gained + shares_ref[other].astype(F32)
    merged = dot(normalize(hidden + gained), weight_ref[...], (1, 0)).astype(BF)
    lane = iota((MERGED, FACTS), 1)
    facts = jnp.zeros((MERGED, FACTS), I32)
    for index in range(5):
        facts = jnp.where(lane == index, facts_ref[index], facts)
    facts = facts.astype(F32).astype(BF)
    for y in range(4):
        here = facts_ref[5] == y
        rows_ref[y, :, :width] = jnp.where(here, merged, jnp.zeros_like(merged))
        rows_ref[y, :, width:] = jnp.where(here, facts, jnp.zeros_like(facts))


def project_kernel(rows_ref, tokens_ref, qkv_ref, prompt_ref, heads_ref):
    width = tokens_ref.shape[1]
    facts = rows_ref[:, width:].astype(F32)
    cell = iota((MERGED, 1), 0)
    a, b = (cell // 8).astype(F32), (cell % 8).astype(F32)
    offset, high, wide, there = (facts[:, i : i + 1] for i in (1, 2, 3, 4))
    target = offset + a * wide + b
    usable = (a < high) & (b < wide) & (there > 0.0)
    target = jnp.where(usable, target, -1.0)
    table = (target == iota((MERGED, BLOCK), 1).astype(F32)).astype(BF)
    placed = dot(table, rows_ref[...], (0, 0))
    covered = placed[:, width + 4 : width + 5] > 0.0
    prompt = jnp.where(covered, placed[:, :width], tokens_ref[...].astype(F32))
    prompt_ref[...] = prompt.astype(BF)
    normed = normalize(prompt)
    for part in range(3):
        projected = dot(qkv_ref[part], normed, (1, 1)).astype(F32)
        for head in range(4):
            heads_ref[head, part] = projected[head * HEAD : (head + 1) * HEAD].astype(BF)


def attend_kernel(facts_ref, lengths_ref, own_ref, near_ref, far_ref,
                  own2_ref, near2_ref, far2_ref, sent_ref, keys_ref, values_ref):
    z, c = facts_ref[0], facts_ref[1]
    for plane, (mine, other) in enumerate(
        ((far_ref, far2_ref), (near_ref, near2_ref), (own_ref, own2_ref))
    ):
        skip = 1 if plane == 2 else 0
        for y in range(4):
            at = (plane * 8 + 2 * y) * BLOCK
            for half in range(2):
                lanes = pl.ds(at + half * BLOCK, BLOCK)
                for part, store in ((0, keys_ref), (1, values_ref)):
                    picked = jnp.where(
                        c == half, mine[y, skip + part], other[y, part]
                    )
                    store[:, lanes] = picked
    row = iota((BLOCK, 1), 0)
    column = iota((BLOCK, WINDOW), 1)
    for j in range(4):
        base = (z - 2) * 1024 + j * 256
        here = 2048 + c * BLOCK + row
        start = jnp.zeros((BLOCK, 1), I32)
        end = jnp.int32(0)
        for prompt in range(16):
            end = end + lengths_ref[prompt]
            start = jnp.where(end <= here + base, end, start)
        query = own_ref[j, 0]
        window = pl.ds(j * 256, WINDOW)
        scores = dot(query, keys_ref[:, window], (0, 0)) * SCALE
        visible = (column <= here) & (column >= start - base)
        scores = jnp.where(visible, scores, -jnp.inf)
        expons = jnp.exp(scores - jnp.max(scores, axis=1, keepdims=True))
        total = jnp.sum(expons, axis=1, keepdims=True)
        summed = dot(values_ref[:, window], expons.astype(BF), (1, 1))
        total = jnp.transpose(jnp.broadcast_to(total, (BLOCK, BLOCK)))
        context = (summed / total[:HEAD]).astype(BF)
        for t in range(4):
            sent_ref[t, j] = context


def output_kernel(facts_ref, context_ref, w0_ref, w1_ref, w2_ref, w3_ref, prompt_ref, out_ref):
    total = prompt_ref[...].astype(F32)
    for by, weight in enumerate((w0_ref, w1_ref, w2_ref, w3_ref)):
        piece = context_ref[lax.rem(facts_ref[2] + 4 - by, 4)]
        total = total + dot(piece, weight[...], (0, 0))
    out_ref[...] = total.astype(BF)


def local(
    patches,
    picture_grid,
    vision_qkv,
    vision_out,
    merge_weight,
    picture_block,
    picture_offset,
    tokens,
    prompt_lengths,
    text_qkv,
    text_out,
):
    count, width = patches.shape[1:]
    local_width = vision_qkv.shape[2]
    wide = width + FACTS
    z = lax.axis_index("z")
    c = lax.axis_index("c")
    t = lax.axis_index("t")
    picture = patches[0]
    block = picture_block[0]

    share = call(vision_kernel, shape((count, width)), [SMEM, VMEM, VMEM, VMEM])(
        picture_grid, picture, vision_qkv.transpose(1, 2, 0), vision_out
    )
    shares = lax.all_to_all(share.reshape(4, MERGED, width), "t", 0, 0, tiled=True)
    chosen = slot_of(t * MERGED + jnp.arange(MERGED))[:, None] == jnp.arange(count)[None, :]
    own = jnp.dot(chosen.astype(BF), picture, preferred_element_type=F32).astype(BF)
    facts = jnp.stack([block, picture_offset[0], picture_grid[0, 0], picture_grid[0, 1], 1])
    facts = jnp.where(t == 0, facts, 0)
    facts = jnp.concatenate([facts, (block % 8 // 2)[None]]).astype(I32)
    routed = call(merge_kernel, shape((4, MERGED, wide)), [SMEM, VMEM, VMEM, VMEM])(
        facts, own, shares, merge_weight[0]
    )

    got = lax.all_to_all(routed.reshape(16, 16, wide), ("y", "t"), 0, 0, tiled=True)
    got, tokens = lax.optimization_barrier((got, tokens))
    pieces = [tokens] + [around(tokens, "t", by) for by in range(1, 4)]
    got = jnp.sum(got.reshape(4, 4, 16, wide).astype(F32), axis=1).astype(BF)
    got = jnp.concatenate([got, around(got, "c", 1)])
    to = got[:, 0, width].astype(F32).astype(I32)
    pick = (got[:, 0, width + 4] > 0) & (to % 2 == c)
    pick = pick[None, :] & (to[None, :] // 8 == jnp.arange(8)[:, None])
    routed = jnp.einsum("zk,krd->zrd", pick.astype(BF), got, preferred_element_type=F32).astype(BF)
    got = lax.all_to_all(routed, "z", 0, 0, tiled=True)
    got = jnp.sum(got.astype(F32), axis=0).astype(BF)
    got = jnp.broadcast_to(got[None], (4, 16, wide))
    got = lax.all_to_all(got, "t", 0, 0, tiled=True).reshape(MERGED, wide)
    own_tokens = jnp.zeros((4, BLOCK, local_width), BF)
    for by, piece in enumerate(pieces):
        own_tokens = lax.dynamic_update_index_in_dim(own_tokens, piece, (t - by) % 4, 0)
    own_tokens = own_tokens.transpose(1, 0, 2).reshape(BLOCK, width)

    prompt_in, heads = call(
        project_kernel, [shape((BLOCK, width)), shape((4, 3, HEAD, BLOCK))], [VMEM] * 3
    )(got, own_tokens, text_qkv.transpose(1, 2, 0))
    heads, text_out = lax.optimization_barrier((heads, text_out))
    weights = [text_out] + [around(text_out, "t", by) for by in range(1, 4)]
    mine = lax.all_to_all(heads, "y", 0, 0, tiled=True)
    pair = mine[:, 1:]
    near, far = ahead(pair, "z", 1), ahead(pair, "z", 2)
    facts = jnp.stack([z, c, t]).astype(I32)
    sent = call(
        attend_kernel,
        shape((4, 4, HEAD, BLOCK)),
        [SMEM, SMEM] + [VMEM] * 6,
        [pltpu.VMEM((HEAD, 24 * BLOCK), BF)] * 2,
    )(facts, prompt_lengths, mine, near, far, *(around(x, "c", 1) for x in (pair, near, far)))
    context = lax.all_to_all(sent.reshape(16, HEAD, BLOCK), ("t", "y"), 0, 0, tiled=True)
    return call(output_kernel, shape((BLOCK, width)), [SMEM] + [VMEM] * 6)(
        facts, context.reshape(4, local_width, BLOCK), *weights, prompt_in
    )


def solution(mesh):
    split = Mesh(np.asarray(mesh.devices).reshape(8, 4, 2, 4), ("z", "y", "c", "t"))
    seq = ("z", "y", "c")
    placed = (
        P(seq, None, None),
        P(seq, None),
        P(None, None, "t"),
        P("t", None),
        P("t", None, None),
        P(seq),
        P(seq),
        P(seq, "t"),
        P(),
        P(None, None, "t"),
        P("t", None),
    )
    return jax.shard_map(
        local, mesh=split, in_specs=placed, out_specs=P(seq, None), check_vma=False
    )
```

```python
import jax
import jax.numpy as jnp
import numpy as np
from jax import lax
from jax.experimental import pallas as pl
from jax.experimental.pallas import tpu as pltpu
from jax.sharding import Mesh
from jax.sharding import PartitionSpec as P

HEAD = 88
MAXGRID = 16
BLOCK = 128
MERGED = 64
EPSILON = 1e-06
SCALE = HEAD ** (-0.5)
BF = jnp.bfloat16
F32 = jnp.float32
I32 = jnp.int32
VMEM = pltpu.VMEM
SMEM = pltpu.SMEM
FACTS = 128
WINDOW = 18 * BLOCK


def ahead(x, axis, by):
    count = lax.axis_size(axis)
    return lax.ppermute(x, axis, [(i, i + by) for i in range(count - by)])


def around(x, axis, by):
    count = lax.axis_size(axis)
    return lax.ppermute(x, axis, [(i, (i + by) % count) for i in range(count)])


def call(kernel, out_shape, spaces, scratch=(), limit=8):
    single = not isinstance(out_shape, (list, tuple))
    outs = pl.BlockSpec(memory_space=VMEM)
    return pl.pallas_call(
        kernel,
        out_shape=out_shape,
        in_specs=[pl.BlockSpec(memory_space=s) for s in spaces],
        out_specs=outs if single else [outs] * len(out_shape),
        scratch_shapes=scratch,
        compiler_params=pltpu.CompilerParams(vmem_limit_bytes=limit << 20),
    )


def shape(dims, dtype=BF):
    return jax.ShapeDtypeStruct(dims, dtype)


def iota(dims, axis):
    return lax.broadcasted_iota(I32, dims, axis)


def dot(a, b, over):
    return lax.dot_general(
        a, b, (((over[0],), (over[1],)), ((), ())), preferred_element_type=F32
    )


def normalize(values):
    centre = jnp.mean(values, axis=-1, keepdims=True)
    shifted = values - centre
    spread = jnp.mean(shifted * shifted, axis=-1, keepdims=True)
    return (shifted * lax.rsqrt(spread + EPSILON)).astype(BF)


def slot_of(row):
    i, j = row // 128, (row // 64) % 2
    a, b = (row // 8) % 8, row % 8
    return (2 * a + i) * MAXGRID + 2 * b + j


def vision_kernel(
    grid_ref, picture_hbm, qkv_hbm, out_hbm, share_ref, picture_ref, qkv_ref, out_ref, arrived
):
    copies = [pltpu.make_async_copy(picture_hbm, picture_ref, arrived.at[0])]
    for part in range(3):
        copies.append(
            pltpu.make_async_copy(qkv_hbm.at[part], qkv_ref.at[part], arrived.at[1 + part])
        )
    copies.append(pltpu.make_async_copy(out_hbm, out_ref, arrived.at[4]))
    for copy in copies:
        copy.start()
    count = picture_ref.shape[0]
    local_width = qkv_ref.shape[1]
    copies[0].wait()
    normed = normalize(picture_ref[...].astype(F32))
    parts = []
    for part in range(3):
        copies[1 + part].wait()
        parts.append(dot(qkv_ref[part], normed, (1, 1)))
    slots = iota((count, 1), 0)
    usable = (slots // MAXGRID < 2 * grid_ref[0, 0]) & (slots % MAXGRID < 2 * grid_ref[0, 1])
    contexts = []
    for first in range(0, local_width, HEAD):
        q, k, v = (x[first : first + HEAD].astype(BF) for x in parts)
        scores = dot(k, q, (0, 0)) * SCALE
        scores = jnp.where(usable, scores, -jnp.inf)
        expons = jnp.exp(scores - jnp.max(scores, axis=0, keepdims=True))
        total = jnp.sum(expons, axis=0, keepdims=True)
        contexts.append(dot(v, expons.astype(BF), (1, 0)) / total)
    context = jnp.concatenate(contexts, axis=0).astype(BF)
    order = slot_of(iota((count, count), 0)) == iota((count, count), 1)
    context = dot(order.astype(BF), context, (1, 1)).astype(BF)
    copies[4].wait()
    share_ref[...] = dot(context, out_ref[...], (1, 0)).astype(BF)


def sum_kernel(parts_ref, rows_ref):
    for y in range(4):
        total = parts_ref[y, 0].astype(F32)
        for t in range(1, 4):
            total = total + parts_ref[y, t].astype(F32)
        rows_ref[y] = total.astype(BF)


def select_kernel(place_ref, mine_ref, other_ref, routed_ref):
    width = mine_ref.shape[2] - FACTS
    chosen = []
    for rows_ref in (mine_ref, other_ref):
        for y in range(4):
            facts = rows_ref[y, 0:1, width:].astype(F32)
            block, there = facts[:, 0:1], facts[:, 4:5]
            same_core = block - 2.0 * jnp.floor(block * 0.5) == place_ref[1].astype(F32)
            to = jnp.where(same_core & (there > 0.0), jnp.floor(block * 0.125), -1.0)
            chosen.append((to, rows_ref, y))
    for z in range(8):
        rows = jnp.zeros(mine_ref.shape[1:], F32)
        for to, rows_ref, y in chosen:
            rows = jnp.where(to == float(z), rows_ref[y].astype(F32), rows)
        routed_ref[z] = rows.astype(BF)


def merge_kernel(facts_ref, own_ref, shares_ref, weight_ref, rows_ref):
    width = own_ref.shape[1]
    hidden = own_ref[...].astype(F32)
    gained = shares_ref[0].astype(F32)
    for other in range(1, 4):
        gained = gained + shares_ref[other].astype(F32)
    merged = dot(normalize(hidden + gained), weight_ref[...], (1, 0)).astype(BF)
    lane = iota((MERGED, FACTS), 1)
    facts = jnp.zeros((MERGED, FACTS), I32)
    for index in range(5):
        facts = jnp.where(lane == index, facts_ref[index], facts)
    facts = facts.astype(F32).astype(BF)
    for y in range(4):
        here = facts_ref[5] == y
        rows_ref[y, :, :width] = jnp.where(here, merged, jnp.zeros_like(merged))
        rows_ref[y, :, width:] = jnp.where(here, facts, jnp.zeros_like(facts))


def project_kernel(
    place_ref, r0_ref, r1_ref, r2_ref, r3_ref, tokens_ref, qkv_ref, prompt_ref, heads_ref
):
    width = tokens_ref.shape[1]
    pieces, firsts = [], []
    for by, piece in enumerate((r0_ref, r1_ref, r2_ref, r3_ref)):
        pieces.append(piece[...])
        firsts.append(jnp.full((16, 1), 16 * lax.rem(place_ref[2] + 4 - by, 4), I32))
    rows = jnp.concatenate(pieces, axis=0)
    cell = jnp.concatenate(firsts, axis=0) + iota((MERGED, 1), 0) % 16
    facts = rows[:, width:].astype(F32)
    a, b = (cell // 8).astype(F32), (cell % 8).astype(F32)
    offset, high, wide, there = (facts[:, i : i + 1] for i in (1, 2, 3, 4))
    target = offset + a * wide + b
    usable = (a < high) & (b < wide) & (there > 0.0)
    target = jnp.where(usable, target, -1.0)
    table = (target == iota((MERGED, BLOCK), 1).astype(F32)).astype(BF)
    placed = dot(table, rows, (0, 0))
    covered = placed[:, width + 4 : width + 5] > 0.0
    prompt = jnp.where(covered, placed[:, :width], tokens_ref[...].astype(F32))
    prompt_ref[...] = prompt.astype(BF)
    normed = normalize(prompt)
    for part in range(3):
        projected = dot(qkv_ref[part], normed, (1, 1))
        for head in range(4):
            heads_ref[head, part] = projected[head * HEAD : (head + 1) * HEAD].astype(BF)


def attend_kernel(facts_ref, lengths_ref, own_ref, near_ref, far_ref,
                  own2_ref, near2_ref, far2_ref, sent_ref, keys_ref, values_ref):
    z, c = facts_ref[0], facts_ref[1]
    for plane, (mine, other) in enumerate(
        ((far_ref, far2_ref), (near_ref, near2_ref), (own_ref, own2_ref))
    ):
        skip = 1 if plane == 2 else 0
        for y in range(4):
            at = (plane * 8 + 2 * y) * BLOCK
            for half in range(2):
                lanes = pl.ds(at + half * BLOCK, BLOCK)
                for part, store in ((0, keys_ref), (1, values_ref)):
                    picked = jnp.where(
                        c == half, mine[y, skip + part], other[y, part]
                    )
                    store[:, lanes] = picked
    row = iota((BLOCK, 1), 0)
    column = iota((BLOCK, WINDOW), 1)
    for j in range(4):
        base = (z - 2) * 1024 + j * 256
        here = 2048 + c * BLOCK + row
        start = jnp.zeros((BLOCK, 1), I32)
        end = jnp.int32(0)
        for prompt in range(16):
            end = end + lengths_ref[prompt]
            start = jnp.where(end <= here + base, end, start)
        query = own_ref[j, 0]
        window = pl.ds(j * 256, WINDOW)
        scores = dot(query, keys_ref[:, window], (0, 0)) * SCALE
        visible = (column <= here) & (column >= start - base)
        scores = jnp.where(visible, scores, -jnp.inf)
        expons = jnp.exp(scores - jnp.max(scores, axis=1, keepdims=True))
        total = jnp.sum(expons, axis=1, keepdims=True)
        summed = dot(values_ref[:, window], expons.astype(BF), (1, 1))
        total = jnp.transpose(jnp.broadcast_to(total, (BLOCK, BLOCK)))
        context = (summed / total[:HEAD]).astype(BF)
        for t in range(4):
            sent_ref[t, j] = context


def output_kernel(
    place_ref, context_ref, w0_ref, m1_ref, m2_ref, m3_ref, o1_ref, o2_ref, o3_ref,
    prompt_ref, out_ref,
):
    c, t = place_ref[1], place_ref[2]
    half = w0_ref.shape[0] // 2
    total = prompt_ref[...].astype(F32)
    for part in range(2):
        total = total + dot(context_ref[t, part], w0_ref[part * half : (part + 1) * half], (0, 0))
    for by, mine, other in ((1, m1_ref, o1_ref), (2, m2_ref, o2_ref), (3, m3_ref, o3_ref)):
        source = lax.rem(t + 4 - by, 4)
        total = total + dot(context_ref[source, c], mine[...], (0, 0))
        total = total + dot(context_ref[source, 1 - c], other[...], (0, 0))
    out_ref[...] = total.astype(BF)


def local(
    patches,
    picture_grid,
    vision_qkv,
    vision_out,
    merge_weight,
    picture_block,
    picture_offset,
    tokens,
    prompt_lengths,
    text_qkv,
    text_out,
):
    count, width = patches.shape[1:]
    local_width = vision_qkv.shape[2]
    wide = width + FACTS
    z = lax.axis_index("z")
    c = lax.axis_index("c")
    t = lax.axis_index("t")
    picture = patches[0]
    block = picture_block[0]

    place = jnp.stack([z, c, t]).astype(I32)
    share = call(
        vision_kernel,
        shape((count, width)),
        [SMEM, pl.ANY, pl.ANY, pl.ANY],
        [
            VMEM((count, width), BF),
            VMEM((3, local_width, width), BF),
            VMEM((local_width, width), BF),
            pltpu.SemaphoreType.DMA((5,)),
        ],
        limit=20,
    )(picture_grid, picture, vision_qkv.transpose(1, 2, 0), vision_out)
    shares = lax.all_to_all(share.reshape(4, MERGED, width), "t", 0, 0, tiled=True)
    chosen = slot_of(t * MERGED + jnp.arange(MERGED))[:, None] == jnp.arange(count)[None, :]
    own = jnp.dot(chosen.astype(BF), picture, preferred_element_type=F32).astype(BF)
    facts = jnp.stack([block, picture_offset[0], picture_grid[0, 0], picture_grid[0, 1], 1])
    facts = jnp.where(t == 0, facts, 0)
    facts = jnp.concatenate([facts, (block % 8 // 2)[None]]).astype(I32)
    routed = call(merge_kernel, shape((4, MERGED, wide)), [SMEM, VMEM, VMEM, VMEM])(
        facts, own, shares, merge_weight[0]
    )

    got = lax.all_to_all(routed.reshape(16, 16, wide), ("y", "t"), 0, 0, tiled=True)
    got = call(sum_kernel, shape((4, 16, wide)), [VMEM])(got.reshape(4, 4, 16, wide))
    other = around(got, "c", 1)
    routed = call(select_kernel, shape((8, 16, wide)), [SMEM, VMEM, VMEM])(place, got, other)
    routed, tokens, text_out = lax.optimization_barrier((routed, tokens, text_out))
    half = local_width // 2
    near_half = lax.dynamic_slice_in_dim(text_out, c * half, half, 0)
    from_left, from_right = around(near_half, "t", 1), around(near_half, "t", -1)
    pieces = [tokens] + [around(tokens, "t", by) for by in range(1, 4)]
    got = lax.all_to_all(routed, "z", 0, 0, tiled=True)
    got = jnp.sum(got.astype(F32), axis=0).astype(BF)
    rows = [got] + [around(got, "t", by) for by in range(1, 4)]
    own_tokens = jnp.zeros((4, BLOCK, local_width), BF)
    for by, piece in enumerate(pieces):
        own_tokens = lax.dynamic_update_index_in_dim(own_tokens, piece, (t - by) % 4, 0)
    own_tokens = own_tokens.transpose(1, 0, 2).reshape(BLOCK, width)

    prompt_in, heads = call(
        project_kernel,
        [shape((BLOCK, width)), shape((4, 3, HEAD, BLOCK))],
        [SMEM] + [VMEM] * 6,
    )(place, *rows, own_tokens, text_qkv.transpose(1, 2, 0))
    heads, from_left, from_right = lax.optimization_barrier((heads, from_left, from_right))
    far_halves = (
        around(from_left[: half // 2], "t", 1),
        around(from_right[half // 2 :], "t", -1),
    )
    mine = lax.all_to_all(heads, "y", 0, 0, tiled=True)
    pair = mine[:, 1:]
    near, far = ahead(pair, "z", 1), ahead(pair, "z", 2)
    others = [around(x, "c", 1) for x in (pair, near, far)]
    weights = [from_left, jnp.concatenate(far_halves), from_right]
    weights = weights + [around(x, "c", 1) for x in weights]
    sent = call(
        attend_kernel,
        shape((4, 4, HEAD, BLOCK)),
        [SMEM, SMEM] + [VMEM] * 6,
        [pltpu.VMEM((HEAD, 24 * BLOCK), BF)] * 2,
        limit=16,
    )(place, prompt_lengths, mine, near, far, *others)
    context = lax.all_to_all(sent.reshape(16, HEAD, BLOCK), ("t", "y"), 0, 0, tiled=True)
    return call(output_kernel, shape((BLOCK, width)), [SMEM] + [VMEM] * 9)(
        place, context.reshape(4, 2, half, BLOCK), text_out, *weights, prompt_in
    )


def solution(mesh):
    split = Mesh(np.asarray(mesh.devices).reshape(8, 4, 2, 4), ("z", "y", "c", "t"))
    seq = ("z", "y", "c")
    placed = (
        P(seq, None, None),
        P(seq, None),
        P(None, None, "t"),
        P("t", None),
        P("t", None, None),
        P(seq),
        P(seq),
        P(seq, "t"),
        P(),
        P(None, None, "t"),
        P("t", None),
    )
    return jax.shard_map(
        local, mesh=split, in_specs=placed, out_specs=P(seq, None), check_vma=False
    )
```

```python
import jax
import jax.numpy as jnp
import numpy as np
from jax import lax
from jax.experimental import pallas as pl
from jax.experimental.pallas import tpu as pltpu
from jax.sharding import Mesh
from jax.sharding import PartitionSpec as P

HEAD = 88
MAXGRID = 16
BLOCK = 128
MERGED = 64
EPSILON = 1e-06
SCALE = HEAD ** (-0.5)
BF = jnp.bfloat16
F32 = jnp.float32
I32 = jnp.int32
VMEM = pltpu.VMEM
SMEM = pltpu.SMEM
HBM = pltpu.HBM
FACTS = 128
WINDOW = 18 * BLOCK


def ahead(x, axis, by):
    count = lax.axis_size(axis)
    return lax.ppermute(x, axis, [(i, i + by) for i in range(count - by)])


def around(x, axis, by):
    count = lax.axis_size(axis)
    return lax.ppermute(x, axis, [(i, (i + by) % count) for i in range(count)])


def call(kernel, out_shape, spaces, scratch=(), limit=8):
    single = not isinstance(out_shape, (list, tuple))
    outs = pl.BlockSpec(memory_space=VMEM)
    return pl.pallas_call(
        kernel,
        out_shape=out_shape,
        in_specs=[pl.BlockSpec(memory_space=s) for s in spaces],
        out_specs=outs if single else [outs] * len(out_shape),
        scratch_shapes=scratch,
        compiler_params=pltpu.CompilerParams(vmem_limit_bytes=limit << 20),
    )


def shape(dims, dtype=BF):
    return jax.ShapeDtypeStruct(dims, dtype)


def iota(dims, axis):
    return lax.broadcasted_iota(I32, dims, axis)


def dot(a, b, over):
    return lax.dot_general(
        a, b, (((over[0],), (over[1],)), ((), ())), preferred_element_type=F32
    )


def normalize(values):
    centre = jnp.mean(values, axis=-1, keepdims=True)
    shifted = values - centre
    spread = jnp.mean(shifted * shifted, axis=-1, keepdims=True)
    return (shifted * lax.rsqrt(spread + EPSILON)).astype(BF)


def slot_of(row):
    i, j = row // 128, (row // 64) % 2
    a, b = (row // 8) % 8, row % 8
    return (2 * a + i) * MAXGRID + 2 * b + j


def vision_kernel(
    grid_ref, picture_hbm, qkv_hbm, out_hbm, share_ref, picture_ref, qkv_ref, out_ref, arrived
):
    copies = [pltpu.make_async_copy(picture_hbm, picture_ref, arrived.at[0])]
    for part in range(3):
        copies.append(
            pltpu.make_async_copy(qkv_hbm.at[part], qkv_ref.at[part], arrived.at[1 + part])
        )
    copies.append(pltpu.make_async_copy(out_hbm, out_ref, arrived.at[4]))
    for copy in copies:
        copy.start()
    count = picture_ref.shape[0]
    local_width = qkv_ref.shape[1]
    copies[0].wait()
    normed = normalize(picture_ref[...].astype(F32))
    parts = []
    for part in range(3):
        copies[1 + part].wait()
        parts.append(dot(qkv_ref[part], normed, (1, 1)))
    slots = iota((count, 1), 0)
    usable = (slots // MAXGRID < 2 * grid_ref[0, 0]) & (slots % MAXGRID < 2 * grid_ref[0, 1])
    contexts = []
    for first in range(0, local_width, HEAD):
        q, k, v = (x[first : first + HEAD].astype(BF) for x in parts)
        scores = dot(k, q, (0, 0)) * SCALE
        scores = jnp.where(usable, scores, -jnp.inf)
        expons = jnp.exp(scores - jnp.max(scores, axis=0, keepdims=True))
        total = jnp.sum(expons, axis=0, keepdims=True)
        contexts.append(dot(v, expons.astype(BF), (1, 0)) / total)
    context = jnp.concatenate(contexts, axis=0).astype(BF)
    order = slot_of(iota((count, count), 0)) == iota((count, count), 1)
    context = dot(order.astype(BF), context, (1, 1)).astype(BF)
    copies[4].wait()
    share_ref[...] = dot(context, out_ref[...], (1, 0)).astype(BF)


def sum_kernel(parts_ref, rows_ref):
    for y in range(4):
        total = parts_ref[y, 0].astype(F32)
        for t in range(1, 4):
            total = total + parts_ref[y, t].astype(F32)
        rows_ref[y] = total.astype(BF)


def select_kernel(place_ref, mine_ref, other_ref, routed_ref):
    width = mine_ref.shape[2] - FACTS
    routed_ref[...] = jnp.zeros(routed_ref.shape, BF)
    for rows_ref in (mine_ref, other_ref):
        for y in range(4):
            facts = rows_ref[y, 0:1, width:].astype(F32)
            block = facts[0, 0].astype(I32)

            @pl.when((facts[0, 4] > 0.0) & (block % 2 == place_ref[1]))
            def _():
                routed_ref[block // 8] = rows_ref[y]


def merge_kernel(facts_ref, own_ref, shares_ref, weight_ref, rows_ref):
    width = own_ref.shape[1]
    hidden = own_ref[...].astype(F32)
    gained = shares_ref[0].astype(F32)
    for other in range(1, 4):
        gained = gained + shares_ref[other].astype(F32)
    merged = dot(normalize(hidden + gained), weight_ref[...], (1, 0)).astype(BF)
    lane = iota((MERGED, FACTS), 1)
    facts = jnp.zeros((MERGED, FACTS), I32)
    for index in range(5):
        facts = jnp.where(lane == index, facts_ref[index], facts)
    facts = facts.astype(F32).astype(BF)
    for y in range(4):
        here = facts_ref[5] == y
        rows_ref[y, :, :width] = jnp.where(here, merged, jnp.zeros_like(merged))
        rows_ref[y, :, width:] = jnp.where(here, facts, jnp.zeros_like(facts))


def placed_rows(place_ref, pieces_refs, tokens_ref):
    width = tokens_ref.shape[1]
    pieces, firsts = [], []
    for by, piece in enumerate(pieces_refs):
        pieces.append(piece[...])
        firsts.append(jnp.full((16, 1), 16 * lax.rem(place_ref[2] + 4 - by, 4), I32))
    rows = jnp.concatenate(pieces, axis=0)
    cell = jnp.concatenate(firsts, axis=0) + iota((MERGED, 1), 0) % 16
    facts = rows[:, width:].astype(F32)
    a, b = (cell // 8).astype(F32), (cell % 8).astype(F32)
    offset, high, wide, there = (facts[:, i : i + 1] for i in (1, 2, 3, 4))
    target = offset + a * wide + b
    usable = (a < high) & (b < wide) & (there > 0.0)
    target = jnp.where(usable, target, -1.0)
    table = (target == iota((MERGED, BLOCK), 1).astype(F32)).astype(BF)
    placed = dot(table, rows, (0, 0))
    covered = placed[:, width + 4 : width + 5] > 0.0
    return jnp.where(covered, placed[:, :width], tokens_ref[...].astype(F32))


def place_kernel(place_ref, r0_ref, r1_ref, r2_ref, r3_ref, tokens_ref, prompt_ref):
    pieces = (r0_ref, r1_ref, r2_ref, r3_ref)
    prompt_ref[...] = placed_rows(place_ref, pieces, tokens_ref).astype(BF)


def project_kernel(
    place_ref, r0_ref, r1_ref, r2_ref, r3_ref, tokens_ref, qkv_ref, heads_ref
):
    pieces = (r0_ref, r1_ref, r2_ref, r3_ref)
    normed = normalize(placed_rows(place_ref, pieces, tokens_ref))
    for part in range(3):
        projected = dot(qkv_ref[part], normed, (1, 1))
        for head in range(4):
            heads_ref[head, part] = projected[head * HEAD : (head + 1) * HEAD].astype(BF)


def attend_kernel(facts_ref, lengths_ref, own_ref, near_ref, far_ref,
                  own2_ref, near2_ref, far2_ref, sent_ref, keys_ref, values_ref):
    z, c = facts_ref[0], facts_ref[1]
    for plane, (mine, other) in enumerate(
        ((far_ref, far2_ref), (near_ref, near2_ref), (own_ref, own2_ref))
    ):
        skip = 1 if plane == 2 else 0
        for y in range(4):
            at = (plane * 8 + 2 * y) * BLOCK
            for half in range(2):
                lanes = pl.ds(at + half * BLOCK, BLOCK)
                for part, store in ((0, keys_ref), (1, values_ref)):
                    picked = jnp.where(
                        c == half, mine[y, skip + part], other[y, part]
                    )
                    store[:, lanes] = picked
    row = iota((BLOCK, 1), 0)
    column = iota((BLOCK, WINDOW), 1)
    for j in range(4):
        base = (z - 2) * 1024 + j * 256
        here = 2048 + c * BLOCK + row
        start = jnp.zeros((BLOCK, 1), I32)
        end = jnp.int32(0)
        for prompt in range(16):
            end = end + lengths_ref[prompt]
            start = jnp.where(end <= here + base, end, start)
        query = own_ref[j, 0]
        window = pl.ds(j * 256, WINDOW)
        scores = dot(query, keys_ref[:, window], (0, 0)) * SCALE
        visible = (column <= here) & (column >= start - base)
        scores = jnp.where(visible, scores, -jnp.inf)
        expons = jnp.exp(scores - jnp.max(scores, axis=1, keepdims=True))
        total = jnp.sum(expons, axis=1, keepdims=True)
        summed = dot(values_ref[:, window], expons.astype(BF), (1, 1))
        total = jnp.transpose(jnp.broadcast_to(total, (BLOCK, BLOCK)))
        context = (summed / total[:HEAD]).astype(BF)
        for t in range(4):
            sent_ref[t, j] = context


def output_kernel(
    place_ref, context_ref, w0_ref, m1_ref, m2_ref, m3_ref, o1_ref, o2_ref, o3_ref,
    prompt_ref, out_ref,
):
    c, t = place_ref[1], place_ref[2]
    half = m1_ref.shape[0]
    width = out_ref.shape[1]
    pairs = [(context_ref[t, part].T, w0_ref.at[part * half : (part + 1) * half]) for part in (0, 1)]
    for by, mine, other in ((1, m1_ref, o1_ref), (2, m2_ref, o2_ref), (3, m3_ref, o3_ref)):
        source = lax.rem(t + 4 - by, 4)
        pairs.append((context_ref[source, c].T, mine))
        pairs.append((context_ref[source, 1 - c].T, other))
    for first in range(0, width, 256):
        strip = slice(first, min(first + 256, width))
        total = prompt_ref[:, strip].astype(F32)
        for context, weight in pairs:
            total = total + dot(context, weight[:, strip], (1, 0))
        out_ref[:, strip] = total.astype(BF)


def local(
    patches,
    picture_grid,
    vision_qkv,
    vision_out,
    merge_weight,
    picture_block,
    picture_offset,
    tokens,
    prompt_lengths,
    text_qkv,
    text_out,
):
    count, width = patches.shape[1:]
    local_width = vision_qkv.shape[2]
    wide = width + FACTS
    z = lax.axis_index("z")
    c = lax.axis_index("c")
    t = lax.axis_index("t")
    picture = patches[0]
    block = picture_block[0]

    place = jnp.stack([z, c, t]).astype(I32)
    share = call(
        vision_kernel,
        shape((count, width)),
        [SMEM, HBM, HBM, HBM],
        [
            VMEM((count, width), BF),
            VMEM((3, local_width, width), BF),
            VMEM((local_width, width), BF),
            pltpu.SemaphoreType.DMA((5,)),
        ],
        limit=60,
    )(picture_grid, picture, vision_qkv.transpose(1, 2, 0), vision_out)
    shares = lax.all_to_all(share.reshape(4, MERGED, width), "t", 0, 0, tiled=True)
    chosen = slot_of(t * MERGED + jnp.arange(MERGED))[:, None] == jnp.arange(count)[None, :]
    own = jnp.dot(chosen.astype(BF), picture, preferred_element_type=F32).astype(BF)
    own, tokens = lax.optimization_barrier((own, tokens))
    pieces = [tokens] + [around(tokens, "t", by) for by in range(1, 4)]
    facts = jnp.stack([block, picture_offset[0], picture_grid[0, 0], picture_grid[0, 1], 1])
    facts = jnp.where(t == 0, facts, 0)
    facts = jnp.concatenate([facts, (block % 8 // 2)[None]]).astype(I32)
    routed = call(merge_kernel, shape((4, MERGED, wide)), [SMEM, VMEM, VMEM, VMEM])(
        facts, own, shares, merge_weight[0]
    )

    got = lax.all_to_all(routed.reshape(16, 16, wide), ("y", "t"), 0, 0, tiled=True)
    got = call(sum_kernel, shape((4, 16, wide)), [VMEM])(got.reshape(4, 4, 16, wide))
    other = around(got, "c", 1)
    routed = call(select_kernel, shape((8, 16, wide)), [SMEM, VMEM, VMEM])(place, got, other)
    routed, text_out = lax.optimization_barrier((routed, text_out))
    half = local_width // 2
    near_half = lax.dynamic_slice_in_dim(text_out, c * half, half, 0)
    from_left, from_right = around(near_half, "t", 1), around(near_half, "t", -1)
    got = lax.all_to_all(routed, "z", 0, 0, tiled=True)
    got = jnp.sum(got.astype(F32), axis=0).astype(BF)
    rows = [got] + [around(got, "t", by) for by in range(1, 4)]
    own_tokens = jnp.zeros((4, BLOCK, local_width), BF)
    for by, piece in enumerate(pieces):
        own_tokens = lax.dynamic_update_index_in_dim(own_tokens, piece, (t - by) % 4, 0)
    own_tokens = own_tokens.transpose(1, 0, 2).reshape(BLOCK, width)

    heads = call(
        project_kernel,
        shape((4, 3, HEAD, BLOCK)),
        [SMEM] + [VMEM] * 6,
    )(place, *rows, own_tokens, text_qkv.transpose(1, 2, 0))
    mine = lax.all_to_all(heads, "y", 0, 0, tiled=True)
    mine, from_left, from_right = lax.optimization_barrier((mine, from_left, from_right))
    mine, own_tokens = lax.optimization_barrier((mine, own_tokens))
    prompt_in = call(place_kernel, shape((BLOCK, width)), [SMEM] + [VMEM] * 5)(
        place, *rows, own_tokens
    )
    far_halves = (
        around(from_left[: half // 2], "t", 1),
        around(from_right[half // 2 :], "t", -1),
    )
    pair = mine[:, 1:]
    near, far = ahead(pair, "z", 1), ahead(pair, "z", 2)
    others = [around(x, "c", 1) for x in (pair, near, far)]
    weights = [from_left, jnp.concatenate(far_halves), from_right]
    weights = weights + [around(x, "c", 1) for x in weights]
    sent = call(
        attend_kernel,
        shape((4, 4, HEAD, BLOCK)),
        [SMEM, SMEM] + [VMEM] * 6,
        [pltpu.VMEM((HEAD, 24 * BLOCK), BF)] * 2,
        limit=16,
    )(place, prompt_lengths, mine, near, far, *others)
    context = lax.all_to_all(sent.reshape(16, HEAD, BLOCK), ("t", "y"), 0, 0, tiled=True)
    return call(output_kernel, shape((BLOCK, width)), [SMEM] + [VMEM] * 9)(
        place, context.reshape(4, 2, half, BLOCK), text_out, *weights, prompt_in
    )


def solution(mesh):
    split = Mesh(np.asarray(mesh.devices).reshape(8, 4, 2, 4), ("z", "y", "c", "t"))
    seq = ("z", "y", "c")
    placed = (
        P(seq, None, None),
        P(seq, None),
        P(None, None, "t"),
        P("t", None),
        P("t", None, None),
        P(seq),
        P(seq),
        P(seq, "t"),
        P(),
        P(None, None, "t"),
        P("t", None),
    )
    return jax.shard_map(
        local, mesh=split, in_specs=placed, out_specs=P(seq, None), check_vma=False
    )
```

```python
import jax
import jax.numpy as jnp
import numpy as np
from jax import lax
from jax.experimental import pallas as pl
from jax.experimental.pallas import tpu as pltpu
from jax.sharding import Mesh
from jax.sharding import PartitionSpec as P

HEAD = 88
MAXGRID = 16
BLOCK = 128
MERGED = 64
EPSILON = 1e-06
SCALE = HEAD ** (-0.5)
BF = jnp.bfloat16
F32 = jnp.float32
I32 = jnp.int32
VMEM = pltpu.VMEM
SMEM = pltpu.SMEM
HBM = pltpu.HBM
FACTS = 128
WINDOW = 18 * BLOCK


def ahead(x, axis, by):
    count = lax.axis_size(axis)
    return lax.ppermute(x, axis, [(i, i + by) for i in range(count - by)])


def around(x, axis, by):
    count = lax.axis_size(axis)
    return lax.ppermute(x, axis, [(i, (i + by) % count) for i in range(count)])


def call(kernel, out_shape, spaces, scratch=(), limit=8):
    single = not isinstance(out_shape, (list, tuple))
    outs = pl.BlockSpec(memory_space=VMEM)
    return pl.pallas_call(
        kernel,
        out_shape=out_shape,
        in_specs=[pl.BlockSpec(memory_space=s) for s in spaces],
        out_specs=outs if single else [outs] * len(out_shape),
        scratch_shapes=scratch,
        compiler_params=pltpu.CompilerParams(vmem_limit_bytes=limit << 20),
    )


def shape(dims, dtype=BF):
    return jax.ShapeDtypeStruct(dims, dtype)


def iota(dims, axis):
    return lax.broadcasted_iota(I32, dims, axis)


def dot(a, b, over):
    return lax.dot_general(
        a, b, (((over[0],), (over[1],)), ((), ())), preferred_element_type=F32
    )


def normalize(values):
    centre = jnp.mean(values, axis=-1, keepdims=True)
    shifted = values - centre
    spread = jnp.mean(shifted * shifted, axis=-1, keepdims=True)
    return (shifted * lax.rsqrt(spread + EPSILON)).astype(BF)


def slot_of(row):
    i, j = row // 128, (row // 64) % 2
    a, b = (row // 8) % 8, row % 8
    return (2 * a + i) * MAXGRID + 2 * b + j


def vision_kernel(
    grid_ref, picture_hbm, qkv_hbm, out_hbm, share_ref, picture_ref, qkv_ref, out_ref, arrived
):
    copies = [pltpu.make_async_copy(picture_hbm, picture_ref, arrived.at[0])]
    for part in range(3):
        copies.append(
            pltpu.make_async_copy(qkv_hbm.at[part], qkv_ref.at[part], arrived.at[1 + part])
        )
    copies.append(pltpu.make_async_copy(out_hbm, out_ref, arrived.at[4]))
    for copy in copies:
        copy.start()
    count = picture_ref.shape[0]
    local_width = qkv_ref.shape[1]
    copies[0].wait()
    normed = normalize(picture_ref[...].astype(F32))
    parts = []
    for part in range(3):
        copies[1 + part].wait()
        parts.append(dot(qkv_ref[part], normed, (1, 1)))
    slots = iota((count, 1), 0)
    usable = (slots // MAXGRID < 2 * grid_ref[0, 0]) & (slots % MAXGRID < 2 * grid_ref[0, 1])
    contexts = []
    for first in range(0, local_width, HEAD):
        q, k, v = (x[first : first + HEAD].astype(BF) for x in parts)
        scores = dot(k, q, (0, 0)) * SCALE
        scores = jnp.where(usable, scores, -jnp.inf)
        expons = jnp.exp(scores - jnp.max(scores, axis=0, keepdims=True))
        total = jnp.sum(expons, axis=0, keepdims=True)
        contexts.append(dot(v, expons.astype(BF), (1, 0)) / total)
    context = jnp.concatenate(contexts, axis=0).astype(BF)
    order = slot_of(iota((count, count), 0)) == iota((count, count), 1)
    context = dot(order.astype(BF), context, (1, 1)).astype(BF)
    copies[4].wait()
    share_ref[...] = dot(context, out_ref[...], (1, 0)).astype(BF)


def sum_kernel(parts_ref, rows_ref):
    for y in range(4):
        total = parts_ref[y, 0].astype(F32)
        for t in range(1, 4):
            total = total + parts_ref[y, t].astype(F32)
        rows_ref[y] = total.astype(BF)


def select_kernel(place_ref, mine_ref, other_ref, routed_ref):
    wide = mine_ref.shape[2]
    width = wide - FACTS
    rows = jnp.concatenate(
        [mine_ref[...].reshape(64, wide), other_ref[...].reshape(64, wide)], axis=0
    )
    facts = rows[:, width:].astype(F32)
    block, there = facts[:, 0:1], facts[:, 4:5]
    same_core = block - 2.0 * jnp.floor(block * 0.5) == place_ref[1].astype(F32)
    to = jnp.where(same_core & (there > 0.0), jnp.floor(block * 0.125), -1.0).astype(I32)
    source, target = iota((128, 128), 0), iota((128, 128), 1)
    chosen = (to == target // 16) & (source % 16 == target % 16)
    routed = dot(chosen.astype(BF), rows, (0, 0))
    routed_ref[...] = routed.astype(BF).reshape(8, 16, wide)


def merge_kernel(
    facts_ref, own_ref, shares_ref, weight_hbm, rows_ref, weight_ref, arrived
):
    width = own_ref.shape[1]
    deep = width // 4
    copies = []
    for piece in range(4):
        at = pl.ds(piece * deep, deep)
        copies.append(
            pltpu.make_async_copy(weight_hbm.at[at], weight_ref.at[at], arrived.at[piece])
        )
        copies[-1].start()
    total = own_ref[...].astype(F32)
    for other in range(4):
        total = total + shares_ref[other].astype(F32)
    normed = normalize(total)
    for copy in copies:
        copy.wait()
    merged = dot(normed, weight_ref[...], (1, 0)).astype(BF)
    lane = iota((MERGED, FACTS), 1)
    facts = jnp.zeros((MERGED, FACTS), I32)
    for index in range(5):
        facts = jnp.where(lane == index, facts_ref[index], facts)
    facts = facts.astype(F32).astype(BF)
    for y in range(4):
        here = facts_ref[5] == y
        rows_ref[y, :, :width] = jnp.where(here, merged, jnp.zeros_like(merged))
        rows_ref[y, :, width:] = jnp.where(here, facts, jnp.zeros_like(facts))


def placed_rows(place_ref, pieces_refs, tokens_ref):
    width = tokens_ref.shape[1]
    pieces, firsts = [], []
    for by, piece in enumerate(pieces_refs):
        pieces.append(piece[...])
        firsts.append(jnp.full((16, 1), 16 * lax.rem(place_ref[2] + 4 - by, 4), I32))
    rows = jnp.concatenate(pieces, axis=0)
    cell = jnp.concatenate(firsts, axis=0) + iota((MERGED, 1), 0) % 16
    facts = rows[:, width:].astype(F32)
    a, b = (cell // 8).astype(F32), (cell % 8).astype(F32)
    offset, high, wide, there = (facts[:, i : i + 1] for i in (1, 2, 3, 4))
    target = offset + a * wide + b
    usable = (a < high) & (b < wide) & (there > 0.0)
    target = jnp.where(usable, target, -1.0)
    table = (target == iota((MERGED, BLOCK), 1).astype(F32)).astype(BF)
    placed = dot(table, rows, (0, 0))
    covered = placed[:, width + 4 : width + 5] > 0.0
    return jnp.where(covered, placed[:, :width], tokens_ref[...].astype(F32))


def place_kernel(place_ref, r0_ref, r1_ref, r2_ref, r3_ref, tokens_ref, prompt_ref):
    pieces = (r0_ref, r1_ref, r2_ref, r3_ref)
    prompt_ref[...] = placed_rows(place_ref, pieces, tokens_ref).astype(BF)


def project_kernel(
    place_ref, r0_ref, r1_ref, r2_ref, r3_ref, tokens_ref, qkv_ref, heads_ref
):
    pieces = (r0_ref, r1_ref, r2_ref, r3_ref)
    normed = normalize(placed_rows(place_ref, pieces, tokens_ref))
    for part in range(3):
        projected = dot(qkv_ref[part], normed, (1, 1))
        for head in range(4):
            heads_ref[head, part] = projected[head * HEAD : (head + 1) * HEAD].astype(BF)


def attend_kernel(facts_ref, lengths_ref, own_ref, near_ref, far_ref,
                  own2_ref, near2_ref, far2_ref, sent_ref, keys_ref, values_ref):
    z, c = facts_ref[0], facts_ref[1]
    for plane, (mine, other) in enumerate(
        ((far_ref, far2_ref), (near_ref, near2_ref), (own_ref, own2_ref))
    ):
        skip = 1 if plane == 2 else 0
        for y in range(4):
            at = (plane * 8 + 2 * y) * BLOCK
            for half in range(2):
                lanes = pl.ds(at + half * BLOCK, BLOCK)
                for part, store in ((0, keys_ref), (1, values_ref)):
                    picked = jnp.where(
                        c == half, mine[y, skip + part], other[y, part]
                    )
                    store[:, lanes] = picked
    row = iota((BLOCK, 1), 0)
    column = iota((BLOCK, WINDOW), 1)
    for j in range(4):
        base = (z - 2) * 1024 + j * 256
        here = 2048 + c * BLOCK + row
        start = jnp.zeros((BLOCK, 1), I32)
        end = jnp.int32(0)
        for prompt in range(16):
            end = end + lengths_ref[prompt]
            start = jnp.where(end <= here + base, end, start)
        query = own_ref[j, 0]
        window = pl.ds(j * 256, WINDOW)
        scores = dot(query, keys_ref[:, window], (0, 0)) * SCALE
        visible = (column <= here) & (column >= start - base)
        scores = jnp.where(visible, scores, -jnp.inf)
        expons = jnp.exp(scores - jnp.max(scores, axis=1, keepdims=True))
        total = jnp.sum(expons, axis=1, keepdims=True)
        summed = dot(values_ref[:, window], expons.astype(BF), (1, 1))
        total = jnp.transpose(jnp.broadcast_to(total, (BLOCK, BLOCK)))
        context = (summed / total[:HEAD]).astype(BF)
        for t in range(4):
            sent_ref[t, j] = context


def output_kernel(
    place_ref, context_ref, w0_ref, m2_ref, m1_ref, m3_ref, o2_ref, o1_ref, o3_ref,
    prompt_ref, out_ref,
):
    c, t = place_ref[1], place_ref[2]
    half = m1_ref.shape[0]
    width = out_ref.shape[1]
    pairs = [(context_ref[t, part].T, w0_ref.at[part * half : (part + 1) * half]) for part in (0, 1)]
    for by, mine, other in ((1, m1_ref, o1_ref), (2, m2_ref, o2_ref), (3, m3_ref, o3_ref)):
        source = lax.rem(t + 4 - by, 4)
        pairs.append((context_ref[source, c].T, mine))
        pairs.append((context_ref[source, 1 - c].T, other))
    for first in range(0, width, 256):
        strip = slice(first, min(first + 256, width))
        total = prompt_ref[:, strip].astype(F32)
        for context, weight in pairs:
            total = total + dot(context, weight[:, strip], (1, 0))
        out_ref[:, strip] = total.astype(BF)


def local(
    patches,
    picture_grid,
    vision_qkv,
    vision_out,
    merge_weight,
    picture_block,
    picture_offset,
    tokens,
    prompt_lengths,
    text_qkv,
    text_out,
):
    count, width = patches.shape[1:]
    local_width = vision_qkv.shape[2]
    wide = width + FACTS
    z = lax.axis_index("z")
    c = lax.axis_index("c")
    t = lax.axis_index("t")
    picture = patches[0]
    block = picture_block[0]

    place = jnp.stack([z, c, t]).astype(I32)
    share = call(
        vision_kernel,
        shape((count, width)),
        [SMEM, HBM, HBM, HBM],
        [
            VMEM((count, width), BF),
            VMEM((3, local_width, width), BF),
            VMEM((local_width, width), BF),
            pltpu.SemaphoreType.DMA((5,)),
        ],
        limit=60,
    )(picture_grid, picture, vision_qkv.transpose(1, 2, 0), vision_out)
    shares = lax.all_to_all(share.reshape(4, MERGED, width), "t", 0, 0, tiled=True)
    chosen = slot_of(t * MERGED + jnp.arange(MERGED))[:, None] == jnp.arange(count)[None, :]
    own = jnp.dot(chosen.astype(BF), picture, preferred_element_type=F32).astype(BF)
    facts = jnp.stack([block, picture_offset[0], picture_grid[0, 0], picture_grid[0, 1], 1])
    facts = jnp.where(t == 0, facts, 0)
    facts = jnp.concatenate([facts, (block % 8 // 2)[None]]).astype(I32)
    routed = call(
        merge_kernel,
        shape((4, MERGED, wide)),
        [SMEM, VMEM, VMEM, HBM],
        [VMEM((width, width), BF), pltpu.SemaphoreType.DMA((4,))],
        limit=60,
    )(
        facts, own, shares, merge_weight[0]
    )

    got = lax.all_to_all(routed.reshape(16, 16, wide), ("y", "t"), 0, 0, tiled=True)
    got = call(sum_kernel, shape((4, 16, wide)), [VMEM])(got.reshape(4, 4, 16, wide))
    other = around(got, "c", 1)
    routed = call(select_kernel, shape((8, 16, wide)), [SMEM, VMEM, VMEM])(place, got, other)
    routed, text_out = lax.optimization_barrier((routed, text_out))
    half = local_width // 2
    near_half = lax.dynamic_slice_in_dim(text_out, c * half, half, 0)
    near_half, tokens = lax.optimization_barrier((near_half, tokens))
    halves = [around(near_half, "t", by) for by in (2, 1, 3)]
    pieces = [tokens] + [around(tokens, "t", by) for by in range(1, 4)]
    got = lax.all_to_all(routed, "z", 0, 0, tiled=True)
    got = jnp.sum(got.astype(F32), axis=0).astype(BF)
    rows = [got] + [around(got, "t", by) for by in range(1, 4)]
    own_tokens = jnp.zeros((4, BLOCK, local_width), BF)
    for by, piece in enumerate(pieces):
        own_tokens = lax.dynamic_update_index_in_dim(own_tokens, piece, (t - by) % 4, 0)
    own_tokens = own_tokens.transpose(1, 0, 2).reshape(BLOCK, width)
    heads = call(
        project_kernel,
        shape((4, 3, HEAD, BLOCK)),
        [SMEM] + [VMEM] * 6,
    )(place, *rows, own_tokens, text_qkv.transpose(1, 2, 0))
    heads, late_tokens = lax.optimization_barrier((heads, own_tokens))
    mine = lax.all_to_all(heads, "y", 0, 0, tiled=True)
    prompt_in = call(place_kernel, shape((BLOCK, width)), [SMEM] + [VMEM] * 5)(
        place, *rows, late_tokens
    )
    pair = mine[:, 1:]
    near, far = ahead(pair, "z", 1), ahead(pair, "z", 2)
    others = [around(x, "c", 1) for x in (pair, near, far)]
    halves = halves + [around(x, "c", 1) for x in halves]
    sent = call(
        attend_kernel,
        shape((4, 4, HEAD, BLOCK)),
        [SMEM, SMEM] + [VMEM] * 6,
        [pltpu.VMEM((HEAD, 24 * BLOCK), BF)] * 2,
        limit=16,
    )(place, prompt_lengths, mine, near, far, *others)
    context = lax.all_to_all(sent.reshape(16, HEAD, BLOCK), ("t", "y"), 0, 0, tiled=True)
    return call(output_kernel, shape((BLOCK, width)), [SMEM] + [VMEM] * 9)(
        place, context.reshape(4, 2, half, BLOCK), text_out, *halves, prompt_in
    )


def solution(mesh):
    split = Mesh(np.asarray(mesh.devices).reshape(8, 4, 2, 4), ("z", "y", "c", "t"))
    seq = ("z", "y", "c")
    placed = (
        P(seq, None, None),
        P(seq, None),
        P(None, None, "t"),
        P("t", None),
        P("t", None, None),
        P(seq),
        P(seq),
        P(seq, "t"),
        P(),
        P(None, None, "t"),
        P("t", None),
    )
    return jax.shard_map(
        local, mesh=split, in_specs=placed, out_specs=P(seq, None), check_vma=False
    )
```

```python
import jax
import jax.numpy as jnp
import numpy as np
from jax import lax
from jax.experimental import pallas as pl
from jax.experimental.pallas import tpu as pltpu
from jax.sharding import Mesh
from jax.sharding import PartitionSpec as P

HEAD = 88
MAXGRID = 16
BLOCK = 128
MERGED = 64
EPSILON = 1e-06
SCALE2 = HEAD ** (-0.5) / float(np.log(2.0))
BF = jnp.bfloat16
F32 = jnp.float32
I32 = jnp.int32
VMEM = pltpu.VMEM
SMEM = pltpu.SMEM
HBM = pltpu.HBM
FACTS = 128
WINDOW = 18 * BLOCK


def ahead(x, axis, by):
    count = lax.axis_size(axis)
    return lax.ppermute(x, axis, [(i, i + by) for i in range(count - by)])


def around(x, axis, by):
    count = lax.axis_size(axis)
    return lax.ppermute(x, axis, [(i, (i + by) % count) for i in range(count)])


def call(kernel, out_shape, spaces, scratch=(), limit=8):
    single = not isinstance(out_shape, (list, tuple))
    outs = pl.BlockSpec(memory_space=VMEM)
    return pl.pallas_call(
        kernel,
        out_shape=out_shape,
        in_specs=[pl.BlockSpec(memory_space=s) for s in spaces],
        out_specs=outs if single else [outs] * len(out_shape),
        scratch_shapes=scratch,
        compiler_params=pltpu.CompilerParams(vmem_limit_bytes=limit << 20),
    )


def shape(dims, dtype=BF):
    return jax.ShapeDtypeStruct(dims, dtype)


def iota(dims, axis):
    return lax.broadcasted_iota(I32, dims, axis)


def dot(a, b, over):
    return lax.dot_general(
        a, b, (((over[0],), (over[1],)), ((), ())), preferred_element_type=F32
    )


def normalize(values):
    centre = jnp.mean(values, axis=-1, keepdims=True)
    shifted = values - centre
    spread = jnp.mean(shifted * shifted, axis=-1, keepdims=True)
    return (shifted * lax.rsqrt(spread + EPSILON)).astype(BF)


def slot_of(row):
    i, j = row // 128, (row // 64) % 2
    a, b = (row // 8) % 8, row % 8
    return (2 * a + i) * MAXGRID + 2 * b + j


def vision_kernel(
    place_ref, grid_ref, picture_hbm, qkv_hbm, out_hbm, s0_ref, s1_ref, s2_ref, s3_ref,
    picture_ref, qkv_ref, out_ref, arrived,
):
    copies = [pltpu.make_async_copy(picture_hbm, picture_ref, arrived.at[0])]
    for part in range(3):
        copies.append(
            pltpu.make_async_copy(qkv_hbm.at[part], qkv_ref.at[part], arrived.at[1 + part])
        )
    copies.append(pltpu.make_async_copy(out_hbm, out_ref, arrived.at[4]))
    for copy in copies:
        copy.start()
    count = picture_ref.shape[0]
    local_width = qkv_ref.shape[1]
    copies[0].wait()
    normed = normalize(picture_ref[...].astype(F32))
    parts = []
    for part in range(3):
        copies[1 + part].wait()
        parts.append(dot(qkv_ref[part], normed, (1, 1)))
    slots = iota((count, 1), 0)
    usable = (slots // MAXGRID < 2 * grid_ref[0, 0]) & (slots % MAXGRID < 2 * grid_ref[0, 1])
    contexts = []
    for first in range(0, local_width, HEAD):
        q, k, v = (x[first : first + HEAD].astype(BF) for x in parts)
        scores = jnp.where(usable, dot(k, q, (0, 0)), -jnp.inf)
        expons = jnp.exp2((scores - jnp.max(scores, axis=0, keepdims=True)) * SCALE2)
        total = jnp.sum(expons, axis=0, keepdims=True)
        contexts.append(dot(v, expons.astype(BF), (1, 0)) / total)
    context = jnp.concatenate(contexts, axis=0).astype(BF)
    row = (iota((count, count), 0) + place_ref[2] * MERGED) % count
    order = slot_of(row) == iota((count, count), 1)
    context = dot(order.astype(BF), context, (1, 1)).astype(BF)
    copies[4].wait()
    share = dot(context, out_ref[...], (1, 0)).astype(BF)
    for by, share_ref in enumerate((s0_ref, s1_ref, s2_ref, s3_ref)):
        share_ref[...] = share[by * MERGED : (by + 1) * MERGED]


def sum_kernel(parts_ref, rows_ref):
    for y in range(4):
        total = parts_ref[y, 0].astype(F32)
        for t in range(1, 4):
            total = total + parts_ref[y, t].astype(F32)
        rows_ref[y] = total.astype(BF)


def select_kernel(place_ref, mine_ref, other_ref, routed_ref):
    wide = mine_ref.shape[2]
    width = wide - FACTS
    rows = jnp.concatenate(
        [mine_ref[...].reshape(64, wide), other_ref[...].reshape(64, wide)], axis=0
    )
    facts = rows[:, width:].astype(F32)
    block, there = facts[:, 0:1], facts[:, 4:5]
    same_core = block - 2.0 * jnp.floor(block * 0.5) == place_ref[1].astype(F32)
    to = jnp.where(same_core & (there > 0.0), jnp.floor(block * 0.125), -1.0).astype(I32)
    source, target = iota((128, 128), 0), iota((128, 128), 1)
    chosen = (to == target // 16) & (source % 16 == target % 16)
    routed = dot(chosen.astype(BF), rows, (0, 0))
    routed_ref[...] = routed.astype(BF).reshape(8, 16, wide)


def merge_kernel(facts_ref, own_ref, s0_ref, s1_ref, s2_ref, s3_ref, weight_ref, rows_ref):
    width = own_ref.shape[1]
    total = own_ref[...].astype(F32)
    for share in (s0_ref, s1_ref, s2_ref, s3_ref):
        total = total + share[...].astype(F32)
    merged = dot(normalize(total), weight_ref[...], (1, 0)).astype(BF)
    lane = iota((MERGED, FACTS), 1)
    facts = jnp.zeros((MERGED, FACTS), I32)
    for index in range(5):
        facts = jnp.where(lane == index, facts_ref[index], facts)
    facts = facts.astype(F32).astype(BF)
    for y in range(4):
        here = facts_ref[5] == y
        rows_ref[y, :, :width] = jnp.where(here, merged, jnp.zeros_like(merged))
        rows_ref[y, :, width:] = jnp.where(here, facts, jnp.zeros_like(facts))


def placed_rows(place_ref, pieces_refs, tokens_ref):
    width = tokens_ref.shape[1]
    pieces, firsts = [], []
    for by, piece in enumerate(pieces_refs):
        pieces.append(piece[...])
        firsts.append(jnp.full((16, 1), 16 * lax.rem(place_ref[2] + 4 - by, 4), I32))
    rows = jnp.concatenate(pieces, axis=0)
    cell = jnp.concatenate(firsts, axis=0) + iota((MERGED, 1), 0) % 16
    facts = rows[:, width:].astype(F32)
    a, b = (cell // 8).astype(F32), (cell % 8).astype(F32)
    offset, high, wide, there = (facts[:, i : i + 1] for i in (1, 2, 3, 4))
    target = offset + a * wide + b
    usable = (a < high) & (b < wide) & (there > 0.0)
    target = jnp.where(usable, target, -1.0)
    table = (target == iota((MERGED, BLOCK), 1).astype(F32)).astype(BF)
    placed = dot(table, rows, (0, 0))
    covered = placed[:, width + 4 : width + 5] > 0.0
    return jnp.where(covered, placed[:, :width], tokens_ref[...].astype(F32))


def place_kernel(place_ref, r0_ref, r1_ref, r2_ref, r3_ref, tokens_ref, prompt_ref):
    pieces = (r0_ref, r1_ref, r2_ref, r3_ref)
    prompt_ref[...] = placed_rows(place_ref, pieces, tokens_ref).astype(BF)


def project_kernel(
    place_ref, r0_ref, r1_ref, r2_ref, r3_ref, tokens_ref, qkv_ref, heads_ref
):
    pieces = (r0_ref, r1_ref, r2_ref, r3_ref)
    normed = normalize(placed_rows(place_ref, pieces, tokens_ref))
    for part in range(3):
        projected = dot(qkv_ref[part], normed, (1, 1))
        for head in range(4):
            heads_ref[head, part] = projected[head * HEAD : (head + 1) * HEAD].astype(BF)


def attend_kernel(facts_ref, lengths_ref, own_ref, near_ref, far_ref,
                  own2_ref, near2_ref, far2_ref, sent_ref, keys_ref, values_ref):
    z, c = facts_ref[0], facts_ref[1]
    for plane, (mine, other) in enumerate(
        ((far_ref, far2_ref), (near_ref, near2_ref), (own_ref, own2_ref))
    ):
        skip = 1 if plane == 2 else 0
        for y in range(4):
            at = (plane * 8 + 2 * y) * BLOCK
            for half in range(2):
                lanes = pl.ds(at + half * BLOCK, BLOCK)
                for part, store in ((0, keys_ref), (1, values_ref)):
                    picked = jnp.where(
                        c == half, mine[y, skip + part], other[y, part]
                    )
                    store[:, lanes] = picked
    row = iota((BLOCK, 1), 0)
    column = iota((BLOCK, WINDOW), 1)
    for j in range(4):
        base = (z - 2) * 1024 + j * 256
        here = 2048 + c * BLOCK + row
        start = jnp.zeros((BLOCK, 1), I32)
        end = jnp.int32(0)
        for prompt in range(16):
            end = end + lengths_ref[prompt]
            start = jnp.where(end <= here + base, end, start)
        query = own_ref[j, 0]
        window = pl.ds(j * 256, WINDOW)
        scores = dot(query, keys_ref[:, window], (0, 0))
        visible = (column <= here) & (column >= start - base)
        scores = jnp.where(visible, scores, -jnp.inf)
        expons = jnp.exp2((scores - jnp.max(scores, axis=1, keepdims=True)) * SCALE2)
        total = jnp.sum(expons, axis=1, keepdims=True)
        summed = dot(values_ref[:, window], expons.astype(BF), (1, 1))
        total = jnp.transpose(jnp.broadcast_to(total, (BLOCK, BLOCK)))
        context = (summed / total[:HEAD]).astype(BF)
        for t in range(4):
            sent_ref[t, j] = context


def output_kernel(
    place_ref, context_ref, w0_ref, m2_ref, m1_ref, m3_ref, o2_ref, o1_ref, o3_ref,
    prompt_ref, out_ref,
):
    c, t = place_ref[1], place_ref[2]
    half = m1_ref.shape[0]
    width = out_ref.shape[1]
    pairs = [(context_ref[t, part].T, w0_ref.at[part * half : (part + 1) * half]) for part in (0, 1)]
    for by, mine, other in ((1, m1_ref, o1_ref), (2, m2_ref, o2_ref), (3, m3_ref, o3_ref)):
        source = lax.rem(t + 4 - by, 4)
        pairs.append((context_ref[source, c].T, mine))
        pairs.append((context_ref[source, 1 - c].T, other))
    for first in range(0, width, 256):
        strip = slice(first, min(first + 256, width))
        total = prompt_ref[:, strip].astype(F32)
        for context, weight in pairs:
            total = total + dot(context, weight[:, strip], (1, 0))
        out_ref[:, strip] = total.astype(BF)


def local(
    patches,
    picture_grid,
    vision_qkv,
    vision_out,
    merge_weight,
    picture_block,
    picture_offset,
    tokens,
    prompt_lengths,
    text_qkv,
    text_out,
):
    count, width = patches.shape[1:]
    local_width = vision_qkv.shape[2]
    wide = width + FACTS
    z = lax.axis_index("z")
    c = lax.axis_index("c")
    t = lax.axis_index("t")
    picture = patches[0]
    block = picture_block[0]

    place = jnp.stack([z, c, t]).astype(I32)
    share = call(
        vision_kernel,
        [shape((MERGED, width))] * 4,
        [SMEM, SMEM, HBM, HBM, HBM],
        [
            VMEM((count, width), BF),
            VMEM((3, local_width, width), BF),
            VMEM((local_width, width), BF),
            pltpu.SemaphoreType.DMA((5,)),
        ],
        limit=60,
    )(place, picture_grid, picture, vision_qkv.transpose(1, 2, 0), vision_out)
    shares = [share[0]] + [around(share[by], "t", by) for by in range(1, 4)]
    chosen = slot_of(t * MERGED + jnp.arange(MERGED))[:, None] == jnp.arange(count)[None, :]
    own = jnp.dot(chosen.astype(BF), picture, preferred_element_type=F32).astype(BF)
    facts = jnp.stack([block, picture_offset[0], picture_grid[0, 0], picture_grid[0, 1], 1])
    facts = jnp.where(t == 0, facts, 0)
    facts = jnp.concatenate([facts, (block % 8 // 2)[None]]).astype(I32)
    routed = call(merge_kernel, shape((4, MERGED, wide)), [SMEM] + [VMEM] * 6)(
        facts, own, *shares, merge_weight[0]
    )

    got = lax.all_to_all(routed.reshape(16, 16, wide), ("y", "t"), 0, 0, tiled=True)
    got = call(sum_kernel, shape((4, 16, wide)), [VMEM])(got.reshape(4, 4, 16, wide))
    other = around(got, "c", 1)
    routed = call(select_kernel, shape((8, 16, wide)), [SMEM, VMEM, VMEM])(place, got, other)
    routed, text_out = lax.optimization_barrier((routed, text_out))
    half = local_width // 2
    near_half = lax.dynamic_slice_in_dim(text_out, c * half, half, 0)
    near_half, tokens = lax.optimization_barrier((near_half, tokens))
    halves = [None] + [around(near_half, "t", by) for by in (1, 3)]
    pieces = [tokens] + [around(tokens, "t", by) for by in range(1, 4)]
    got = lax.all_to_all(routed, "z", 0, 0, tiled=True)
    got = jnp.sum(got.astype(F32), axis=0).astype(BF)
    rows = [got] + [around(got, "t", by) for by in range(1, 4)]
    own_tokens = jnp.zeros((4, BLOCK, local_width), BF)
    for by, piece in enumerate(pieces):
        own_tokens = lax.dynamic_update_index_in_dim(own_tokens, piece, (t - by) % 4, 0)
    own_tokens = own_tokens.transpose(1, 0, 2).reshape(BLOCK, width)
    heads = call(
        project_kernel,
        shape((4, 3, HEAD, BLOCK)),
        [SMEM] + [VMEM] * 6,
    )(place, *rows, own_tokens, text_qkv.transpose(1, 2, 0))
    heads, late_tokens, near_half = lax.optimization_barrier((heads, own_tokens, near_half))
    halves[0] = around(near_half, "t", 2)
    mine = lax.all_to_all(heads, "y", 0, 0, tiled=True)
    prompt_in = call(place_kernel, shape((BLOCK, width)), [SMEM] + [VMEM] * 5)(
        place, *rows, late_tokens
    )
    pair = mine[:, 1:]
    near, far = ahead(pair, "z", 1), ahead(pair, "z", 2)
    others = [around(x, "c", 1) for x in (pair, near, far)]
    halves = halves + [around(x, "c", 1) for x in halves]
    sent = call(
        attend_kernel,
        shape((4, 4, HEAD, BLOCK)),
        [SMEM, SMEM] + [VMEM] * 6,
        [pltpu.VMEM((HEAD, 24 * BLOCK), BF)] * 2,
        limit=16,
    )(place, prompt_lengths, mine, near, far, *others)
    context = lax.all_to_all(sent.reshape(16, HEAD, BLOCK), ("t", "y"), 0, 0, tiled=True)
    return call(output_kernel, shape((BLOCK, width)), [SMEM] + [VMEM] * 9)(
        place, context.reshape(4, 2, half, BLOCK), text_out, *halves, prompt_in
    )


def solution(mesh):
    split = Mesh(np.asarray(mesh.devices).reshape(8, 4, 2, 4), ("z", "y", "c", "t"))
    seq = ("z", "y", "c")
    placed = (
        P(seq, None, None),
        P(seq, None),
        P(None, None, "t"),
        P("t", None),
        P("t", None, None),
        P(seq),
        P(seq),
        P(seq, "t"),
        P(),
        P(None, None, "t"),
        P("t", None),
    )
    return jax.shard_map(
        local, mesh=split, in_specs=placed, out_specs=P(seq, None), check_vma=False
    )
```

```python
import jax
import jax.numpy as jnp
import numpy as np
from jax import lax
from jax.experimental import pallas as pl
from jax.experimental.pallas import tpu as pltpu
from jax.sharding import Mesh
from jax.sharding import PartitionSpec as P

HEAD = 88
MAXGRID = 16
BLOCK = 128
MERGED = 64
EPSILON = 1e-06
SCALE2 = HEAD ** (-0.5) / float(np.log(2.0))
BF = jnp.bfloat16
F32 = jnp.float32
I32 = jnp.int32
VMEM = pltpu.VMEM
SMEM = pltpu.SMEM
HBM = pltpu.HBM
FACTS = 128
STRIP = 256
WINDOW = 18 * BLOCK


def ahead(x, axis, by):
    count = lax.axis_size(axis)
    return lax.ppermute(x, axis, [(i, i + by) for i in range(count - by)])


def around(x, axis, by):
    count = lax.axis_size(axis)
    return lax.ppermute(x, axis, [(i, (i + by) % count) for i in range(count)])


def call(kernel, out_shape, spaces, scratch=(), limit=8, flops=None):
    single = not isinstance(out_shape, (list, tuple))
    outs = pl.BlockSpec(memory_space=VMEM)
    cost = flops and pl.CostEstimate(flops=flops, transcendentals=0, bytes_accessed=flops // 400)
    return pl.pallas_call(
        kernel,
        out_shape=out_shape,
        in_specs=[pl.BlockSpec(memory_space=s) for s in spaces],
        out_specs=outs if single else [outs] * len(out_shape),
        scratch_shapes=scratch,
        compiler_params=pltpu.CompilerParams(vmem_limit_bytes=limit << 20),
        cost_estimate=cost,
    )


def shape(dims, dtype=BF):
    return jax.ShapeDtypeStruct(dims, dtype)


def iota(dims, axis):
    return lax.broadcasted_iota(I32, dims, axis)


def dot(a, b, over):
    return lax.dot_general(
        a, b, (((over[0],), (over[1],)), ((), ())), preferred_element_type=F32
    )


def normalize(values):
    centre = jnp.mean(values, axis=-1, keepdims=True)
    shifted = values - centre
    spread = jnp.mean(shifted * shifted, axis=-1, keepdims=True)
    return (shifted * lax.rsqrt(spread + EPSILON)).astype(BF)


def slot_of(row):
    i, j = row // 128, (row // 64) % 2
    a, b = (row // 8) % 8, row % 8
    return (2 * a + i) * MAXGRID + 2 * b + j


def vision_kernel(
    place_ref, grid_ref, picture_hbm, qkv_hbm, out_hbm, s0_ref, s1_ref, s2_ref, s3_ref,
    picture_ref, qkv_ref, out_ref, arrived,
):
    copies = [pltpu.make_async_copy(picture_hbm, picture_ref, arrived.at[0])]
    for part in range(3):
        copies.append(
            pltpu.make_async_copy(qkv_hbm.at[part], qkv_ref.at[part], arrived.at[1 + part])
        )
    copies.append(pltpu.make_async_copy(out_hbm, out_ref, arrived.at[4]))
    for copy in copies:
        copy.start()
    count = picture_ref.shape[0]
    local_width = qkv_ref.shape[1]
    copies[0].wait()
    normed = normalize(picture_ref[...].astype(F32))
    parts = []
    for part in range(3):
        copies[1 + part].wait()
        parts.append(dot(qkv_ref[part], normed, (1, 1)))
    slots = iota((count, 1), 0)
    usable = (slots // MAXGRID < 2 * grid_ref[0, 0]) & (slots % MAXGRID < 2 * grid_ref[0, 1])
    contexts = []
    for first in range(0, local_width, HEAD):
        q, k, v = (x[first : first + HEAD].astype(BF) for x in parts)
        scores = jnp.where(usable, dot(k, q, (0, 0)), -jnp.inf)
        expons = jnp.exp2((scores - jnp.max(scores, axis=0, keepdims=True)) * SCALE2)
        total = jnp.sum(expons, axis=0, keepdims=True)
        contexts.append(dot(v, expons.astype(BF), (1, 0)) / total)
    context = jnp.concatenate(contexts, axis=0).astype(BF)
    row = (iota((count, count), 0) + place_ref[2] * MERGED) % count
    order = slot_of(row) == iota((count, count), 1)
    context = dot(order.astype(BF), context, (1, 1)).astype(BF)
    copies[4].wait()
    share = dot(context, out_ref[...], (1, 0)).astype(BF)
    for by, share_ref in enumerate((s0_ref, s1_ref, s2_ref, s3_ref)):
        share_ref[...] = share[by * MERGED : (by + 1) * MERGED]


def sum_kernel(parts_ref, rows_ref):
    for y in range(4):
        total = parts_ref[y, 0].astype(F32)
        for t in range(1, 4):
            total = total + parts_ref[y, t].astype(F32)
        rows_ref[y] = total.astype(BF)


def select_kernel(place_ref, mine_ref, other_ref, routed_ref):
    wide = mine_ref.shape[2]
    width = wide - FACTS
    rows = jnp.concatenate(
        [mine_ref[...].reshape(64, wide), other_ref[...].reshape(64, wide)], axis=0
    )
    facts = rows[:, width:].astype(F32)
    block, there = facts[:, 0:1], facts[:, 4:5]
    same_core = block - 2.0 * jnp.floor(block * 0.5) == place_ref[1].astype(F32)
    to = jnp.where(same_core & (there > 0.0), jnp.floor(block * 0.125), -1.0).astype(I32)
    source, target = iota((128, 128), 0), iota((128, 128), 1)
    chosen = (to == target // 16) & (source % 16 == target % 16)
    routed = dot(chosen.astype(BF), rows, (0, 0))
    routed_ref[...] = routed.astype(BF).reshape(8, 16, wide)


def own_kernel(place_ref, picture_ref, share_ref, own_ref):
    count = picture_ref.shape[0]
    row = iota((MERGED, count), 0) + place_ref[2] * MERGED
    chosen = (slot_of(row) == iota((MERGED, count), 1)).astype(BF)
    own_ref[...] = dot(chosen, picture_ref[...], (1, 0)) + share_ref[...].astype(F32)


def merge_kernel(facts_ref, own_ref, s1_ref, s2_ref, s3_ref, top_ref, low_ref, rows_ref):
    width = own_ref.shape[1]
    total = own_ref[...]
    for share in (s1_ref, s2_ref, s3_ref):
        total = total + share[...].astype(F32)
    normed = normalize(total)
    deep = top_ref.shape[0]
    merged = dot(normed[:, :deep], top_ref[...], (1, 0))
    merged = (merged + dot(normed[:, deep:], low_ref[...], (1, 0))).astype(BF)
    lane = iota((MERGED, FACTS), 1)
    facts = jnp.zeros((MERGED, FACTS), I32)
    for index in range(5):
        facts = jnp.where(lane == index, facts_ref[index], facts)
    facts = facts.astype(F32).astype(BF)
    for y in range(4):
        here = facts_ref[5] == y
        rows_ref[y, :, :width] = jnp.where(here, merged, jnp.zeros_like(merged))
        rows_ref[y, :, width:] = jnp.where(here, facts, jnp.zeros_like(facts))


def placed_rows(place_ref, pieces_refs, tokens_ref):
    width = tokens_ref.shape[1]
    pieces, firsts = [], []
    for by, piece in enumerate(pieces_refs):
        pieces.append(piece[...])
        firsts.append(jnp.full((16, 1), 16 * lax.rem(place_ref[2] + 4 - by, 4), I32))
    rows = jnp.concatenate(pieces, axis=0)
    cell = jnp.concatenate(firsts, axis=0) + iota((MERGED, 1), 0) % 16
    facts = rows[:, width:].astype(F32)
    a, b = (cell // 8).astype(F32), (cell % 8).astype(F32)
    offset, high, wide, there = (facts[:, i : i + 1] for i in (1, 2, 3, 4))
    target = offset + a * wide + b
    usable = (a < high) & (b < wide) & (there > 0.0)
    target = jnp.where(usable, target, -1.0)
    table = (target == iota((MERGED, BLOCK), 1).astype(F32)).astype(BF)
    placed = dot(table, rows, (0, 0))
    covered = placed[:, width + 4 : width + 5] > 0.0
    return jnp.where(covered, placed[:, :width], tokens_ref[...].astype(F32))


def place_kernel(place_ref, r0_ref, r1_ref, r2_ref, r3_ref, tokens_ref, prompt_ref):
    pieces = (r0_ref, r1_ref, r2_ref, r3_ref)
    prompt_ref[...] = placed_rows(place_ref, pieces, tokens_ref).astype(BF)


def project_kernel(
    place_ref, r0_ref, r1_ref, r2_ref, r3_ref, tokens_ref, qkv_ref, heads_ref
):
    pieces = (r0_ref, r1_ref, r2_ref, r3_ref)
    normed = normalize(placed_rows(place_ref, pieces, tokens_ref))
    for part in range(3):
        projected = dot(qkv_ref[part], normed, (1, 1))
        for head in range(4):
            heads_ref[head, part] = projected[head * HEAD : (head + 1) * HEAD].astype(BF)


def attend_kernel(facts_ref, lengths_ref, own_ref, near_ref, far_ref,
                  own2_ref, near2_ref, far2_ref, sent_ref, keys_ref, values_ref):
    z, c = facts_ref[0], facts_ref[1]
    for plane, (mine, other) in enumerate(
        ((far_ref, far2_ref), (near_ref, near2_ref), (own_ref, own2_ref))
    ):
        skip = 1 if plane == 2 else 0
        for y in range(4):
            at = (plane * 8 + 2 * y) * BLOCK
            mine_at = pl.ds(pl.multiple_of(at + c * BLOCK, BLOCK), BLOCK)
            other_at = pl.ds(pl.multiple_of(at + (1 - c) * BLOCK, BLOCK), BLOCK)
            for part, store in ((0, keys_ref), (1, values_ref)):
                store[:, mine_at] = mine[y, skip + part]
                store[:, other_at] = other[y, part]
    row = iota((BLOCK, 1), 0)
    column = iota((BLOCK, STRIP), 1)
    for j in range(4):
        base = (z - 2) * 1024 + j * 256
        here = 2048 + c * BLOCK + row
        start = jnp.zeros((BLOCK, 1), I32)
        end = jnp.int32(0)
        for prompt in range(16):
            end = end + lengths_ref[prompt]
            start = jnp.where(end <= here + base, end, start)
        low = start - base
        query = own_ref[j, 0].T
        strips, top = [], None
        for first in range(0, WINDOW, STRIP):
            scores = dot(query, keys_ref[:, pl.ds(j * 256 + first, STRIP)], (1, 0))
            visible = column >= low - first
            if first + STRIP > 2048:
                visible = visible & (column <= here - first)
            scores = jnp.where(visible, scores, -jnp.inf)
            top = scores if top is None else jnp.maximum(top, scores)
            strips.append(scores)
        top = jnp.max(top, axis=1, keepdims=True)
        total = jnp.zeros((BLOCK, STRIP), F32)
        summed = jnp.zeros((HEAD, BLOCK), F32)
        for strip, scores in enumerate(strips):
            expons = jnp.exp2((scores - top) * SCALE2)
            total = total + expons
            values = values_ref[:, pl.ds(j * 256 + strip * STRIP, STRIP)]
            summed = summed + dot(values, expons.astype(BF), (1, 1))
        total = jnp.sum(total, axis=1, keepdims=True)
        total = jnp.transpose(jnp.broadcast_to(total, (BLOCK, BLOCK)))
        context = (summed / total[:HEAD]).astype(BF)
        for t in range(4):
            sent_ref[t, j] = context


def output_kernel(
    place_ref, context_ref, w0_ref, m2_ref, m1_ref, m3_ref, o2_ref, o1_ref, o3_ref,
    prompt_ref, out_ref,
):
    c, t = place_ref[1], place_ref[2]
    half = m1_ref.shape[0]
    width = out_ref.shape[1]
    pairs = [(context_ref[t, part].T, w0_ref.at[part * half : (part + 1) * half]) for part in (0, 1)]
    for by, mine, other in ((1, m1_ref, o1_ref), (2, m2_ref, o2_ref), (3, m3_ref, o3_ref)):
        source = lax.rem(t + 4 - by, 4)
        pairs.append((context_ref[source, c].T, mine))
        pairs.append((context_ref[source, 1 - c].T, other))
    for first in range(0, width, 256):
        strip = slice(first, min(first + 256, width))
        total = prompt_ref[:, strip].astype(F32)
        for context, weight in pairs:
            total = total + dot(context, weight[:, strip], (1, 0))
        out_ref[:, strip] = total.astype(BF)


def local(
    patches,
    picture_grid,
    vision_qkv,
    vision_out,
    merge_weight,
    picture_block,
    picture_offset,
    tokens,
    prompt_lengths,
    text_qkv,
    text_out,
):
    count, width = patches.shape[1:]
    local_width = vision_qkv.shape[2]
    wide = width + FACTS
    z = lax.axis_index("z")
    c = lax.axis_index("c")
    t = lax.axis_index("t")
    picture = patches[0]
    block = picture_block[0]

    place = jnp.stack([z, c, t]).astype(I32)
    share = call(
        vision_kernel,
        [shape((MERGED, width))] * 4,
        [SMEM, SMEM, HBM, HBM, HBM],
        [
            VMEM((count, width), BF),
            VMEM((3, local_width, width), BF),
            VMEM((local_width, width), BF),
            pltpu.SemaphoreType.DMA((5,)),
        ],
        limit=60,
    )(place, picture_grid, picture, vision_qkv.transpose(1, 2, 0), vision_out)
    shares = [around(share[by], "t", by) for by in range(1, 4)]
    own = call(own_kernel, shape((MERGED, width), F32), [SMEM, VMEM, VMEM], flops=8 * 10**9)(
        place, picture, share[0]
    )
    own, merge_weight = lax.optimization_barrier((own, merge_weight))
    merge_parts = (merge_weight[0, : width // 2], merge_weight[0, width // 2 :])
    facts = jnp.stack([block, picture_offset[0], picture_grid[0, 0], picture_grid[0, 1], 1])
    facts = jnp.where(t == 0, facts, 0)
    facts = jnp.concatenate([facts, (block % 8 // 2)[None]]).astype(I32)
    routed = call(merge_kernel, shape((4, MERGED, wide)), [SMEM] + [VMEM] * 6)(
        facts, own, *shares, *merge_parts
    )

    got = lax.all_to_all(routed.reshape(16, 16, wide), ("y", "t"), 0, 0, tiled=True)
    got = call(sum_kernel, shape((4, 16, wide)), [VMEM])(got.reshape(4, 4, 16, wide))
    other = around(got, "c", 1)
    routed = call(select_kernel, shape((8, 16, wide)), [SMEM, VMEM, VMEM])(place, got, other)
    routed, text_out = lax.optimization_barrier((routed, text_out))
    half = local_width // 2
    near_half = lax.dynamic_slice_in_dim(text_out, c * half, half, 0)
    near_half, tokens = lax.optimization_barrier((near_half, tokens))
    halves = [None] + [around(near_half, "t", by) for by in (1, 3)]
    pieces = [tokens] + [around(tokens, "t", by) for by in range(1, 4)]
    got = lax.all_to_all(routed, "z", 0, 0, tiled=True)
    got = jnp.sum(got.astype(F32), axis=0).astype(BF)
    rows = [got] + [around(got, "t", by) for by in range(1, 4)]
    own_tokens = jnp.zeros((4, BLOCK, local_width), BF)
    for by, piece in enumerate(pieces):
        own_tokens = lax.dynamic_update_index_in_dim(own_tokens, piece, (t - by) % 4, 0)
    own_tokens = own_tokens.transpose(1, 0, 2).reshape(BLOCK, width)
    heads = call(
        project_kernel,
        shape((4, 3, HEAD, BLOCK)),
        [SMEM] + [VMEM] * 6,
    )(place, *rows, own_tokens, text_qkv.transpose(1, 2, 0))
    heads, late_tokens, near_half = lax.optimization_barrier((heads, own_tokens, near_half))
    halves[0] = around(near_half, "t", 2)
    mine = lax.all_to_all(heads, "y", 0, 0, tiled=True)
    prompt_in = call(place_kernel, shape((BLOCK, width)), [SMEM] + [VMEM] * 5)(
        place, *rows, late_tokens
    )
    pair = mine[:, 1:]
    near, far = ahead(pair, "z", 1), ahead(pair, "z", 2)
    others = [around(x, "c", 1) for x in (pair, near, far)]
    halves = halves + [around(x, "c", 1) for x in halves]
    sent = call(
        attend_kernel,
        shape((4, 4, HEAD, BLOCK)),
        [SMEM, SMEM] + [VMEM] * 6,
        [pltpu.VMEM((HEAD, 24 * BLOCK), BF)] * 2,
        limit=16,
    )(place, prompt_lengths, mine, near, far, *others)
    context = lax.all_to_all(sent.reshape(16, HEAD, BLOCK), ("t", "y"), 0, 0, tiled=True)
    return call(output_kernel, shape((BLOCK, width)), [SMEM] + [VMEM] * 9)(
        place, context.reshape(4, 2, half, BLOCK), text_out, *halves, prompt_in
    )


def solution(mesh):
    split = Mesh(np.asarray(mesh.devices).reshape(8, 4, 2, 4), ("z", "y", "c", "t"))
    seq = ("z", "y", "c")
    placed = (
        P(seq, None, None),
        P(seq, None),
        P(None, None, "t"),
        P("t", None),
        P("t", None, None),
        P(seq),
        P(seq),
        P(seq, "t"),
        P(),
        P(None, None, "t"),
        P("t", None),
    )
    return jax.shard_map(
        local, mesh=split, in_specs=placed, out_specs=P(seq, None), check_vma=False
    )
```

```python
import jax
import jax.numpy as jnp
import numpy as np
from jax import lax
from jax.experimental import pallas as pl
from jax.experimental.pallas import tpu as pltpu
from jax.sharding import Mesh
from jax.sharding import PartitionSpec as P

HEAD = 88
MAXGRID = 16
BLOCK = 128
MERGED = 64
EPSILON = 1e-06
SCALE2 = HEAD ** (-0.5) / float(np.log(2.0))
BF = jnp.bfloat16
F32 = jnp.float32
I32 = jnp.int32
VMEM = pltpu.VMEM
SMEM = pltpu.SMEM
HBM = pltpu.HBM
FACTS = 128
STRIP = 256


def ahead(x, axis, by):
    count = lax.axis_size(axis)
    return lax.ppermute(x, axis, [(i, i + by) for i in range(count - by)])


def around(x, axis, by):
    count = lax.axis_size(axis)
    return lax.ppermute(x, axis, [(i, (i + by) % count) for i in range(count)])


def call(kernel, out_shape, spaces, scratch=(), limit=8, flops=None):
    single = not isinstance(out_shape, (list, tuple))
    outs = pl.BlockSpec(memory_space=VMEM)
    cost = flops and pl.CostEstimate(flops=flops, transcendentals=0, bytes_accessed=flops // 400)
    return pl.pallas_call(
        kernel,
        out_shape=out_shape,
        in_specs=[pl.BlockSpec(memory_space=s) for s in spaces],
        out_specs=outs if single else [outs] * len(out_shape),
        scratch_shapes=scratch,
        compiler_params=pltpu.CompilerParams(vmem_limit_bytes=limit << 20),
        cost_estimate=cost,
    )


def shape(dims, dtype=BF):
    return jax.ShapeDtypeStruct(dims, dtype)


def iota(dims, axis):
    return lax.broadcasted_iota(I32, dims, axis)


def dot(a, b, over):
    return lax.dot_general(
        a, b, (((over[0],), (over[1],)), ((), ())), preferred_element_type=F32
    )


def normalize(values):
    centre = jnp.mean(values, axis=-1, keepdims=True)
    shifted = values - centre
    spread = jnp.mean(shifted * shifted, axis=-1, keepdims=True)
    return (shifted * lax.rsqrt(spread + EPSILON)).astype(BF)


def slot_of(row):
    i, j = row // 128, (row // 64) % 2
    a, b = (row // 8) % 8, row % 8
    return (2 * a + i) * MAXGRID + 2 * b + j


def vision_kernel(
    place_ref, grid_ref, picture_hbm, qkv_hbm, out_hbm, s0_ref, s1_ref, s2_ref, s3_ref,
    picture_ref, qkv_ref, out_ref, arrived,
):
    copies = [pltpu.make_async_copy(picture_hbm, picture_ref, arrived.at[0])]
    for part in range(3):
        copies.append(
            pltpu.make_async_copy(qkv_hbm.at[part], qkv_ref.at[part], arrived.at[1 + part])
        )
    copies.append(pltpu.make_async_copy(out_hbm, out_ref, arrived.at[4]))
    for copy in copies:
        copy.start()
    count = picture_ref.shape[0]
    local_width = qkv_ref.shape[1]
    copies[0].wait()
    normed = normalize(picture_ref[...].astype(F32))
    parts = []
    for part in range(3):
        copies[1 + part].wait()
        parts.append(dot(qkv_ref[part], normed, (1, 1)))
    slots = iota((count, 1), 0)
    usable = (slots // MAXGRID < 2 * grid_ref[0, 0]) & (slots % MAXGRID < 2 * grid_ref[0, 1])
    contexts = []
    for first in range(0, local_width, HEAD):
        q, k, v = (x[first : first + HEAD].astype(BF) for x in parts)
        scores = jnp.where(usable, dot(k, q, (0, 0)), -jnp.inf)
        expons = jnp.exp2((scores - jnp.max(scores, axis=0, keepdims=True)) * SCALE2)
        total = jnp.sum(expons, axis=0, keepdims=True)
        contexts.append(dot(v, expons.astype(BF), (1, 0)) / total)
    context = jnp.concatenate(contexts, axis=0).astype(BF)
    row = (iota((count, count), 0) + place_ref[2] * MERGED) % count
    order = slot_of(row) == iota((count, count), 1)
    context = dot(order.astype(BF), context, (1, 1)).astype(BF)
    copies[4].wait()
    share = dot(context, out_ref[...], (1, 0)).astype(BF)
    for by, share_ref in enumerate((s0_ref, s1_ref, s2_ref, s3_ref)):
        share_ref[...] = share[by * MERGED : (by + 1) * MERGED]


def sum_kernel(parts_ref, rows_ref):
    for y in range(4):
        total = parts_ref[y, 0].astype(F32)
        for t in range(1, 4):
            total = total + parts_ref[y, t].astype(F32)
        rows_ref[y] = total.astype(BF)


def select_kernel(place_ref, mine_ref, other_ref, routed_ref):
    wide = mine_ref.shape[2]
    width = wide - FACTS
    rows = jnp.concatenate(
        [mine_ref[...].reshape(64, wide), other_ref[...].reshape(64, wide)], axis=0
    )
    facts = rows[:, width:].astype(F32)
    block, there = facts[:, 0:1], facts[:, 4:5]
    same_core = block - 2.0 * jnp.floor(block * 0.5) == place_ref[1].astype(F32)
    to = jnp.where(same_core & (there > 0.0), jnp.floor(block * 0.125), -1.0).astype(I32)
    source, target = iota((128, 128), 0), iota((128, 128), 1)
    chosen = (to == target // 16) & (source % 16 == target % 16)
    routed = dot(chosen.astype(BF), rows, (0, 0))
    routed_ref[...] = routed.astype(BF).reshape(8, 16, wide)


def own_kernel(place_ref, picture_ref, share_ref, own_ref):
    count = picture_ref.shape[0]
    row = iota((MERGED, count), 0) + place_ref[2] * MERGED
    chosen = (slot_of(row) == iota((MERGED, count), 1)).astype(BF)
    own_ref[...] = dot(chosen, picture_ref[...], (1, 0)) + share_ref[...].astype(F32)


def merge_kernel(facts_ref, own_ref, s1_ref, s2_ref, s3_ref, top_ref, low_ref, rows_ref):
    width = own_ref.shape[1]
    total = own_ref[...]
    for share in (s1_ref, s2_ref, s3_ref):
        total = total + share[...].astype(F32)
    normed = normalize(total)
    deep = top_ref.shape[0]
    merged = dot(normed[:, :deep], top_ref[...], (1, 0))
    merged = (merged + dot(normed[:, deep:], low_ref[...], (1, 0))).astype(BF)
    lane = iota((MERGED, FACTS), 1)
    facts = jnp.zeros((MERGED, FACTS), I32)
    for index in range(5):
        facts = jnp.where(lane == index, facts_ref[index], facts)
    facts = facts.astype(F32).astype(BF)
    for y in range(4):
        here = facts_ref[5] == y
        rows_ref[y, :, :width] = jnp.where(here, merged, jnp.zeros_like(merged))
        rows_ref[y, :, width:] = jnp.where(here, facts, jnp.zeros_like(facts))


def placed_rows(place_ref, pieces_refs, tokens_ref):
    width = tokens_ref.shape[1]
    pieces, firsts = [], []
    for by, piece in enumerate(pieces_refs):
        pieces.append(piece[...])
        firsts.append(jnp.full((16, 1), 16 * lax.rem(place_ref[2] + 4 - by, 4), I32))
    rows = jnp.concatenate(pieces, axis=0)
    cell = jnp.concatenate(firsts, axis=0) + iota((MERGED, 1), 0) % 16
    facts = rows[:, width:].astype(F32)
    a, b = (cell // 8).astype(F32), (cell % 8).astype(F32)
    offset, high, wide, there = (facts[:, i : i + 1] for i in (1, 2, 3, 4))
    target = offset + a * wide + b
    usable = (a < high) & (b < wide) & (there > 0.0)
    target = jnp.where(usable, target, -1.0)
    table = (target == iota((MERGED, BLOCK), 1).astype(F32)).astype(BF)
    placed = dot(table, rows, (0, 0))
    covered = placed[:, width + 4 : width + 5] > 0.0
    return jnp.where(covered, placed[:, :width], tokens_ref[...].astype(F32))


def place_kernel(place_ref, r0_ref, r1_ref, r2_ref, r3_ref, tokens_ref, prompt_ref):
    pieces = (r0_ref, r1_ref, r2_ref, r3_ref)
    prompt_ref[...] = placed_rows(place_ref, pieces, tokens_ref).astype(BF)


def project_kernel(
    place_ref, r0_ref, r1_ref, r2_ref, r3_ref, tokens_ref, qkv_ref, heads_ref
):
    pieces = (r0_ref, r1_ref, r2_ref, r3_ref)
    normed = normalize(placed_rows(place_ref, pieces, tokens_ref))
    for part in range(3):
        projected = dot(qkv_ref[part], normed, (1, 1))
        for head in range(4):
            heads_ref[head, part] = projected[head * HEAD : (head + 1) * HEAD].astype(BF)


def cut_kernel(place_ref, after_hbm, text_hbm, tokens_hbm, near_hbm, copy_hbm, done):
    half = near_hbm.shape[0]
    mine = text_hbm.at[pl.ds(pl.multiple_of(place_ref[1] * half, 16), half)]
    copies = [
        pltpu.make_async_copy(mine, near_hbm, done.at[0]),
        pltpu.make_async_copy(tokens_hbm, copy_hbm, done.at[1]),
    ]
    for copy in copies:
        copy.start()
    for copy in copies:
        copy.wait()


def prompt_start(lengths_ref, position):
    start = jnp.zeros(position.shape, I32)
    end = jnp.int32(0)
    for prompt in range(16):
        end = end + lengths_ref[prompt]
        start = jnp.where(end <= position, end, start)
    return start


def lay_keys(c, planes, keys_ref, values_ref):
    for plane, (mine, other, skip) in enumerate(planes):
        for y in range(4):
            at = (plane * 8 + 2 * y) * BLOCK
            mine_at = pl.ds(pl.multiple_of(at + c * BLOCK, BLOCK), BLOCK)
            other_at = pl.ds(pl.multiple_of(at + (1 - c) * BLOCK, BLOCK), BLOCK)
            for part, store in ((0, keys_ref), (1, values_ref)):
                store[:, mine_at] = mine[y, skip + part]
                store[:, other_at] = other[y, part]


def turned(column):
    return jnp.transpose(jnp.broadcast_to(column, (BLOCK, BLOCK)))


def weigh(strips, top, values_of):
    total = jnp.zeros((BLOCK, STRIP), F32)
    summed = jnp.zeros((HEAD, BLOCK), F32)
    for first, scores in strips:
        expons = jnp.exp2((scores - top) * SCALE2)
        total = total + expons
        summed = summed + dot(values_of(first), expons.astype(BF), (1, 1))
    return jnp.sum(total, axis=1, keepdims=True), summed


def near_kernel(place_ref, lengths_ref, own_ref, near_ref, own2_ref, near2_ref,
                top_ref, total_ref, summed_ref, keys_ref, values_ref):
    z, c = place_ref[0], place_ref[1]
    planes = ((near_ref, near2_ref, 0), (own_ref, own2_ref, 1))
    lay_keys(c, planes, keys_ref, values_ref)
    column = iota((BLOCK, STRIP), 1)
    for j in range(4):
        here = 1024 + j * 256 + c * BLOCK + iota((BLOCK, 1), 0)
        base = (z - 1) * 1024
        low = prompt_start(lengths_ref, here + base) - base
        query = own_ref[j, 0].T
        strips, top = [], None
        for first in range(0, 1024 + (j + 1) * 256, STRIP):
            scores = dot(query, keys_ref[:, first : first + STRIP], (1, 0))
            visible = column >= low - first
            if first >= 1024:
                visible = visible & (column <= here - first)
            scores = jnp.where(visible, scores, -jnp.inf)
            top = scores if top is None else jnp.maximum(top, scores)
            strips.append((first, scores))
        top = jnp.max(top, axis=1, keepdims=True)
        total, summed = weigh(strips, top, lambda first: values_ref[:, first : first + STRIP])
        top_ref[j] = jnp.broadcast_to(top, (BLOCK, BLOCK))
        total_ref[j] = turned(total)[:8]
        summed_ref[j] = summed


def far_kernel(place_ref, lengths_ref, own_ref, far_ref, far2_ref,
               top_ref, total_ref, summed_ref, sent_ref, keys_ref, values_ref):
    z, c = place_ref[0], place_ref[1]
    lay_keys(c, ((far_ref, far2_ref, 0),), keys_ref, values_ref)
    column = iota((BLOCK, STRIP), 1)
    for j in range(4):
        here = 2048 + j * 256 + c * BLOCK + iota((BLOCK, 1), 0)
        base = (z - 2) * 1024
        low = prompt_start(lengths_ref, here + base) - base
        query = own_ref[j, 0].T
        old_top = top_ref[j][:, :1]
        strips, top = [], None
        for first in range(j * 256, 1024, STRIP):
            scores = dot(query, keys_ref[:, first : first + STRIP], (1, 0))
            scores = jnp.where(column >= low - first, scores, -jnp.inf)
            top = scores if top is None else jnp.maximum(top, scores)
            strips.append((first, scores))
        top = jnp.maximum(jnp.max(top, axis=1, keepdims=True), old_top)
        total, summed = weigh(strips, top, lambda first: values_ref[:, first : first + STRIP])
        factor = turned(jnp.exp2((old_top - top) * SCALE2))
        total = total_ref[j][:1] * factor[:1] + turned(total)[:1]
        context = ((summed_ref[j] * factor[:HEAD] + summed) / total).astype(BF)
        for t in range(4):
            sent_ref[t, j] = context


def output_kernel(
    place_ref, context_ref, w0_ref, m2_ref, m1_ref, m3_ref, o2_ref, o1_ref, o3_ref,
    prompt_ref, out_ref,
):
    c, t = place_ref[1], place_ref[2]
    half = m1_ref.shape[0]
    width = out_ref.shape[1]
    pairs = [(context_ref[t, part].T, w0_ref.at[part * half : (part + 1) * half]) for part in (0, 1)]
    for by, mine, other in ((1, m1_ref, o1_ref), (2, m2_ref, o2_ref), (3, m3_ref, o3_ref)):
        source = lax.rem(t + 4 - by, 4)
        pairs.append((context_ref[source, c].T, mine))
        pairs.append((context_ref[source, 1 - c].T, other))
    for first in range(0, width, 256):
        strip = slice(first, min(first + 256, width))
        total = prompt_ref[:, strip].astype(F32)
        for context, weight in pairs:
            total = total + dot(context, weight[:, strip], (1, 0))
        out_ref[:, strip] = total.astype(BF)


def local(
    patches,
    picture_grid,
    vision_qkv,
    vision_out,
    merge_weight,
    picture_block,
    picture_offset,
    tokens,
    prompt_lengths,
    text_qkv,
    text_out,
):
    count, width = patches.shape[1:]
    local_width = vision_qkv.shape[2]
    wide = width + FACTS
    z = lax.axis_index("z")
    c = lax.axis_index("c")
    t = lax.axis_index("t")
    picture = patches[0]
    block = picture_block[0]

    place = jnp.stack([z, c, t]).astype(I32)
    share = call(
        vision_kernel,
        [shape((MERGED, width))] * 4,
        [SMEM, SMEM, HBM, HBM, HBM],
        [
            VMEM((count, width), BF),
            VMEM((3, local_width, width), BF),
            VMEM((local_width, width), BF),
            pltpu.SemaphoreType.DMA((5,)),
        ],
        limit=60,
    )(place, picture_grid, picture, vision_qkv.transpose(1, 2, 0), vision_out)
    shares = [around(share[by], "t", by) for by in range(1, 4)]
    own = call(own_kernel, shape((MERGED, width), F32), [SMEM, VMEM, VMEM], flops=8 * 10**9)(
        place, picture, share[0]
    )
    own, merge_weight = lax.optimization_barrier((own, merge_weight))
    merge_parts = (merge_weight[0, : width // 2], merge_weight[0, width // 2 :])
    facts = jnp.stack([block, picture_offset[0], picture_grid[0, 0], picture_grid[0, 1], 1])
    facts = jnp.where(t == 0, facts, 0)
    facts = jnp.concatenate([facts, (block % 8 // 2)[None]]).astype(I32)
    routed = call(merge_kernel, shape((4, MERGED, wide)), [SMEM] + [VMEM] * 6)(
        facts, own, *shares, *merge_parts
    )

    got = lax.all_to_all(routed.reshape(16, 16, wide), ("y", "t"), 0, 0, tiled=True)
    got = call(sum_kernel, shape((4, 16, wide)), [VMEM])(got.reshape(4, 4, 16, wide))
    other = around(got, "c", 1)
    routed = call(select_kernel, shape((8, 16, wide)), [SMEM, VMEM, VMEM])(place, got, other)
    half = local_width // 2
    near_half, columns = pl.pallas_call(
        cut_kernel,
        out_shape=[shape((half, width)), shape((local_width, BLOCK))],
        in_specs=[pl.BlockSpec(memory_space=SMEM)] + [pl.BlockSpec(memory_space=HBM)] * 3,
        out_specs=[pl.BlockSpec(memory_space=HBM)] * 2,
        scratch_shapes=[pltpu.SemaphoreType.DMA((2,))],
    )(place, routed, text_out, tokens.T)
    near_halves = [around(near_half, "t", by) for by in (1, 3)]
    pieces = [columns] + [around(columns, "t", by) for by in range(1, 4)]
    got = lax.all_to_all(routed, "z", 0, 0, tiled=True)
    got = jnp.sum(got.astype(F32), axis=0).astype(BF)
    rows = [got] + [around(got, "t", by) for by in range(1, 4)]
    own_tokens = jnp.zeros((4, local_width, BLOCK), BF)
    for by, piece in enumerate(pieces):
        own_tokens = lax.dynamic_update_index_in_dim(own_tokens, piece, (t - by) % 4, 0)
    own_tokens = own_tokens.reshape(width, BLOCK).T
    heads = call(
        project_kernel,
        shape((4, 3, HEAD, BLOCK)),
        [SMEM] + [VMEM] * 6,
    )(place, *rows, own_tokens, text_qkv.transpose(1, 2, 0))
    heads, late_tokens, near_half = lax.optimization_barrier((heads, own_tokens, near_half))
    halves = [around(near_half, "t", 2)] + near_halves
    mine = lax.all_to_all(heads, "y", 0, 0, tiled=True)
    prompt_in = call(place_kernel, shape((BLOCK, width)), [SMEM] + [VMEM] * 5)(
        place, *rows, late_tokens
    )
    pair = mine[:, 1:]
    near, far = ahead(pair, "z", 1), ahead(pair, "z", 2)
    own2, near2, far2 = (around(x, "c", 1) for x in (pair, near, far))
    halves = halves + [around(x, "c", 1) for x in halves]
    parts = call(
        near_kernel,
        [shape((4, BLOCK, BLOCK), F32), shape((4, 8, BLOCK), F32), shape((4, HEAD, BLOCK), F32)],
        [SMEM, SMEM] + [VMEM] * 4,
        [VMEM((HEAD, 2048), BF)] * 2,
        limit=16,
    )(place, prompt_lengths, mine, near, own2, near2)
    sent = call(
        far_kernel,
        shape((4, 4, HEAD, BLOCK)),
        [SMEM, SMEM] + [VMEM] * 6,
        [VMEM((HEAD, 1024), BF)] * 2,
        limit=16,
    )(place, prompt_lengths, mine, far, far2, *parts)
    context = lax.all_to_all(sent.reshape(16, HEAD, BLOCK), ("t", "y"), 0, 0, tiled=True)
    return call(output_kernel, shape((BLOCK, width)), [SMEM] + [VMEM] * 9)(
        place, context.reshape(4, 2, half, BLOCK), text_out, *halves, prompt_in
    )


def solution(mesh):
    split = Mesh(np.asarray(mesh.devices).reshape(8, 4, 2, 4), ("z", "y", "c", "t"))
    seq = ("z", "y", "c")
    placed = (
        P(seq, None, None),
        P(seq, None),
        P(None, None, "t"),
        P("t", None),
        P("t", None, None),
        P(seq),
        P(seq),
        P(seq, "t"),
        P(),
        P(None, None, "t"),
        P("t", None),
    )
    return jax.shard_map(
        local, mesh=split, in_specs=placed, out_specs=P(seq, None), check_vma=False
    )
```

```python
import jax
import jax.numpy as jnp
import numpy as np
from jax import lax
from jax.experimental import pallas as pl
from jax.experimental.pallas import tpu as pltpu
from jax.sharding import Mesh
from jax.sharding import PartitionSpec as P

HEAD = 88
MAXGRID = 16
BLOCK = 128
MERGED = 64
EPSILON = 1e-06
SCALE2 = HEAD ** (-0.5) / float(np.log(2.0))
BF = jnp.bfloat16
F32 = jnp.float32
I32 = jnp.int32
VMEM = pltpu.VMEM
SMEM = pltpu.SMEM
HBM = pltpu.HBM
FACTS = 128
STRIP = 256


def ahead(x, axis, by):
    count = lax.axis_size(axis)
    return lax.ppermute(x, axis, [(i, i + by) for i in range(count - by)])


def around(x, axis, by):
    count = lax.axis_size(axis)
    return lax.ppermute(x, axis, [(i, (i + by) % count) for i in range(count)])


def call(kernel, out_shape, spaces, scratch=(), limit=8, flops=None):
    single = not isinstance(out_shape, (list, tuple))
    outs = pl.BlockSpec(memory_space=VMEM)
    cost = flops and pl.CostEstimate(flops=flops, transcendentals=0, bytes_accessed=flops // 400)
    return pl.pallas_call(
        kernel,
        out_shape=out_shape,
        in_specs=[pl.BlockSpec(memory_space=s) for s in spaces],
        out_specs=outs if single else [outs] * len(out_shape),
        scratch_shapes=scratch,
        compiler_params=pltpu.CompilerParams(vmem_limit_bytes=limit << 20),
        cost_estimate=cost,
    )


def shape(dims, dtype=BF):
    return jax.ShapeDtypeStruct(dims, dtype)


def iota(dims, axis):
    return lax.broadcasted_iota(I32, dims, axis)


def dot(a, b, over):
    return lax.dot_general(
        a, b, (((over[0],), (over[1],)), ((), ())), preferred_element_type=F32
    )


def normalize(values):
    centre = jnp.mean(values, axis=-1, keepdims=True)
    shifted = values - centre
    spread = jnp.mean(shifted * shifted, axis=-1, keepdims=True)
    return (shifted * lax.rsqrt(spread + EPSILON)).astype(BF)


def slot_of(row):
    i, j = row // 128, (row // 64) % 2
    a, b = (row // 8) % 8, row % 8
    return (2 * a + i) * MAXGRID + 2 * b + j


def vision_kernel(
    grid_ref, picture_hbm, qkv_hbm, out_hbm, s0_ref, s1_ref, s2_ref, s3_ref,
    picture_ref, qkv_ref, out_ref, arrived,
):
    copies = [pltpu.make_async_copy(picture_hbm, picture_ref, arrived.at[0])]
    for part in range(3):
        copies.append(
            pltpu.make_async_copy(qkv_hbm.at[part], qkv_ref.at[part], arrived.at[1 + part])
        )
    copies.append(pltpu.make_async_copy(out_hbm, out_ref, arrived.at[4]))
    for copy in copies:
        copy.start()
    count = picture_ref.shape[0]
    local_width = qkv_ref.shape[1]
    copies[0].wait()
    normed = normalize(picture_ref[...].astype(F32))
    parts = []
    for part in range(3):
        copies[1 + part].wait()
        parts.append(dot(qkv_ref[part], normed, (1, 1)))
    slots = iota((count, 1), 0)
    usable = (slots // MAXGRID < 2 * grid_ref[0, 0]) & (slots % MAXGRID < 2 * grid_ref[0, 1])
    contexts = []
    for first in range(0, local_width, HEAD):
        q, k, v = (x[first : first + HEAD].astype(BF) for x in parts)
        scores = jnp.where(usable, dot(k, q, (0, 0)), -jnp.inf)
        expons = jnp.exp2((scores - jnp.max(scores, axis=0, keepdims=True)) * SCALE2)
        total = jnp.sum(expons, axis=0, keepdims=True)
        contexts.append(dot(v, expons.astype(BF), (1, 0)) / total)
    context = jnp.concatenate(contexts, axis=0).astype(BF)
    row = (iota((count, count), 0) + lax.axis_index("t") * MERGED) % count
    order = slot_of(row) == iota((count, count), 1)
    context = dot(order.astype(BF), context, (1, 1)).astype(BF)
    copies[4].wait()
    share = dot(context, out_ref[...], (1, 0)).astype(BF)
    for by, share_ref in enumerate((s0_ref, s1_ref, s2_ref, s3_ref)):
        share_ref[...] = share[by * MERGED : (by + 1) * MERGED]


def sum_kernel(parts_ref, rows_ref):
    for y in range(4):
        total = parts_ref[y, 0].astype(F32)
        for t in range(1, 4):
            total = total + parts_ref[y, t].astype(F32)
        rows_ref[y] = total.astype(BF)


def select_kernel(place_ref, mine_ref, other_ref, routed_ref):
    wide = mine_ref.shape[2]
    width = wide - FACTS
    rows = jnp.concatenate(
        [mine_ref[...].reshape(64, wide), other_ref[...].reshape(64, wide)], axis=0
    )
    facts = rows[:, width:].astype(F32)
    block, there = facts[:, 0:1], facts[:, 4:5]
    same_core = block - 2.0 * jnp.floor(block * 0.5) == place_ref[1].astype(F32)
    to = jnp.where(same_core & (there > 0.0), jnp.floor(block * 0.125), -1.0).astype(I32)
    source, target = iota((128, 128), 0), iota((128, 128), 1)
    chosen = (to == target // 16) & (source % 16 == target % 16)
    routed = dot(chosen.astype(BF), rows, (0, 0))
    routed_ref[...] = routed.astype(BF).reshape(8, 16, wide)


def own_kernel(place_ref, picture_ref, share_ref, own_ref):
    count = picture_ref.shape[0]
    row = iota((MERGED, count), 0) + place_ref[2] * MERGED
    chosen = (slot_of(row) == iota((MERGED, count), 1)).astype(BF)
    own_ref[...] = dot(chosen, picture_ref[...], (1, 0)) + share_ref[...].astype(F32)


def merge_kernel(facts_ref, own_ref, s1_ref, s2_ref, s3_ref, w0_ref, w1_ref, w2_ref, rows_ref):
    width = own_ref.shape[1]
    total = own_ref[...]
    for share in (s1_ref, s2_ref, s3_ref):
        total = total + share[...].astype(F32)
    normed = normalize(total)
    first, merged = 0, jnp.zeros((MERGED, width), F32)
    for weight in (w0_ref, w1_ref, w2_ref):
        deep = weight.shape[0]
        merged = merged + dot(normed[:, first : first + deep], weight[...], (1, 0))
        first = first + deep
    merged = merged.astype(BF)
    lane = iota((MERGED, FACTS), 1)
    facts = jnp.zeros((MERGED, FACTS), I32)
    for index in range(5):
        facts = jnp.where(lane == index, facts_ref[index], facts)
    facts = facts.astype(F32).astype(BF)
    for y in range(4):
        here = facts_ref[5] == y
        rows_ref[y, :, :width] = jnp.where(here, merged, jnp.zeros_like(merged))
        rows_ref[y, :, width:] = jnp.where(here, facts, jnp.zeros_like(facts))


def placed_rows(place_ref, pieces_refs, tokens_ref):
    width = tokens_ref.shape[1]
    pieces, firsts = [], []
    for by, piece in enumerate(pieces_refs):
        pieces.append(piece[...])
        firsts.append(jnp.full((16, 1), 16 * lax.rem(place_ref[2] + 4 - by, 4), I32))
    rows = jnp.concatenate(pieces, axis=0)
    cell = jnp.concatenate(firsts, axis=0) + iota((MERGED, 1), 0) % 16
    facts = rows[:, width:].astype(F32)
    a, b = (cell // 8).astype(F32), (cell % 8).astype(F32)
    offset, high, wide, there = (facts[:, i : i + 1] for i in (1, 2, 3, 4))
    target = offset + a * wide + b
    usable = (a < high) & (b < wide) & (there > 0.0)
    target = jnp.where(usable, target, -1.0)
    table = (target == iota((MERGED, BLOCK), 1).astype(F32)).astype(BF)
    placed = dot(table, rows, (0, 0))
    covered = placed[:, width + 4 : width + 5] > 0.0
    return jnp.where(covered, placed[:, :width], tokens_ref[...].astype(F32))


def place_kernel(place_ref, r0_ref, r1_ref, r2_ref, r3_ref, tokens_ref, prompt_ref):
    pieces = (r0_ref, r1_ref, r2_ref, r3_ref)
    prompt_ref[...] = placed_rows(place_ref, pieces, tokens_ref).astype(BF)


def project_kernel(
    place_ref, r0_ref, r1_ref, r2_ref, r3_ref, tokens_ref, qkv_ref, heads_ref
):
    pieces = (r0_ref, r1_ref, r2_ref, r3_ref)
    normed = normalize(placed_rows(place_ref, pieces, tokens_ref))
    for part in range(3):
        projected = dot(qkv_ref[part], normed, (1, 1))
        for head in range(4):
            heads_ref[head, part] = projected[head * HEAD : (head + 1) * HEAD].astype(BF)


def attend_kernel(facts_ref, lengths_ref, own_ref, near_ref, far_ref,
                  own2_ref, near2_ref, far2_ref, sent_ref):
    z, c = facts_ref[0], facts_ref[1]
    blocks = []
    for mine, other, skip in (
        (far_ref, far2_ref, 0), (near_ref, near2_ref, 0), (own_ref, own2_ref, 1)
    ):
        blocks += [(mine, other, skip, y) for y in range(4)]

    def strip_of(strip, part):
        mine, other, skip, y = blocks[strip]
        return jnp.concatenate([mine[y, skip + part], other[y, part]], axis=1)

    row = iota((BLOCK, 1), 0)
    lane = iota((BLOCK, STRIP), 1)
    column = lane + jnp.where(lane < BLOCK, c * BLOCK, -c * BLOCK)
    base = (z - 2) * 1024
    for j in range(4):
        here = 2048 + j * 256 + c * BLOCK + row
        start = jnp.zeros((BLOCK, 1), I32)
        end = jnp.int32(0)
        for prompt in range(16):
            end = end + lengths_ref[prompt]
            start = jnp.where(end <= here + base, end, start)
        low = start - base
        query = own_ref[j, 0].T
        strips, top = [], None
        for strip in range(j, j + 9):
            scores = dot(query, strip_of(strip, 0), (1, 0))
            visible = column >= low - strip * STRIP
            if strip >= 8:
                visible = visible & (column <= here - strip * STRIP)
            scores = jnp.where(visible, scores, -jnp.inf)
            top = scores if top is None else jnp.maximum(top, scores)
            strips.append((strip, scores))
        top = jnp.max(top, axis=1, keepdims=True)
        total = jnp.zeros((BLOCK, STRIP), F32)
        summed = jnp.zeros((HEAD, BLOCK), F32)
        for strip, scores in strips:
            expons = jnp.exp2((scores - top) * SCALE2)
            total = total + expons
            summed = summed + dot(strip_of(strip, 1), expons.astype(BF), (1, 1))
        total = jnp.sum(total, axis=1, keepdims=True)
        total = jnp.transpose(jnp.broadcast_to(total, (BLOCK, BLOCK)))
        context = (summed / total[:HEAD]).astype(BF)
        for t in range(4):
            sent_ref[t, j] = context


def output_kernel(
    place_ref, context_ref, w0_ref, m2_ref, m1_ref, m3_ref, o2_ref, o1_ref, o3_ref,
    prompt_ref, out_ref,
):
    c, t = place_ref[1], place_ref[2]
    half = m1_ref.shape[0]
    width = out_ref.shape[1]
    pairs = [(context_ref[t, part].T, w0_ref.at[part * half : (part + 1) * half]) for part in (0, 1)]
    for by, mine, other in ((1, m1_ref, o1_ref), (2, m2_ref, o2_ref), (3, m3_ref, o3_ref)):
        source = lax.rem(t + 4 - by, 4)
        pairs.append((context_ref[source, c].T, mine))
        pairs.append((context_ref[source, 1 - c].T, other))
    for first in range(0, width, 256):
        strip = slice(first, min(first + 256, width))
        total = prompt_ref[:, strip].astype(F32)
        for context, weight in pairs:
            total = total + dot(context, weight[:, strip], (1, 0))
        out_ref[:, strip] = total.astype(BF)


def local(
    patches,
    picture_grid,
    vision_qkv,
    vision_out,
    merge_weight,
    picture_block,
    picture_offset,
    tokens,
    prompt_lengths,
    text_qkv,
    text_out,
):
    count, width = patches.shape[1:]
    local_width = vision_qkv.shape[2]
    wide = width + FACTS
    z = lax.axis_index("z")
    c = lax.axis_index("c")
    t = lax.axis_index("t")
    picture = patches[0]
    block = picture_block[0]

    place = jnp.stack([z, c, t]).astype(I32)
    share = call(
        vision_kernel,
        [shape((MERGED, width))] * 4,
        [SMEM, HBM, HBM, HBM],
        [
            VMEM((count, width), BF),
            VMEM((3, local_width, width), BF),
            VMEM((local_width, width), BF),
            pltpu.SemaphoreType.DMA((5,)),
        ],
        limit=60,
    )(picture_grid, picture, vision_qkv.transpose(1, 2, 0), vision_out)
    shares = [around(share[by], "t", by) for by in range(1, 4)]
    own = call(own_kernel, shape((MERGED, width), F32), [SMEM, VMEM, VMEM], flops=8 * 10**9)(
        place, picture, share[0]
    )
    own, merge_weight = lax.optimization_barrier((own, merge_weight))
    merge_parts = jnp.split(merge_weight[0], [640, 1024], axis=0)
    facts = jnp.stack([block, picture_offset[0], picture_grid[0, 0], picture_grid[0, 1], 1])
    facts = jnp.where(t == 0, facts, 0)
    facts = jnp.concatenate([facts, (block % 8 // 2)[None]]).astype(I32)
    routed = call(merge_kernel, shape((4, MERGED, wide)), [SMEM] + [VMEM] * 7)(
        facts, own, *shares, *merge_parts
    )

    got = lax.all_to_all(routed.reshape(16, 16, wide), ("y", "t"), 0, 0, tiled=True)
    got = call(sum_kernel, shape((4, 16, wide)), [VMEM])(got.reshape(4, 4, 16, wide))
    other = around(got, "c", 1)
    routed = call(select_kernel, shape((8, 16, wide)), [SMEM, VMEM, VMEM])(place, got, other)
    routed, text_out = lax.optimization_barrier((routed, text_out))
    half = local_width // 2
    near_half = lax.dynamic_slice_in_dim(text_out, c * half, half, 0)
    near_half, tokens = lax.optimization_barrier((near_half, tokens))
    halves = [None] + [around(near_half, "t", by) for by in (1, 3)]
    pieces = [tokens] + [around(tokens, "t", by) for by in range(1, 4)]
    got = lax.all_to_all(routed, "z", 0, 0, tiled=True)
    got = jnp.sum(got.astype(F32), axis=0).astype(BF)
    rows = [got] + [around(got, "t", by) for by in range(1, 4)]
    own_tokens = jnp.zeros((4, BLOCK, local_width), BF)
    for by, piece in enumerate(pieces):
        own_tokens = lax.dynamic_update_index_in_dim(own_tokens, piece, (t - by) % 4, 0)
    own_tokens = own_tokens.transpose(1, 0, 2).reshape(BLOCK, width)
    heads = call(
        project_kernel,
        shape((4, 3, HEAD, BLOCK)),
        [SMEM] + [VMEM] * 6,
    )(place, *rows, own_tokens, text_qkv.transpose(1, 2, 0))
    heads, late_tokens, near_half = lax.optimization_barrier((heads, own_tokens, near_half))
    halves[0] = around(near_half, "t", 2)
    mine = lax.all_to_all(heads, "y", 0, 0, tiled=True)
    prompt_in = call(place_kernel, shape((BLOCK, width)), [SMEM] + [VMEM] * 5)(
        place, *rows, late_tokens
    )
    pair = mine[:, 1:]
    near, far = ahead(pair, "z", 1), ahead(pair, "z", 2)
    others = [around(x, "c", 1) for x in (pair, near, far)]
    halves = halves + [around(x, "c", 1) for x in halves]
    sent = call(
        attend_kernel,
        shape((4, 4, HEAD, BLOCK)),
        [SMEM, SMEM] + [VMEM] * 6,
        limit=16,
    )(place, prompt_lengths, mine, near, far, *others)
    context = lax.all_to_all(sent.reshape(16, HEAD, BLOCK), ("t", "y"), 0, 0, tiled=True)
    return call(output_kernel, shape((BLOCK, width)), [SMEM] + [VMEM] * 9)(
        place, context.reshape(4, 2, half, BLOCK), text_out, *halves, prompt_in
    )


def solution(mesh):
    split = Mesh(np.asarray(mesh.devices).reshape(8, 4, 2, 4), ("z", "y", "c", "t"))
    seq = ("z", "y", "c")
    placed = (
        P(seq, None, None),
        P(seq, None),
        P(None, None, "t"),
        P("t", None),
        P("t", None, None),
        P(seq),
        P(seq),
        P(seq, "t"),
        P(),
        P(None, None, "t"),
        P("t", None),
    )
    return jax.shard_map(
        local, mesh=split, in_specs=placed, out_specs=P(seq, None), check_vma=False
    )
```

```python
import jax
import jax.numpy as jnp
import numpy as np
from jax import lax
from jax.experimental import pallas as pl
from jax.experimental.pallas import tpu as pltpu
from jax.sharding import Mesh
from jax.sharding import PartitionSpec as P

HEAD = 88
MAXGRID = 16
BLOCK = 128
MERGED = 64
EPSILON = 1e-06
SCALE2 = HEAD ** (-0.5) / float(np.log(2.0))
BF = jnp.bfloat16
F32 = jnp.float32
I32 = jnp.int32
VMEM = pltpu.VMEM
SMEM = pltpu.SMEM
HBM = pltpu.HBM
FACTS = 128
STRIP = 256


def ahead(x, axis, by):
    count = lax.axis_size(axis)
    return lax.ppermute(x, axis, [(i, i + by) for i in range(count - by)])


def around(x, axis, by):
    count = lax.axis_size(axis)
    return lax.ppermute(x, axis, [(i, (i + by) % count) for i in range(count)])


def call(kernel, out_shape, spaces, scratch=(), limit=8, flops=None):
    single = not isinstance(out_shape, (list, tuple))
    outs = pl.BlockSpec(memory_space=VMEM)
    cost = flops and pl.CostEstimate(flops=flops, transcendentals=0, bytes_accessed=flops // 400)
    return pl.pallas_call(
        kernel,
        out_shape=out_shape,
        in_specs=[pl.BlockSpec(memory_space=s) for s in spaces],
        out_specs=outs if single else [outs] * len(out_shape),
        scratch_shapes=scratch,
        compiler_params=pltpu.CompilerParams(vmem_limit_bytes=limit << 20),
        cost_estimate=cost,
    )


def shape(dims, dtype=BF):
    return jax.ShapeDtypeStruct(dims, dtype)


def iota(dims, axis):
    return lax.broadcasted_iota(I32, dims, axis)


def dot(a, b, over):
    return lax.dot_general(
        a, b, (((over[0],), (over[1],)), ((), ())), preferred_element_type=F32
    )


def normalize(values):
    centre = jnp.mean(values, axis=-1, keepdims=True)
    shifted = values - centre
    spread = jnp.mean(shifted * shifted, axis=-1, keepdims=True)
    return (shifted * lax.rsqrt(spread + EPSILON)).astype(BF)


def slot_of(row):
    i, j = row // 128, (row // 64) % 2
    a, b = (row // 8) % 8, row % 8
    return (2 * a + i) * MAXGRID + 2 * b + j


def vision_kernel(
    grid_ref, picture_hbm, qkv_hbm, out_hbm, s0_ref, s1_ref, s2_ref, s3_ref,
    picture_ref, qkv_ref, out_ref, arrived,
):
    copies = [pltpu.make_async_copy(picture_hbm, picture_ref, arrived.at[0])]
    for part in range(3):
        copies.append(
            pltpu.make_async_copy(qkv_hbm.at[part], qkv_ref.at[part], arrived.at[1 + part])
        )
    copies.append(pltpu.make_async_copy(out_hbm, out_ref, arrived.at[4]))
    for copy in copies:
        copy.start()
    count = picture_ref.shape[0]
    local_width = qkv_ref.shape[1]
    copies[0].wait()
    normed = normalize(picture_ref[...].astype(F32))
    parts = []
    for part in range(3):
        copies[1 + part].wait()
        parts.append(dot(qkv_ref[part], normed, (1, 1)))
    slots = iota((count, 1), 0)
    usable = (slots // MAXGRID < 2 * grid_ref[0, 0]) & (slots % MAXGRID < 2 * grid_ref[0, 1])
    contexts = []
    for first in range(0, local_width, HEAD):
        q, k, v = (x[first : first + HEAD].astype(BF) for x in parts)
        scores = jnp.where(usable, dot(k, q, (0, 0)), -jnp.inf)
        expons = jnp.exp2((scores - jnp.max(scores, axis=0, keepdims=True)) * SCALE2)
        total = jnp.sum(expons, axis=0, keepdims=True)
        contexts.append(dot(v, expons.astype(BF), (1, 0)) / total)
    context = jnp.concatenate(contexts, axis=0).astype(BF)
    row = (iota((count, count), 0) + lax.axis_index("t") * MERGED) % count
    order = slot_of(row) == iota((count, count), 1)
    context = dot(order.astype(BF), context, (1, 1)).astype(BF)
    copies[4].wait()
    share = dot(context, out_ref[...], (1, 0)).astype(BF)
    for by, share_ref in enumerate((s0_ref, s1_ref, s2_ref, s3_ref)):
        share_ref[...] = share[by * MERGED : (by + 1) * MERGED]


def sum_kernel(parts_ref, rows_ref):
    for y in range(4):
        total = parts_ref[y, 0].astype(F32)
        for t in range(1, 4):
            total = total + parts_ref[y, t].astype(F32)
        rows_ref[y] = total.astype(BF)


def select_kernel(place_ref, mine_ref, other_ref, *routed_refs):
    wide = mine_ref.shape[2]
    width = wide - FACTS
    rows = jnp.concatenate(
        [mine_ref[...].reshape(64, wide), other_ref[...].reshape(64, wide)], axis=0
    )
    facts = rows[:, width:].astype(F32)
    block, there = facts[:, 0:1], facts[:, 4:5]
    same_core = block - 2.0 * jnp.floor(block * 0.5) == place_ref[1].astype(F32)
    to = jnp.where(same_core & (there > 0.0), jnp.floor(block * 0.125), -1.0).astype(I32)
    source, target = iota((128, 128), 0), iota((128, 128), 1)
    plane = (place_ref[0] + target // 16) % 8
    chosen = (to == plane) & (source % 16 == target % 16)
    routed = dot(chosen.astype(BF), rows, (0, 0)).astype(BF)
    for by, routed_ref in enumerate(routed_refs):
        routed_ref[...] = routed[by * 16 : (by + 1) * 16]


def join_kernel(*refs):
    total = refs[0][...].astype(F32)
    for ref in refs[1:-1]:
        total = total + ref[...].astype(F32)
    refs[-1][...] = total.astype(BF)


def own_kernel(place_ref, picture_ref, share_ref, own_ref):
    count = picture_ref.shape[0]
    row = iota((MERGED, count), 0) + place_ref[2] * MERGED
    chosen = (slot_of(row) == iota((MERGED, count), 1)).astype(BF)
    own_ref[...] = dot(chosen, picture_ref[...], (1, 0)) + share_ref[...].astype(F32)


def merge_kernel(facts_ref, own_ref, s1_ref, s2_ref, s3_ref, w0_ref, w1_ref, w2_ref, rows_ref):
    width = own_ref.shape[1]
    total = own_ref[...]
    for share in (s1_ref, s2_ref, s3_ref):
        total = total + share[...].astype(F32)
    normed = normalize(total)
    first, merged = 0, jnp.zeros((MERGED, width), F32)
    for weight in (w0_ref, w1_ref, w2_ref):
        deep = weight.shape[0]
        merged = merged + dot(normed[:, first : first + deep], weight[...], (1, 0))
        first = first + deep
    merged = merged.astype(BF)
    lane = iota((MERGED, FACTS), 1)
    facts = jnp.zeros((MERGED, FACTS), I32)
    for index in range(5):
        facts = jnp.where(lane == index, facts_ref[index], facts)
    facts = facts.astype(F32).astype(BF)
    for y in range(4):
        here = facts_ref[5] == y
        rows_ref[y, :, :width] = jnp.where(here, merged, jnp.zeros_like(merged))
        rows_ref[y, :, width:] = jnp.where(here, facts, jnp.zeros_like(facts))


def placed_rows(place_ref, pieces_refs, tokens_ref):
    width = tokens_ref.shape[1]
    pieces, firsts = [], []
    for by, piece in enumerate(pieces_refs):
        pieces.append(piece[...])
        firsts.append(jnp.full((16, 1), 16 * lax.rem(place_ref[2] + 4 - by, 4), I32))
    rows = jnp.concatenate(pieces, axis=0)
    cell = jnp.concatenate(firsts, axis=0) + iota((MERGED, 1), 0) % 16
    facts = rows[:, width:].astype(F32)
    a, b = (cell // 8).astype(F32), (cell % 8).astype(F32)
    offset, high, wide, there = (facts[:, i : i + 1] for i in (1, 2, 3, 4))
    target = offset + a * wide + b
    usable = (a < high) & (b < wide) & (there > 0.0)
    target = jnp.where(usable, target, -1.0)
    table = (target == iota((MERGED, BLOCK), 1).astype(F32)).astype(BF)
    placed = dot(table, rows, (0, 0))
    covered = placed[:, width + 4 : width + 5] > 0.0
    return jnp.where(covered, placed[:, :width], tokens_ref[...].astype(F32))


def place_kernel(place_ref, r0_ref, r1_ref, r2_ref, r3_ref, tokens_ref, prompt_ref):
    pieces = (r0_ref, r1_ref, r2_ref, r3_ref)
    prompt_ref[...] = placed_rows(place_ref, pieces, tokens_ref).astype(BF)


def project_kernel(
    place_ref, r0_ref, r1_ref, r2_ref, r3_ref, tokens_ref, qkv_ref, heads_ref
):
    pieces = (r0_ref, r1_ref, r2_ref, r3_ref)
    normed = normalize(placed_rows(place_ref, pieces, tokens_ref))
    for part in range(3):
        projected = dot(qkv_ref[part], normed, (1, 1))
        for head in range(4):
            heads_ref[head, part] = projected[head * HEAD : (head + 1) * HEAD].astype(BF)


def attend_kernel(facts_ref, lengths_ref, own_ref, near_ref, far_ref,
                  own2_ref, near2_ref, far2_ref, sent_ref):
    z, c = facts_ref[0], facts_ref[1]
    blocks = []
    for mine, other, skip in (
        (far_ref, far2_ref, 0), (near_ref, near2_ref, 0), (own_ref, own2_ref, 1)
    ):
        blocks += [(mine, other, skip, y) for y in range(4)]

    def strip_of(strip, part):
        mine, other, skip, y = blocks[strip]
        return jnp.concatenate([mine[y, skip + part], other[y, part]], axis=1)

    row = iota((BLOCK, 1), 0)
    lane = iota((BLOCK, STRIP), 1)
    column = lane + jnp.where(lane < BLOCK, c * BLOCK, -c * BLOCK)
    base = (z - 2) * 1024
    for j in range(4):
        here = 2048 + j * 256 + c * BLOCK + row
        start = jnp.zeros((BLOCK, 1), I32)
        end = jnp.int32(0)
        for prompt in range(16):
            end = end + lengths_ref[prompt]
            start = jnp.where(end <= here + base, end, start)
        low = start - base
        query = own_ref[j, 0].T
        strips, top = [], None
        for strip in range(j, j + 9):
            scores = dot(query, strip_of(strip, 0), (1, 0))
            visible = column >= low - strip * STRIP
            if strip >= 8:
                visible = visible & (column <= here - strip * STRIP)
            scores = jnp.where(visible, scores, -jnp.inf)
            top = scores if top is None else jnp.maximum(top, scores)
            strips.append((strip, scores))
        top = jnp.max(top, axis=1, keepdims=True)
        total = jnp.zeros((BLOCK, STRIP), F32)
        summed = jnp.zeros((HEAD, BLOCK), F32)
        for strip, scores in strips:
            expons = jnp.exp2((scores - top) * SCALE2)
            total = total + expons
            summed = summed + dot(strip_of(strip, 1), expons.astype(BF), (1, 1))
        total = jnp.sum(total, axis=1, keepdims=True)
        total = jnp.transpose(jnp.broadcast_to(total, (BLOCK, BLOCK)))
        context = (summed / total[:HEAD]).astype(BF)
        for t in range(4):
            sent_ref[t, j] = context


def output_kernel(
    place_ref, context_ref, w0_ref, m2_ref, m1_ref, m3_ref, o2_ref, o1_ref, o3_ref,
    prompt_ref, out_ref,
):
    c, t = place_ref[1], place_ref[2]
    half = m1_ref.shape[0]
    width = out_ref.shape[1]
    pairs = [(context_ref[t, part].T, w0_ref.at[part * half : (part + 1) * half]) for part in (0, 1)]
    for by, mine, other in ((1, m1_ref, o1_ref), (2, m2_ref, o2_ref), (3, m3_ref, o3_ref)):
        source = lax.rem(t + 4 - by, 4)
        pairs.append((context_ref[source, c].T, mine))
        pairs.append((context_ref[source, 1 - c].T, other))
    for first in range(0, width, 256):
        strip = slice(first, min(first + 256, width))
        total = prompt_ref[:, strip].astype(F32)
        for context, weight in pairs:
            total = total + dot(context, weight[:, strip], (1, 0))
        out_ref[:, strip] = total.astype(BF)


def local(
    patches,
    picture_grid,
    vision_qkv,
    vision_out,
    merge_weight,
    picture_block,
    picture_offset,
    tokens,
    prompt_lengths,
    text_qkv,
    text_out,
):
    count, width = patches.shape[1:]
    local_width = vision_qkv.shape[2]
    wide = width + FACTS
    z = lax.axis_index("z")
    c = lax.axis_index("c")
    t = lax.axis_index("t")
    picture = patches[0]
    block = picture_block[0]

    place = jnp.stack([z, c, t]).astype(I32)
    share = call(
        vision_kernel,
        [shape((MERGED, width))] * 4,
        [SMEM, HBM, HBM, HBM],
        [
            VMEM((count, width), BF),
            VMEM((3, local_width, width), BF),
            VMEM((local_width, width), BF),
            pltpu.SemaphoreType.DMA((5,)),
        ],
        limit=60,
    )(picture_grid, picture, vision_qkv.transpose(1, 2, 0), vision_out)
    shares = [around(share[by], "t", by) for by in range(1, 4)]
    own = call(own_kernel, shape((MERGED, width), F32), [SMEM, VMEM, VMEM], flops=8 * 10**9)(
        place, picture, share[0]
    )
    own, merge_weight = lax.optimization_barrier((own, merge_weight))
    merge_parts = jnp.split(merge_weight[0], [640, 1024], axis=0)
    facts = jnp.stack([block, picture_offset[0], picture_grid[0, 0], picture_grid[0, 1], 1])
    facts = jnp.where(t == 0, facts, 0)
    facts = jnp.concatenate([facts, (block % 8 // 2)[None]]).astype(I32)
    routed = call(merge_kernel, shape((4, MERGED, wide)), [SMEM] + [VMEM] * 7)(
        facts, own, *shares, *merge_parts
    )

    got = lax.all_to_all(routed.reshape(16, 16, wide), ("y", "t"), 0, 0, tiled=True)
    got = call(sum_kernel, shape((4, 16, wide)), [VMEM])(got.reshape(4, 4, 16, wide))
    other = around(got, "c", 1)
    routed = call(select_kernel, [shape((16, wide))] * 8, [SMEM, VMEM, VMEM])(place, got, other)
    *routed, text_out = lax.optimization_barrier((*routed, text_out))
    half = local_width // 2
    near_half = lax.dynamic_slice_in_dim(text_out, c * half, half, 0)
    near_half, tokens = lax.optimization_barrier((near_half, tokens))
    halves = [None] + [around(near_half, "t", by) for by in (1, 3)]
    pieces = [tokens] + [around(tokens, "t", by) for by in range(1, 4)]
    routed = [routed[0]] + [around(routed[by], "z", by) for by in range(1, 8)]
    got = call(join_kernel, shape((16, wide)), [VMEM] * 8)(*routed)
    rows = [got] + [around(got, "t", by) for by in range(1, 4)]
    own_tokens = jnp.zeros((4, BLOCK, local_width), BF)
    for by, piece in enumerate(pieces):
        own_tokens = lax.dynamic_update_index_in_dim(own_tokens, piece, (t - by) % 4, 0)
    own_tokens = own_tokens.transpose(1, 0, 2).reshape(BLOCK, width)
    heads = call(
        project_kernel,
        shape((4, 3, HEAD, BLOCK)),
        [SMEM] + [VMEM] * 6,
    )(place, *rows, own_tokens, text_qkv.transpose(1, 2, 0))
    heads, late_tokens, near_half = lax.optimization_barrier((heads, own_tokens, near_half))
    halves[0] = around(near_half, "t", 2)
    mine = lax.all_to_all(heads, "y", 0, 0, tiled=True)
    prompt_in = call(place_kernel, shape((BLOCK, width)), [SMEM] + [VMEM] * 5)(
        place, *rows, late_tokens
    )
    pair = mine[:, 1:]
    near, far = ahead(pair, "z", 1), ahead(pair, "z", 2)
    others = [around(x, "c", 1) for x in (pair, near, far)]
    halves = halves + [around(x, "c", 1) for x in halves]
    sent = call(
        attend_kernel,
        shape((4, 4, HEAD, BLOCK)),
        [SMEM, SMEM] + [VMEM] * 6,
        limit=16,
    )(place, prompt_lengths, mine, near, far, *others)
    context = lax.all_to_all(sent.reshape(16, HEAD, BLOCK), ("t", "y"), 0, 0, tiled=True)
    return call(output_kernel, shape((BLOCK, width)), [SMEM] + [VMEM] * 9)(
        place, context.reshape(4, 2, half, BLOCK), text_out, *halves, prompt_in
    )


def solution(mesh):
    split = Mesh(np.asarray(mesh.devices).reshape(8, 4, 2, 4), ("z", "y", "c", "t"))
    seq = ("z", "y", "c")
    placed = (
        P(seq, None, None),
        P(seq, None),
        P(None, None, "t"),
        P("t", None),
        P("t", None, None),
        P(seq),
        P(seq),
        P(seq, "t"),
        P(),
        P(None, None, "t"),
        P("t", None),
    )
    return jax.shard_map(
        local, mesh=split, in_specs=placed, out_specs=P(seq, None), check_vma=False
    )
```

```python
import jax
import jax.numpy as jnp
import numpy as np
from jax import lax
from jax.experimental import pallas as pl
from jax.experimental.pallas import tpu as pltpu
from jax.sharding import Mesh
from jax.sharding import PartitionSpec as P

HEAD = 88
MAXGRID = 16
BLOCK = 128
MERGED = 64
EPSILON = 1e-06
SCALE2 = HEAD ** (-0.5) / float(np.log(2.0))
BF = jnp.bfloat16
F32 = jnp.float32
I32 = jnp.int32
VMEM = pltpu.VMEM
SMEM = pltpu.SMEM
HBM = pltpu.HBM
FACTS = 128
STRIP = 256


def ahead(x, axis, by):
    count = lax.axis_size(axis)
    return lax.ppermute(x, axis, [(i, i + by) for i in range(count - by)])


def around(x, axis, by):
    count = lax.axis_size(axis)
    return lax.ppermute(x, axis, [(i, (i + by) % count) for i in range(count)])


def call(kernel, out_shape, spaces, scratch=(), limit=8, flops=None):
    single = not isinstance(out_shape, (list, tuple))
    outs = pl.BlockSpec(memory_space=VMEM)
    cost = flops and pl.CostEstimate(flops=flops, transcendentals=0, bytes_accessed=flops // 400)
    return pl.pallas_call(
        kernel,
        out_shape=out_shape,
        in_specs=[pl.BlockSpec(memory_space=s) for s in spaces],
        out_specs=outs if single else [outs] * len(out_shape),
        scratch_shapes=scratch,
        compiler_params=pltpu.CompilerParams(vmem_limit_bytes=limit << 20),
        cost_estimate=cost,
    )


def shape(dims, dtype=BF):
    return jax.ShapeDtypeStruct(dims, dtype)


def iota(dims, axis):
    return lax.broadcasted_iota(I32, dims, axis)


def dot(a, b, over):
    return lax.dot_general(
        a, b, (((over[0],), (over[1],)), ((), ())), preferred_element_type=F32
    )


def normalize(values):
    centre = jnp.mean(values, axis=-1, keepdims=True)
    shifted = values - centre
    spread = jnp.mean(shifted * shifted, axis=-1, keepdims=True)
    return (shifted * lax.rsqrt(spread + EPSILON)).astype(BF)


def slot_of(row):
    i, j = row // 128, (row // 64) % 2
    a, b = (row // 8) % 8, row % 8
    return (2 * a + i) * MAXGRID + 2 * b + j


def vision_kernel(
    grid_ref, picture_hbm, qkv_hbm, out_hbm, s0_ref, s1_ref, s2_ref, s3_ref,
    picture_ref, qkv_ref, out_ref, arrived,
):
    copies = [pltpu.make_async_copy(picture_hbm, picture_ref, arrived.at[0])]
    for part in range(3):
        copies.append(
            pltpu.make_async_copy(qkv_hbm.at[part], qkv_ref.at[part], arrived.at[1 + part])
        )
    copies.append(pltpu.make_async_copy(out_hbm, out_ref, arrived.at[4]))
    for copy in copies:
        copy.start()
    count = picture_ref.shape[0]
    local_width = qkv_ref.shape[1]
    copies[0].wait()
    normed = normalize(picture_ref[...].astype(F32))
    parts = []
    for part in range(3):
        copies[1 + part].wait()
        parts.append(dot(qkv_ref[part], normed, (1, 1)))
    slots = iota((count, 1), 0)
    usable = (slots // MAXGRID < 2 * grid_ref[0, 0]) & (slots % MAXGRID < 2 * grid_ref[0, 1])
    contexts = []
    for first in range(0, local_width, HEAD):
        q, k, v = (x[first : first + HEAD].astype(BF) for x in parts)
        scores = jnp.where(usable, dot(k, q, (0, 0)), -jnp.inf)
        expons = jnp.exp2((scores - jnp.max(scores, axis=0, keepdims=True)) * SCALE2)
        total = jnp.sum(expons, axis=0, keepdims=True)
        contexts.append(dot(v, expons.astype(BF), (1, 0)) / total)
    context = jnp.concatenate(contexts, axis=0).astype(BF)
    row = (iota((count, count), 0) + lax.axis_index("t") * MERGED) % count
    order = slot_of(row) == iota((count, count), 1)
    context = dot(order.astype(BF), context, (1, 1)).astype(BF)
    copies[4].wait()
    share = dot(context, out_ref[...], (1, 0)).astype(BF)
    for by, share_ref in enumerate((s0_ref, s1_ref, s2_ref, s3_ref)):
        share_ref[...] = share[by * MERGED : (by + 1) * MERGED]


def sum_kernel(parts_ref, rows_ref):
    for y in range(4):
        total = parts_ref[y, 0].astype(F32)
        for t in range(1, 4):
            total = total + parts_ref[y, t].astype(F32)
        rows_ref[y] = total.astype(BF)


def join_kernel(parts_ref, rows_ref):
    total = parts_ref[0].astype(F32)
    for part in range(1, 8):
        total = total + parts_ref[part].astype(F32)
    rows_ref[...] = total.astype(BF)


def select_kernel(place_ref, mine_ref, other_ref, routed_ref):
    wide = mine_ref.shape[2]
    width = wide - FACTS
    rows = jnp.concatenate(
        [mine_ref[...].reshape(64, wide), other_ref[...].reshape(64, wide)], axis=0
    )
    facts = rows[:, width:].astype(F32)
    block, there = facts[:, 0:1], facts[:, 4:5]
    same_core = block - 2.0 * jnp.floor(block * 0.5) == place_ref[1].astype(F32)
    to = jnp.where(same_core & (there > 0.0), jnp.floor(block * 0.125), -1.0).astype(I32)
    source, target = iota((128, 128), 0), iota((128, 128), 1)
    chosen = (to == target // 16) & (source % 16 == target % 16)
    routed = dot(chosen.astype(BF), rows, (0, 0))
    routed_ref[...] = routed.astype(BF).reshape(8, 16, wide)


def own_kernel(
    place_ref, grid_ref, block_ref, offset_ref, picture_ref, share_ref, own_ref, facts_ref
):
    t, block = place_ref[2], block_ref[0]
    count = picture_ref.shape[0]
    row = iota((MERGED, count), 0) + t * MERGED
    chosen = (slot_of(row) == iota((MERGED, count), 1)).astype(BF)
    own_ref[...] = dot(chosen, picture_ref[...], (1, 0)) + share_ref[...].astype(F32)
    lane, line = iota((8, FACTS), 1), iota((8, FACTS), 0)
    facts = jnp.zeros((8, FACTS), I32)
    for index, fact in enumerate((block, offset_ref[0], grid_ref[0, 0], grid_ref[0, 1], 1)):
        facts = jnp.where((lane == index) & (t == 0), fact, facts)
    facts_ref[...] = jnp.where(line == 0, facts, block % 8 // 2).astype(F32)


def merge_kernel(facts_ref, own_ref, s1_ref, s2_ref, s3_ref, w0_ref, w1_ref, w2_ref, rows_ref):
    width = own_ref.shape[1]
    total = own_ref[...]
    for share in (s1_ref, s2_ref, s3_ref):
        total = total + share[...].astype(F32)
    normed = normalize(total)
    first, merged = 0, jnp.zeros((MERGED, width), F32)
    for weight in (w0_ref, w1_ref, w2_ref):
        deep = weight.shape[0]
        merged = merged + dot(normed[:, first : first + deep], weight[...], (1, 0))
        first = first + deep
    merged = merged.astype(BF)
    facts = jnp.broadcast_to(facts_ref[0:1, :], (MERGED, FACTS)).astype(BF)
    to_y = facts_ref[1:2, 0:1]
    for y in range(4):
        here = to_y == float(y)
        rows_ref[y, :, :width] = jnp.where(here, merged, jnp.zeros_like(merged))
        rows_ref[y, :, width:] = jnp.where(here, facts, jnp.zeros_like(facts))


def placed_rows(place_ref, pieces_refs, tokens_ref):
    width = tokens_ref.shape[1]
    pieces, firsts = [], []
    for by, piece in enumerate(pieces_refs):
        pieces.append(piece[...])
        firsts.append(jnp.full((16, 1), 16 * lax.rem(place_ref[2] + 4 - by, 4), I32))
    rows = jnp.concatenate(pieces, axis=0)
    cell = jnp.concatenate(firsts, axis=0) + iota((MERGED, 1), 0) % 16
    facts = rows[:, width:].astype(F32)
    a, b = (cell // 8).astype(F32), (cell % 8).astype(F32)
    offset, high, wide, there = (facts[:, i : i + 1] for i in (1, 2, 3, 4))
    target = offset + a * wide + b
    usable = (a < high) & (b < wide) & (there > 0.0)
    target = jnp.where(usable, target, -1.0)
    table = (target == iota((MERGED, BLOCK), 1).astype(F32)).astype(BF)
    placed = dot(table, rows, (0, 0))
    covered = placed[:, width + 4 : width + 5] > 0.0
    return jnp.where(covered, placed[:, :width], tokens_ref[...].astype(F32))


def place_kernel(place_ref, r0_ref, r1_ref, r2_ref, r3_ref, tokens_ref, prompt_ref):
    pieces = (r0_ref, r1_ref, r2_ref, r3_ref)
    prompt_ref[...] = placed_rows(place_ref, pieces, tokens_ref).astype(BF)


def project_kernel(
    place_ref, r0_ref, r1_ref, r2_ref, r3_ref, tokens_ref, qkv_ref, heads_ref
):
    pieces = (r0_ref, r1_ref, r2_ref, r3_ref)
    normed = normalize(placed_rows(place_ref, pieces, tokens_ref))
    for part in range(3):
        projected = dot(qkv_ref[part], normed, (1, 1))
        for head in range(4):
            heads_ref[head, part] = projected[head * HEAD : (head + 1) * HEAD].astype(BF)


def attend_kernel(facts_ref, lengths_ref, own_ref, near_ref, far_ref,
                  own2_ref, near2_ref, far2_ref, sent_ref):
    z, c = facts_ref[0], facts_ref[1]
    blocks = []
    for mine, other, skip in (
        (far_ref, far2_ref, 0), (near_ref, near2_ref, 0), (own_ref, own2_ref, 1)
    ):
        blocks += [(mine, other, skip, y) for y in range(4)]

    def strip_of(strip, part):
        mine, other, skip, y = blocks[strip]
        return jnp.concatenate([mine[y, skip + part], other[y, part]], axis=1)

    row = iota((BLOCK, 1), 0)
    lane = iota((BLOCK, STRIP), 1)
    column = lane + jnp.where(lane < BLOCK, c * BLOCK, -c * BLOCK)
    base = (z - 2) * 1024
    for j in range(4):
        here = 2048 + j * 256 + c * BLOCK + row
        start = jnp.zeros((BLOCK, 1), I32)
        end = jnp.int32(0)
        for prompt in range(16):
            end = end + lengths_ref[prompt]
            start = jnp.where(end <= here + base, end, start)
        low = start - base
        query = own_ref[j, 0].T
        strips, top = [], None
        for strip in range(j, j + 9):
            scores = dot(query, strip_of(strip, 0), (1, 0))
            visible = column >= low - strip * STRIP
            if strip >= 8:
                visible = visible & (column <= here - strip * STRIP)
            scores = jnp.where(visible, scores, -jnp.inf)
            top = scores if top is None else jnp.maximum(top, scores)
            strips.append((strip, scores))
        top = jnp.max(top, axis=1, keepdims=True)
        total = jnp.zeros((BLOCK, STRIP), F32)
        summed = jnp.zeros((HEAD, BLOCK), F32)
        for strip, scores in strips:
            expons = jnp.exp2((scores - top) * SCALE2)
            total = total + expons
            summed = summed + dot(strip_of(strip, 1), expons.astype(BF), (1, 1))
        total = jnp.sum(total, axis=1, keepdims=True)
        total = jnp.transpose(jnp.broadcast_to(total, (BLOCK, BLOCK)))
        context = (summed / total[:HEAD]).astype(BF)
        for t in range(4):
            sent_ref[t, j] = context


def output_kernel(
    place_ref, context_ref, w0_ref, m2_ref, m1_ref, m3_ref, o2_ref, o1_ref, o3_ref,
    prompt_ref, out_ref,
):
    c, t = place_ref[1], place_ref[2]
    half = m1_ref.shape[0]
    width = out_ref.shape[1]
    pairs = [(context_ref[t, part].T, w0_ref.at[part * half : (part + 1) * half]) for part in (0, 1)]
    for by, mine, other in ((1, m1_ref, o1_ref), (2, m2_ref, o2_ref), (3, m3_ref, o3_ref)):
        source = lax.rem(t + 4 - by, 4)
        pairs.append((context_ref[source, c].T, mine))
        pairs.append((context_ref[source, 1 - c].T, other))
    for first in range(0, width, 256):
        strip = slice(first, min(first + 256, width))
        total = prompt_ref[:, strip].astype(F32)
        for context, weight in pairs:
            total = total + dot(context, weight[:, strip], (1, 0))
        out_ref[:, strip] = total.astype(BF)


def local(
    patches,
    picture_grid,
    vision_qkv,
    vision_out,
    merge_weight,
    picture_block,
    picture_offset,
    tokens,
    prompt_lengths,
    text_qkv,
    text_out,
):
    count, width = patches.shape[1:]
    local_width = vision_qkv.shape[2]
    wide = width + FACTS
    z = lax.axis_index("z")
    c = lax.axis_index("c")
    t = lax.axis_index("t")
    picture = patches[0]

    place = jnp.stack([z, c, t]).astype(I32)
    share = call(
        vision_kernel,
        [shape((MERGED, width))] * 4,
        [SMEM, HBM, HBM, HBM],
        [
            VMEM((count, width), BF),
            VMEM((3, local_width, width), BF),
            VMEM((local_width, width), BF),
            pltpu.SemaphoreType.DMA((5,)),
        ],
        limit=60,
    )(picture_grid, picture, vision_qkv.transpose(1, 2, 0), vision_out)
    shares = [around(share[by], "t", by) for by in range(1, 4)]
    own, facts = call(
        own_kernel,
        [shape((MERGED, width), F32), shape((8, FACTS), F32)],
        [SMEM] * 4 + [VMEM] * 2,
        flops=8 * 10**9,
    )(place, picture_grid, picture_block, picture_offset, picture, share[0])
    own, merge_weight = lax.optimization_barrier((own, merge_weight))
    merge_parts = jnp.split(merge_weight[0], [640, 1024], axis=0)
    routed = call(merge_kernel, shape((4, MERGED, wide)), [VMEM] * 8)(
        facts, own, *shares, *merge_parts
    )

    got = lax.all_to_all(routed.reshape(16, 16, wide), ("y", "t"), 0, 0, tiled=True)
    got = call(sum_kernel, shape((4, 16, wide)), [VMEM])(got.reshape(4, 4, 16, wide))
    other = around(got, "c", 1)
    routed = call(select_kernel, shape((8, 16, wide)), [SMEM, VMEM, VMEM])(place, got, other)
    routed, text_out = lax.optimization_barrier((routed, text_out))
    half = local_width // 2
    near_half = lax.dynamic_slice_in_dim(text_out, c * half, half, 0)
    near_half, tokens = lax.optimization_barrier((near_half, tokens))
    halves = [None] + [around(near_half, "t", by) for by in (1, 3)]
    pieces = [tokens] + [around(tokens, "t", by) for by in range(1, 4)]
    got = lax.all_to_all(routed, "z", 0, 0, tiled=True)
    got = call(join_kernel, shape((16, wide)), [VMEM])(got)
    rows = [got] + [around(got, "t", by) for by in range(1, 4)]
    own_tokens = jnp.zeros((4, BLOCK, local_width), BF)
    for by, piece in enumerate(pieces):
        own_tokens = lax.dynamic_update_index_in_dim(own_tokens, piece, (t - by) % 4, 0)
    own_tokens = own_tokens.transpose(1, 0, 2).reshape(BLOCK, width)
    heads = call(
        project_kernel,
        shape((4, 3, HEAD, BLOCK)),
        [SMEM] + [VMEM] * 6,
    )(place, *rows, own_tokens, text_qkv.transpose(1, 2, 0))
    heads, late_tokens, near_half = lax.optimization_barrier((heads, own_tokens, near_half))
    halves[0] = around(near_half, "t", 2)
    mine = lax.all_to_all(heads, "y", 0, 0, tiled=True)
    prompt_in = call(place_kernel, shape((BLOCK, width)), [SMEM] + [VMEM] * 5)(
        place, *rows, late_tokens
    )
    pair = mine[:, 1:]
    near, far = ahead(pair, "z", 1), ahead(pair, "z", 2)
    others = [around(x, "c", 1) for x in (pair, near, far)]
    halves = halves + [around(x, "c", 1) for x in halves]
    sent = call(
        attend_kernel,
        shape((4, 4, HEAD, BLOCK)),
        [SMEM, SMEM] + [VMEM] * 6,
        limit=16,
    )(place, prompt_lengths, mine, near, far, *others)
    context = lax.all_to_all(sent.reshape(16, HEAD, BLOCK), ("t", "y"), 0, 0, tiled=True)
    return call(output_kernel, shape((BLOCK, width)), [SMEM] + [VMEM] * 9)(
        place, context.reshape(4, 2, half, BLOCK), text_out, *halves, prompt_in
    )


def solution(mesh):
    split = Mesh(np.asarray(mesh.devices).reshape(8, 4, 2, 4), ("z", "y", "c", "t"))
    seq = ("z", "y", "c")
    placed = (
        P(seq, None, None),
        P(seq, None),
        P(None, None, "t"),
        P("t", None),
        P("t", None, None),
        P(seq),
        P(seq),
        P(seq, "t"),
        P(),
        P(None, None, "t"),
        P("t", None),
    )
    return jax.shard_map(
        local, mesh=split, in_specs=placed, out_specs=P(seq, None), check_vma=False
    )
```

```python
import jax
import jax.numpy as jnp
import numpy as np
from jax import lax
from jax.experimental import pallas as pl
from jax.experimental.pallas import tpu as pltpu
from jax.sharding import Mesh
from jax.sharding import PartitionSpec as P

HEAD = 88
MAXGRID = 16
BLOCK = 128
MERGED = 64
EPSILON = 1e-06
SCALE2 = HEAD ** (-0.5) / float(np.log(2.0))
BF = jnp.bfloat16
F32 = jnp.float32
I32 = jnp.int32
VMEM = pltpu.VMEM
SMEM = pltpu.SMEM
HBM = pltpu.HBM
FACTS = 128
STRIP = 256


def ahead(x, axis, by):
    count = lax.axis_size(axis)
    return lax.ppermute(x, axis, [(i, i + by) for i in range(count - by)])


def around(x, axis, by):
    count = lax.axis_size(axis)
    return lax.ppermute(x, axis, [(i, (i + by) % count) for i in range(count)])


def call(kernel, out_shape, spaces, scratch=(), limit=8, flops=None, tail=()):
    single = not isinstance(out_shape, (list, tuple))
    outs = pl.BlockSpec(memory_space=VMEM)
    cost = flops and pl.CostEstimate(flops=flops, transcendentals=0, bytes_accessed=flops // 400)
    return pl.pallas_call(
        kernel,
        out_shape=out_shape,
        in_specs=[pl.BlockSpec(memory_space=s) for s in spaces],
        out_specs=outs if single else [outs] * (len(out_shape) - len(tail)) + [pl.BlockSpec(memory_space=x) for x in tail],
        scratch_shapes=scratch,
        compiler_params=pltpu.CompilerParams(vmem_limit_bytes=limit << 20),
        cost_estimate=cost,
    )


def shape(dims, dtype=BF):
    return jax.ShapeDtypeStruct(dims, dtype)


def iota(dims, axis):
    return lax.broadcasted_iota(I32, dims, axis)


def dot(a, b, over):
    return lax.dot_general(
        a, b, (((over[0],), (over[1],)), ((), ())), preferred_element_type=F32
    )


def normalize(values):
    centre = jnp.mean(values, axis=-1, keepdims=True)
    shifted = values - centre
    spread = jnp.mean(shifted * shifted, axis=-1, keepdims=True)
    return (shifted * lax.rsqrt(spread + EPSILON)).astype(BF)


def slot_of(row):
    i, j = row // 128, (row // 64) % 2
    a, b = (row // 8) % 8, row % 8
    return (2 * a + i) * MAXGRID + 2 * b + j


def vision_kernel(
    grid_ref, picture_hbm, qkv_hbm, out_hbm, s0_ref, s1_ref, s2_ref, s3_ref,
    picture_ref, qkv_ref, out_ref, arrived,
):
    copies = [pltpu.make_async_copy(picture_hbm, picture_ref, arrived.at[0])]
    for part in range(3):
        copies.append(
            pltpu.make_async_copy(qkv_hbm.at[part], qkv_ref.at[part], arrived.at[1 + part])
        )
    copies.append(pltpu.make_async_copy(out_hbm, out_ref, arrived.at[4]))
    for copy in copies:
        copy.start()
    count = picture_ref.shape[0]
    local_width = qkv_ref.shape[1]
    copies[0].wait()
    normed = normalize(picture_ref[...].astype(F32))
    parts = []
    for part in range(3):
        copies[1 + part].wait()
        parts.append(dot(qkv_ref[part], normed, (1, 1)))
    slots = iota((count, 1), 0)
    usable = (slots // MAXGRID < 2 * grid_ref[0, 0]) & (slots % MAXGRID < 2 * grid_ref[0, 1])
    contexts = []
    for first in range(0, local_width, HEAD):
        q, k, v = (x[first : first + HEAD].astype(BF) for x in parts)
        scores = jnp.where(usable, dot(k, q, (0, 0)), -jnp.inf)
        expons = jnp.exp2((scores - jnp.max(scores, axis=0, keepdims=True)) * SCALE2)
        total = jnp.sum(expons, axis=0, keepdims=True)
        contexts.append(dot(v, expons.astype(BF), (1, 0)) / total)
    context = jnp.concatenate(contexts, axis=0).astype(BF)
    row = (iota((count, count), 0) + lax.axis_index("t") * MERGED) % count
    order = slot_of(row) == iota((count, count), 1)
    context = dot(order.astype(BF), context, (1, 1)).astype(BF)
    copies[4].wait()
    share = dot(context, out_ref[...], (1, 0)).astype(BF)
    for by, share_ref in enumerate((s0_ref, s1_ref, s2_ref, s3_ref)):
        share_ref[...] = share[by * MERGED : (by + 1) * MERGED]


def sum_kernel(parts_ref, rows_ref):
    for y in range(4):
        total = parts_ref[y, 0].astype(F32)
        for t in range(1, 4):
            total = total + parts_ref[y, t].astype(F32)
        rows_ref[y] = total.astype(BF)


def join_kernel(parts_ref, rows_ref):
    total = parts_ref[0].astype(F32)
    for part in range(1, 8):
        total = total + parts_ref[part].astype(F32)
    rows_ref[...] = total.astype(BF)


def select_kernel(place_ref, mine_ref, other_ref, routed_ref, same_ref):
    wide = mine_ref.shape[2]
    width = wide - FACTS
    rows = jnp.concatenate(
        [mine_ref[...].reshape(64, wide), other_ref[...].reshape(64, wide)], axis=0
    )
    facts = rows[:, width:].astype(F32)
    block, there = facts[:, 0:1], facts[:, 4:5]
    same_core = block - 2.0 * jnp.floor(block * 0.5) == place_ref[1].astype(F32)
    to = jnp.where(same_core & (there > 0.0), jnp.floor(block * 0.125), -1.0).astype(I32)
    source, target = iota((128, 128), 0), iota((128, 128), 1)
    chosen = (to == target // 16) & (source % 16 == target % 16)
    routed = dot(chosen.astype(BF), rows, (0, 0))
    routed_ref[...] = routed.astype(BF).reshape(8, 16, wide)
    for index in range(3):
        same_ref[index] = place_ref[index]


def own_kernel(
    place_ref, grid_ref, block_ref, offset_ref, picture_ref, share_ref, own_ref, facts_ref
):
    t, block = place_ref[2], block_ref[0]
    count = picture_ref.shape[0]
    row = iota((MERGED, count), 0) + t * MERGED
    chosen = (slot_of(row) == iota((MERGED, count), 1)).astype(BF)
    own_ref[...] = dot(chosen, picture_ref[...], (1, 0)) + share_ref[...].astype(F32)
    lane, line = iota((8, FACTS), 1), iota((8, FACTS), 0)
    facts = jnp.zeros((8, FACTS), I32)
    for index, fact in enumerate((block, offset_ref[0], grid_ref[0, 0], grid_ref[0, 1], 1)):
        facts = jnp.where((lane == index) & (t == 0), fact, facts)
    facts_ref[...] = jnp.where(line == 0, facts, block % 8 // 2).astype(F32)


def merge_kernel(facts_ref, own_ref, s1_ref, s2_ref, s3_ref, w0_ref, w1_ref, w2_ref, rows_ref):
    width = own_ref.shape[1]
    total = own_ref[...]
    for share in (s1_ref, s2_ref, s3_ref):
        total = total + share[...].astype(F32)
    normed = normalize(total)
    first, merged = 0, jnp.zeros((MERGED, width), F32)
    for weight in (w0_ref, w1_ref, w2_ref):
        deep = weight.shape[0]
        merged = merged + dot(normed[:, first : first + deep], weight[...], (1, 0))
        first = first + deep
    merged = merged.astype(BF)
    facts = jnp.broadcast_to(facts_ref[0:1, :], (MERGED, FACTS)).astype(BF)
    to_y = facts_ref[1:2, 0:1]
    for y in range(4):
        here = to_y == float(y)
        rows_ref[y, :, :width] = jnp.where(here, merged, jnp.zeros_like(merged))
        rows_ref[y, :, width:] = jnp.where(here, facts, jnp.zeros_like(facts))


def placed_rows(place_ref, pieces_refs, tokens_ref):
    width = tokens_ref.shape[1]
    pieces, firsts = [], []
    for by, piece in enumerate(pieces_refs):
        pieces.append(piece[...])
        firsts.append(jnp.full((16, 1), 16 * lax.rem(place_ref[2] + 4 - by, 4), I32))
    rows = jnp.concatenate(pieces, axis=0)
    cell = jnp.concatenate(firsts, axis=0) + iota((MERGED, 1), 0) % 16
    facts = rows[:, width:].astype(F32)
    a, b = (cell // 8).astype(F32), (cell % 8).astype(F32)
    offset, high, wide, there = (facts[:, i : i + 1] for i in (1, 2, 3, 4))
    target = offset + a * wide + b
    usable = (a < high) & (b < wide) & (there > 0.0)
    target = jnp.where(usable, target, -1.0)
    table = (target == iota((MERGED, BLOCK), 1).astype(F32)).astype(BF)
    placed = dot(table, rows, (0, 0))
    covered = placed[:, width + 4 : width + 5] > 0.0
    return jnp.where(covered, placed[:, :width], tokens_ref[...].astype(F32))


def place_kernel(place_ref, r0_ref, r1_ref, r2_ref, r3_ref, tokens_ref, prompt_ref):
    pieces = (r0_ref, r1_ref, r2_ref, r3_ref)
    prompt_ref[...] = placed_rows(place_ref, pieces, tokens_ref).astype(BF)


def project_kernel(
    place_ref, r0_ref, r1_ref, r2_ref, r3_ref, tokens_ref, qkv_ref, heads_ref
):
    pieces = (r0_ref, r1_ref, r2_ref, r3_ref)
    normed = normalize(placed_rows(place_ref, pieces, tokens_ref))
    for part in range(3):
        projected = dot(qkv_ref[part], normed, (1, 1))
        for head in range(4):
            heads_ref[head, part] = projected[head * HEAD : (head + 1) * HEAD].astype(BF)


def attend_kernel(facts_ref, lengths_ref, own_ref, near_ref, far_ref,
                  own2_ref, near2_ref, far2_ref, sent_ref):
    z, c = facts_ref[0], facts_ref[1]
    blocks = []
    for mine, other, skip in (
        (far_ref, far2_ref, 0), (near_ref, near2_ref, 0), (own_ref, own2_ref, 1)
    ):
        blocks += [(mine, other, skip, y) for y in range(4)]

    def strip_of(strip, part):
        mine, other, skip, y = blocks[strip]
        return jnp.concatenate([mine[y, skip + part], other[y, part]], axis=1)

    row = iota((BLOCK, 1), 0)
    lane = iota((BLOCK, STRIP), 1)
    column = lane + jnp.where(lane < BLOCK, c * BLOCK, -c * BLOCK)
    base = (z - 2) * 1024
    for j in range(4):
        here = 2048 + j * 256 + c * BLOCK + row
        start = jnp.zeros((BLOCK, 1), I32)
        end = jnp.int32(0)
        for prompt in range(16):
            end = end + lengths_ref[prompt]
            start = jnp.where(end <= here + base, end, start)
        low = start - base
        query = own_ref[j, 0].T
        strips, top = [], None
        for strip in range(j, j + 9):
            scores = dot(query, strip_of(strip, 0), (1, 0))
            visible = column >= low - strip * STRIP
            if strip >= 8:
                visible = visible & (column <= here - strip * STRIP)
            scores = jnp.where(visible, scores, -jnp.inf)
            top = scores if top is None else jnp.maximum(top, scores)
            strips.append((strip, scores))
        top = jnp.max(top, axis=1, keepdims=True)
        total = jnp.zeros((BLOCK, STRIP), F32)
        summed = jnp.zeros((HEAD, BLOCK), F32)
        for strip, scores in strips:
            expons = jnp.exp2((scores - top) * SCALE2)
            total = total + expons
            summed = summed + dot(strip_of(strip, 1), expons.astype(BF), (1, 1))
        total = jnp.sum(total, axis=1, keepdims=True)
        total = jnp.transpose(jnp.broadcast_to(total, (BLOCK, BLOCK)))
        context = (summed / total[:HEAD]).astype(BF)
        for t in range(4):
            sent_ref[t, j] = context


def output_kernel(
    place_ref, context_ref, w0_ref, m2_ref, m1_ref, m3_ref, o2_ref, o1_ref, o3_ref,
    prompt_ref, out_ref,
):
    c, t = place_ref[1], place_ref[2]
    half = m1_ref.shape[0]
    width = out_ref.shape[1]
    pairs = [(context_ref[t, part].T, w0_ref.at[part * half : (part + 1) * half]) for part in (0, 1)]
    for by, mine, other in ((1, m1_ref, o1_ref), (2, m2_ref, o2_ref), (3, m3_ref, o3_ref)):
        source = lax.rem(t + 4 - by, 4)
        pairs.append((context_ref[source, c].T, mine))
        pairs.append((context_ref[source, 1 - c].T, other))
    for first in range(0, width, 256):
        strip = slice(first, min(first + 256, width))
        total = prompt_ref[:, strip].astype(F32)
        for context, weight in pairs:
            total = total + dot(context, weight[:, strip], (1, 0))
        out_ref[:, strip] = total.astype(BF)


def local(
    patches,
    picture_grid,
    vision_qkv,
    vision_out,
    merge_weight,
    picture_block,
    picture_offset,
    tokens,
    prompt_lengths,
    text_qkv,
    text_out,
):
    count, width = patches.shape[1:]
    local_width = vision_qkv.shape[2]
    wide = width + FACTS
    z = lax.axis_index("z")
    c = lax.axis_index("c")
    t = lax.axis_index("t")
    picture = patches[0]

    place = jnp.stack([z, c, t]).astype(I32)
    share = call(
        vision_kernel,
        [shape((MERGED, width))] * 4,
        [SMEM, HBM, HBM, HBM],
        [
            VMEM((count, width), BF),
            VMEM((3, local_width, width), BF),
            VMEM((local_width, width), BF),
            pltpu.SemaphoreType.DMA((5,)),
        ],
        limit=60,
    )(picture_grid, picture, vision_qkv.transpose(1, 2, 0), vision_out)
    shares = [around(share[by], "t", by) for by in range(1, 4)]
    own, facts = call(
        own_kernel,
        [shape((MERGED, width), F32), shape((8, FACTS), F32)],
        [SMEM] * 4 + [VMEM] * 2,
        flops=8 * 10**9,
    )(place, picture_grid, picture_block, picture_offset, picture, share[0])
    own, text_early = lax.optimization_barrier((own, text_out))
    half = local_width // 2
    near_half = lax.dynamic_slice_in_dim(text_early, c * half, half, 0)
    near_half, merge_weight = lax.optimization_barrier((near_half, merge_weight))
    merge_parts = jnp.split(merge_weight[0], [640, 1024], axis=0)
    routed = call(merge_kernel, shape((4, MERGED, wide)), [VMEM] * 8)(
        facts, own, *shares, *merge_parts
    )

    got = lax.all_to_all(routed.reshape(16, 16, wide), ("y", "t"), 0, 0, tiled=True)
    got = call(sum_kernel, shape((4, 16, wide)), [VMEM])(got.reshape(4, 4, 16, wide))
    other = around(got, "c", 1)
    routed, place = call(
        select_kernel, [shape((8, 16, wide)), shape((3,), I32)], [SMEM, VMEM, VMEM], tail=(SMEM,)
    )(place, got, other)
    place = jnp.maximum(place, 0)
    place, near_half, tokens = lax.optimization_barrier((place, near_half, tokens))
    halves = [None] + [around(near_half, "t", by) for by in (1, 3)]
    pieces = [tokens] + [around(tokens, "t", by) for by in range(1, 4)]
    got = lax.all_to_all(routed, "z", 0, 0, tiled=True)
    got = call(join_kernel, shape((16, wide)), [VMEM])(got)
    rows = [got] + [around(got, "t", by) for by in range(1, 4)]
    own_tokens = jnp.zeros((4, BLOCK, local_width), BF)
    for by, piece in enumerate(pieces):
        own_tokens = lax.dynamic_update_index_in_dim(own_tokens, piece, (t - by) % 4, 0)
    own_tokens = own_tokens.transpose(1, 0, 2).reshape(BLOCK, width)
    heads = call(
        project_kernel,
        shape((4, 3, HEAD, BLOCK)),
        [SMEM] + [VMEM] * 6,
    )(place, *rows, own_tokens, text_qkv.transpose(1, 2, 0))
    heads, late_tokens, near_half = lax.optimization_barrier((heads, own_tokens, near_half))
    halves[0] = around(near_half, "t", 2)
    mine = lax.all_to_all(heads, "y", 0, 0, tiled=True)
    prompt_in = call(place_kernel, shape((BLOCK, width)), [SMEM] + [VMEM] * 5)(
        place, *rows, late_tokens
    )
    pair = mine[:, 1:]
    near, far = ahead(pair, "z", 1), ahead(pair, "z", 2)
    others = [around(x, "c", 1) for x in (pair, near, far)]
    halves = halves + [around(x, "c", 1) for x in halves]
    sent = call(
        attend_kernel,
        shape((4, 4, HEAD, BLOCK)),
        [SMEM, SMEM] + [VMEM] * 6,
        limit=16,
    )(place, prompt_lengths, mine, near, far, *others)
    context = lax.all_to_all(sent.reshape(16, HEAD, BLOCK), ("t", "y"), 0, 0, tiled=True)
    return call(output_kernel, shape((BLOCK, width)), [SMEM] + [VMEM] * 9)(
        place, context.reshape(4, 2, half, BLOCK), text_out, *halves, prompt_in
    )


def solution(mesh):
    split = Mesh(np.asarray(mesh.devices).reshape(8, 4, 2, 4), ("z", "y", "c", "t"))
    seq = ("z", "y", "c")
    placed = (
        P(seq, None, None),
        P(seq, None),
        P(None, None, "t"),
        P("t", None),
        P("t", None, None),
        P(seq),
        P(seq),
        P(seq, "t"),
        P(),
        P(None, None, "t"),
        P("t", None),
    )
    return jax.shard_map(
        local, mesh=split, in_specs=placed, out_specs=P(seq, None), check_vma=False
    )
```

```python
import jax
import jax.numpy as jnp
import numpy as np
from jax import lax
from jax.experimental import pallas as pl
from jax.experimental.pallas import tpu as pltpu
from jax.sharding import Mesh
from jax.sharding import PartitionSpec as P

HEAD = 88
MAXGRID = 16
BLOCK = 128
MERGED = 64
EPSILON = 1e-06
SCALE2 = HEAD ** (-0.5) / float(np.log(2.0))
BF = jnp.bfloat16
F32 = jnp.float32
I32 = jnp.int32
VMEM = pltpu.VMEM
SMEM = pltpu.SMEM
HBM = pltpu.HBM
FACTS = 128
STRIP = 256


def ahead(x, axis, by):
    count = lax.axis_size(axis)
    return lax.ppermute(x, axis, [(i, i + by) for i in range(count - by)])


def around(x, axis, by):
    count = lax.axis_size(axis)
    return lax.ppermute(x, axis, [(i, (i + by) % count) for i in range(count)])


def call(kernel, out_shape, spaces, scratch=(), limit=8, flops=None, tail=()):
    single = not isinstance(out_shape, (list, tuple))
    outs = pl.BlockSpec(memory_space=VMEM)
    cost = flops and pl.CostEstimate(flops=flops, transcendentals=0, bytes_accessed=flops // 400)
    return pl.pallas_call(
        kernel,
        out_shape=out_shape,
        in_specs=[pl.BlockSpec(memory_space=s) for s in spaces],
        out_specs=outs if single else [outs] * (len(out_shape) - len(tail)) + [pl.BlockSpec(memory_space=x) for x in tail],
        scratch_shapes=scratch,
        compiler_params=pltpu.CompilerParams(vmem_limit_bytes=limit << 20),
        cost_estimate=cost,
    )


def shape(dims, dtype=BF):
    return jax.ShapeDtypeStruct(dims, dtype)


def iota(dims, axis):
    return lax.broadcasted_iota(I32, dims, axis)


def dot(a, b, over):
    return lax.dot_general(
        a, b, (((over[0],), (over[1],)), ((), ())), preferred_element_type=F32
    )


def normalize(values):
    centre = jnp.mean(values, axis=-1, keepdims=True)
    shifted = values - centre
    spread = jnp.mean(shifted * shifted, axis=-1, keepdims=True)
    return (shifted * lax.rsqrt(spread + EPSILON)).astype(BF)


def slot_of(row):
    i, j = row // 128, (row // 64) % 2
    a, b = (row // 8) % 8, row % 8
    return (2 * a + i) * MAXGRID + 2 * b + j


def vision_kernel(
    grid_ref, picture_hbm, qkv_hbm, out_hbm, s0_ref, s1_ref, s2_ref, s3_ref,
    picture_ref, qkv_ref, out_ref, arrived,
):
    copies = [pltpu.make_async_copy(picture_hbm, picture_ref, arrived.at[0])]
    for part in range(3):
        copies.append(
            pltpu.make_async_copy(qkv_hbm.at[part], qkv_ref.at[part], arrived.at[1 + part])
        )
    copies.append(pltpu.make_async_copy(out_hbm, out_ref, arrived.at[4]))
    for copy in copies:
        copy.start()
    count = picture_ref.shape[0]
    local_width = qkv_ref.shape[1]
    copies[0].wait()
    normed = normalize(picture_ref[...].astype(F32))
    parts = []
    for part in range(3):
        copies[1 + part].wait()
        parts.append(dot(qkv_ref[part], normed, (1, 1)))
    slots = iota((count, 1), 0)
    usable = (slots // MAXGRID < 2 * grid_ref[0, 0]) & (slots % MAXGRID < 2 * grid_ref[0, 1])
    contexts = []
    for first in range(0, local_width, HEAD):
        q, k, v = (x[first : first + HEAD].astype(BF) for x in parts)
        scores = jnp.where(usable, dot(k, q, (0, 0)), -jnp.inf)
        expons = jnp.exp2((scores - jnp.max(scores, axis=0, keepdims=True)) * SCALE2)
        total = jnp.sum(expons, axis=0, keepdims=True)
        contexts.append(dot(v, expons.astype(BF), (1, 0)) / total)
    context = jnp.concatenate(contexts, axis=0).astype(BF)
    row = (iota((count, count), 0) + lax.axis_index("t") * MERGED) % count
    order = slot_of(row) == iota((count, count), 1)
    context = dot(order.astype(BF), context, (1, 1)).astype(BF)
    copies[4].wait()
    share = dot(context, out_ref[...], (1, 0)).astype(BF)
    for by, share_ref in enumerate((s0_ref, s1_ref, s2_ref, s3_ref)):
        share_ref[...] = share[by * MERGED : (by + 1) * MERGED]


def sum_kernel(parts_ref, rows_ref):
    for y in range(4):
        total = parts_ref[y, 0].astype(F32)
        for t in range(1, 4):
            total = total + parts_ref[y, t].astype(F32)
        rows_ref[y] = total.astype(BF)


def join_kernel(place_ref, parts_ref, rows_ref, same_ref):
    total = parts_ref[0].astype(F32)
    for part in range(1, 8):
        total = total + parts_ref[part].astype(F32)
    rows_ref[...] = total.astype(BF)
    for index in range(3):
        same_ref[index] = place_ref[index]


def select_kernel(place_ref, mine_ref, other_ref, routed_ref, same_ref):
    wide = mine_ref.shape[2]
    width = wide - FACTS
    rows = jnp.concatenate(
        [mine_ref[...].reshape(64, wide), other_ref[...].reshape(64, wide)], axis=0
    )
    facts = rows[:, width:].astype(F32)
    block, there = facts[:, 0:1], facts[:, 4:5]
    same_core = block - 2.0 * jnp.floor(block * 0.5) == place_ref[1].astype(F32)
    to = jnp.where(same_core & (there > 0.0), jnp.floor(block * 0.125), -1.0).astype(I32)
    source, target = iota((128, 128), 0), iota((128, 128), 1)
    chosen = (to == target // 16) & (source % 16 == target % 16)
    routed = dot(chosen.astype(BF), rows, (0, 0))
    routed_ref[...] = routed.astype(BF).reshape(8, 16, wide)
    for index in range(3):
        same_ref[index] = place_ref[index]


def own_kernel(
    place_ref, grid_ref, block_ref, offset_ref, picture_ref, share_ref, own_ref, facts_ref
):
    t, block = place_ref[2], block_ref[0]
    count = picture_ref.shape[0]
    row = iota((MERGED, count), 0) + t * MERGED
    chosen = (slot_of(row) == iota((MERGED, count), 1)).astype(BF)
    own_ref[...] = dot(chosen, picture_ref[...], (1, 0)) + share_ref[...].astype(F32)
    lane, line = iota((8, FACTS), 1), iota((8, FACTS), 0)
    facts = jnp.zeros((8, FACTS), I32)
    for index, fact in enumerate((block, offset_ref[0], grid_ref[0, 0], grid_ref[0, 1], 1)):
        facts = jnp.where((lane == index) & (t == 0), fact, facts)
    facts_ref[...] = jnp.where(line == 0, facts, block % 8 // 2).astype(F32)


def merge_kernel(facts_ref, own_ref, s1_ref, s2_ref, s3_ref, w0_ref, w1_ref, w2_ref, rows_ref):
    width = own_ref.shape[1]
    total = own_ref[...]
    for share in (s1_ref, s2_ref, s3_ref):
        total = total + share[...].astype(F32)
    normed = normalize(total)
    first, merged = 0, jnp.zeros((MERGED, width), F32)
    for weight in (w0_ref, w1_ref, w2_ref):
        deep = weight.shape[0]
        merged = merged + dot(normed[:, first : first + deep], weight[...], (1, 0))
        first = first + deep
    merged = merged.astype(BF)
    facts = jnp.broadcast_to(facts_ref[0:1, :], (MERGED, FACTS)).astype(BF)
    to_y = facts_ref[1:2, 0:1]
    for y in range(4):
        here = to_y == float(y)
        rows_ref[y, :, :width] = jnp.where(here, merged, jnp.zeros_like(merged))
        rows_ref[y, :, width:] = jnp.where(here, facts, jnp.zeros_like(facts))


def placed_rows(place_ref, pieces_refs, tokens_ref):
    width = tokens_ref.shape[1]
    pieces, firsts = [], []
    for by, piece in enumerate(pieces_refs):
        pieces.append(piece[...])
        firsts.append(jnp.full((16, 1), 16 * lax.rem(place_ref[2] + 4 - by, 4), I32))
    rows = jnp.concatenate(pieces, axis=0)
    cell = jnp.concatenate(firsts, axis=0) + iota((MERGED, 1), 0) % 16
    facts = rows[:, width:].astype(F32)
    a, b = (cell // 8).astype(F32), (cell % 8).astype(F32)
    offset, high, wide, there = (facts[:, i : i + 1] for i in (1, 2, 3, 4))
    target = offset + a * wide + b
    usable = (a < high) & (b < wide) & (there > 0.0)
    target = jnp.where(usable, target, -1.0)
    table = (target == iota((MERGED, BLOCK), 1).astype(F32)).astype(BF)
    placed = dot(table, rows, (0, 0))
    covered = placed[:, width + 4 : width + 5] > 0.0
    return jnp.where(covered, placed[:, :width], tokens_ref[...].astype(F32))


def place_kernel(place_ref, r0_ref, r1_ref, r2_ref, r3_ref, tokens_ref, prompt_ref):
    pieces = (r0_ref, r1_ref, r2_ref, r3_ref)
    prompt_ref[...] = placed_rows(place_ref, pieces, tokens_ref).astype(BF)


def project_kernel(
    place_ref, r0_ref, r1_ref, r2_ref, r3_ref, tokens_ref, qkv_ref, heads_ref
):
    pieces = (r0_ref, r1_ref, r2_ref, r3_ref)
    normed = normalize(placed_rows(place_ref, pieces, tokens_ref))
    for part in range(3):
        projected = dot(qkv_ref[part], normed, (1, 1))
        for head in range(4):
            heads_ref[head, part] = projected[head * HEAD : (head + 1) * HEAD].astype(BF)


def attend_kernel(facts_ref, lengths_ref, own_ref, near_ref, far_ref,
                  own2_ref, near2_ref, far2_ref, sent_ref):
    z, c = facts_ref[0], facts_ref[1]
    blocks = []
    for mine, other, skip in (
        (far_ref, far2_ref, 0), (near_ref, near2_ref, 0), (own_ref, own2_ref, 1)
    ):
        blocks += [(mine, other, skip, y) for y in range(4)]

    def strip_of(strip, part):
        mine, other, skip, y = blocks[strip]
        return jnp.concatenate([mine[y, skip + part], other[y, part]], axis=1)

    row = iota((BLOCK, 1), 0)
    lane = iota((BLOCK, STRIP), 1)
    column = lane + jnp.where(lane < BLOCK, c * BLOCK, -c * BLOCK)
    base = (z - 2) * 1024
    for j in range(4):
        here = 2048 + j * 256 + c * BLOCK + row
        start = jnp.zeros((BLOCK, 1), I32)
        end = jnp.int32(0)
        for prompt in range(16):
            end = end + lengths_ref[prompt]
            start = jnp.where(end <= here + base, end, start)
        low = start - base
        query = own_ref[j, 0].T
        strips, top = [], None
        for strip in range(j, j + 9):
            scores = dot(query, strip_of(strip, 0), (1, 0))
            visible = column >= low - strip * STRIP
            if strip >= 8:
                visible = visible & (column <= here - strip * STRIP)
            scores = jnp.where(visible, scores, -jnp.inf)
            top = scores if top is None else jnp.maximum(top, scores)
            strips.append((strip, scores))
        top = jnp.max(top, axis=1, keepdims=True)
        total = jnp.zeros((BLOCK, STRIP), F32)
        summed = jnp.zeros((HEAD, BLOCK), F32)
        for strip, scores in strips:
            expons = jnp.exp2((scores - top) * SCALE2)
            total = total + expons
            summed = summed + dot(strip_of(strip, 1), expons.astype(BF), (1, 1))
        total = jnp.sum(total, axis=1, keepdims=True)
        total = jnp.transpose(jnp.broadcast_to(total, (BLOCK, BLOCK)))
        context = (summed / total[:HEAD]).astype(BF)
        for t in range(4):
            sent_ref[t, j] = context


def output_kernel(
    place_ref, context_ref, w0_ref, m2_ref, m1_ref, m3_ref, o2_ref, o1_ref, o3_ref,
    prompt_ref, out_ref,
):
    c, t = place_ref[1], place_ref[2]
    half = m1_ref.shape[0]
    width = out_ref.shape[1]
    pairs = [(context_ref[t, part].T, w0_ref.at[part * half : (part + 1) * half]) for part in (0, 1)]
    for by, mine, other in ((1, m1_ref, o1_ref), (2, m2_ref, o2_ref), (3, m3_ref, o3_ref)):
        source = lax.rem(t + 4 - by, 4)
        pairs.append((context_ref[source, c].T, mine))
        pairs.append((context_ref[source, 1 - c].T, other))
    for first in range(0, width, 256):
        strip = slice(first, min(first + 256, width))
        total = prompt_ref[:, strip].astype(F32)
        for context, weight in pairs:
            total = total + dot(context, weight[:, strip], (1, 0))
        out_ref[:, strip] = total.astype(BF)


def local(
    patches,
    picture_grid,
    vision_qkv,
    vision_out,
    merge_weight,
    picture_block,
    picture_offset,
    tokens,
    prompt_lengths,
    text_qkv,
    text_out,
):
    count, width = patches.shape[1:]
    local_width = vision_qkv.shape[2]
    wide = width + FACTS
    z = lax.axis_index("z")
    c = lax.axis_index("c")
    t = lax.axis_index("t")
    picture = patches[0]

    place = jnp.stack([z, c, t]).astype(I32)
    share = call(
        vision_kernel,
        [shape((MERGED, width))] * 4,
        [SMEM, HBM, HBM, HBM],
        [
            VMEM((count, width), BF),
            VMEM((3, local_width, width), BF),
            VMEM((local_width, width), BF),
            pltpu.SemaphoreType.DMA((5,)),
        ],
        limit=60,
    )(picture_grid, picture, vision_qkv.transpose(1, 2, 0), vision_out)
    shares = [around(share[by], "t", by) for by in range(1, 4)]
    own, facts = call(
        own_kernel,
        [shape((MERGED, width), F32), shape((8, FACTS), F32)],
        [SMEM] * 4 + [VMEM] * 2,
        flops=8 * 10**9,
    )(place, picture_grid, picture_block, picture_offset, picture, share[0])
    own, text_early = lax.optimization_barrier((own, text_out))
    half = local_width // 2
    near_half = lax.dynamic_slice_in_dim(text_early, c * half, half, 0)
    near_half, merge_weight = lax.optimization_barrier((near_half, merge_weight))
    merge_parts = jnp.split(merge_weight[0], [640, 1024], axis=0)
    routed = call(merge_kernel, shape((4, MERGED, wide)), [VMEM] * 8)(
        facts, own, *shares, *merge_parts
    )

    got = lax.all_to_all(routed.reshape(16, 16, wide), ("y", "t"), 0, 0, tiled=True)
    got = call(sum_kernel, shape((4, 16, wide)), [VMEM])(got.reshape(4, 4, 16, wide))
    other = around(got, "c", 1)
    routed, place = call(
        select_kernel, [shape((8, 16, wide)), shape((3,), I32)], [SMEM, VMEM, VMEM], tail=(SMEM,)
    )(place, got, other)
    place = jnp.maximum(place, 0)
    place, near_half, tokens = lax.optimization_barrier((place, near_half, tokens))
    halves = [None] + [around(near_half, "t", by) for by in (1, 3)]
    pieces = [tokens] + [around(tokens, "t", by) for by in range(1, 4)]
    got = lax.all_to_all(routed, "z", 0, 0, tiled=True)
    got, place = call(
        join_kernel, [shape((16, wide)), shape((3,), I32)], [SMEM, VMEM], tail=(SMEM,)
    )(place, got)
    rows = [got] + [around(got, "t", by) for by in range(1, 4)]
    place = jnp.maximum(place, 0)
    place, near_half = lax.optimization_barrier((place, near_half))
    halves[0] = around(near_half, "t", 2)
    own_tokens = jnp.zeros((4, BLOCK, local_width), BF)
    for by, piece in enumerate(pieces):
        own_tokens = lax.dynamic_update_index_in_dim(own_tokens, piece, (t - by) % 4, 0)
    own_tokens = own_tokens.transpose(1, 0, 2).reshape(BLOCK, width)
    heads = call(
        project_kernel,
        shape((4, 3, HEAD, BLOCK)),
        [SMEM] + [VMEM] * 6,
    )(place, *rows, own_tokens, text_qkv.transpose(1, 2, 0))
    heads, late_tokens = lax.optimization_barrier((heads, own_tokens))
    mine = lax.all_to_all(heads, "y", 0, 0, tiled=True)
    prompt_in = call(place_kernel, shape((BLOCK, width)), [SMEM] + [VMEM] * 5)(
        place, *rows, late_tokens
    )
    pair = mine[:, 1:]
    near, far = ahead(pair, "z", 1), ahead(pair, "z", 2)
    others = [around(x, "c", 1) for x in (pair, near, far)]
    halves = halves + [around(x, "c", 1) for x in halves]
    sent = call(
        attend_kernel,
        shape((4, 4, HEAD, BLOCK)),
        [SMEM, SMEM] + [VMEM] * 6,
        limit=16,
    )(place, prompt_lengths, mine, near, far, *others)
    context = lax.all_to_all(sent.reshape(16, HEAD, BLOCK), ("t", "y"), 0, 0, tiled=True)
    return call(output_kernel, shape((BLOCK, width)), [SMEM] + [VMEM] * 9)(
        place, context.reshape(4, 2, half, BLOCK), text_out, *halves, prompt_in
    )


def solution(mesh):
    split = Mesh(np.asarray(mesh.devices).reshape(8, 4, 2, 4), ("z", "y", "c", "t"))
    seq = ("z", "y", "c")
    placed = (
        P(seq, None, None),
        P(seq, None),
        P(None, None, "t"),
        P("t", None),
        P("t", None, None),
        P(seq),
        P(seq),
        P(seq, "t"),
        P(),
        P(None, None, "t"),
        P("t", None),
    )
    return jax.shard_map(
        local, mesh=split, in_specs=placed, out_specs=P(seq, None), check_vma=False
    )
```

```python
import jax
import jax.numpy as jnp
import numpy as np
from jax import lax
from jax.experimental import pallas as pl
from jax.experimental.pallas import tpu as pltpu
from jax.sharding import Mesh
from jax.sharding import PartitionSpec as P

HEAD = 88
MAXGRID = 16
BLOCK = 128
MERGED = 64
EPSILON = 1e-06
SCALE2 = HEAD ** (-0.5) / float(np.log(2.0))
BF = jnp.bfloat16
F32 = jnp.float32
I32 = jnp.int32
VMEM = pltpu.VMEM
SMEM = pltpu.SMEM
HBM = pltpu.HBM
FACTS = 128
STRIP = 256


def ahead(x, axis, by):
    count = lax.axis_size(axis)
    return lax.ppermute(x, axis, [(i, i + by) for i in range(count - by)])


def around(x, axis, by):
    count = lax.axis_size(axis)
    return lax.ppermute(x, axis, [(i, (i + by) % count) for i in range(count)])


def call(kernel, out_shape, spaces, scratch=(), limit=8, flops=None, tail=()):
    single = not isinstance(out_shape, (list, tuple))
    outs = pl.BlockSpec(memory_space=VMEM)
    cost = flops and pl.CostEstimate(flops=flops, transcendentals=0, bytes_accessed=flops // 400)
    return pl.pallas_call(
        kernel,
        out_shape=out_shape,
        in_specs=[pl.BlockSpec(memory_space=s) for s in spaces],
        out_specs=outs if single else [outs] * (len(out_shape) - len(tail)) + [pl.BlockSpec(memory_space=x) for x in tail],
        scratch_shapes=scratch,
        compiler_params=pltpu.CompilerParams(vmem_limit_bytes=limit << 20),
        cost_estimate=cost,
    )


def shape(dims, dtype=BF):
    return jax.ShapeDtypeStruct(dims, dtype)


def iota(dims, axis):
    return lax.broadcasted_iota(I32, dims, axis)


def dot(a, b, over):
    return lax.dot_general(
        a, b, (((over[0],), (over[1],)), ((), ())), preferred_element_type=F32
    )


def normalize(values):
    centre = jnp.mean(values, axis=-1, keepdims=True)
    shifted = values - centre
    spread = jnp.mean(shifted * shifted, axis=-1, keepdims=True)
    return (shifted * lax.rsqrt(spread + EPSILON)).astype(BF)


def slot_of(row):
    i, j = row // 128, (row // 64) % 2
    a, b = (row // 8) % 8, row % 8
    return (2 * a + i) * MAXGRID + 2 * b + j


def vision_kernel(
    grid_ref, picture_hbm, qkv_hbm, out_hbm, s0_ref, s1_ref, s2_ref, s3_ref,
    picture_ref, qkv_ref, out_ref, arrived,
):
    copies = [pltpu.make_async_copy(picture_hbm, picture_ref, arrived.at[0])]
    for part in range(3):
        copies.append(
            pltpu.make_async_copy(qkv_hbm.at[part], qkv_ref.at[part], arrived.at[1 + part])
        )
    copies.append(pltpu.make_async_copy(out_hbm, out_ref, arrived.at[4]))
    for copy in copies:
        copy.start()
    count = picture_ref.shape[0]
    local_width = qkv_ref.shape[1]
    copies[0].wait()
    normed = normalize(picture_ref[...].astype(F32))
    parts = []
    for part in range(3):
        copies[1 + part].wait()
        parts.append(dot(qkv_ref[part], normed, (1, 1)))
    slots = iota((count, 1), 0)
    usable = (slots // MAXGRID < 2 * grid_ref[0, 0]) & (slots % MAXGRID < 2 * grid_ref[0, 1])
    contexts = []
    for first in range(0, local_width, HEAD):
        q, k, v = (x[first : first + HEAD].astype(BF) for x in parts)
        scores = jnp.where(usable, dot(k, q, (0, 0)), -jnp.inf)
        expons = jnp.exp2((scores - jnp.max(scores, axis=0, keepdims=True)) * SCALE2)
        total = jnp.sum(expons, axis=0, keepdims=True)
        contexts.append(dot(v, expons.astype(BF), (1, 0)) / total)
    context = jnp.concatenate(contexts, axis=0).astype(BF)
    row = (iota((count, count), 0) + lax.axis_index("t") * MERGED) % count
    order = slot_of(row) == iota((count, count), 1)
    context = dot(order.astype(BF), context, (1, 1)).astype(BF)
    copies[4].wait()
    share = dot(context, out_ref[...], (1, 0)).astype(BF)
    for by, share_ref in enumerate((s0_ref, s1_ref, s2_ref, s3_ref)):
        share_ref[...] = share[by * MERGED : (by + 1) * MERGED]


def sum_kernel(parts_ref, rows_ref):
    for y in range(4):
        total = parts_ref[0, y].astype(F32)
        for t in range(1, 4):
            total = total + parts_ref[t, y].astype(F32)
        rows_ref[y] = total.astype(BF)


def join_kernel(parts_ref, rows_ref):
    total = parts_ref[0].astype(F32)
    for part in range(1, 8):
        total = total + parts_ref[part].astype(F32)
    rows_ref[...] = total.astype(BF)


def order_kernel(place_ref, after_ref, same_ref):
    for index in range(3):
        same_ref[index] = place_ref[index]


def select_kernel(place_ref, mine_ref, other_ref, routed_ref):
    wide = mine_ref.shape[2]
    width = wide - FACTS
    rows = jnp.concatenate(
        [mine_ref[...].reshape(64, wide), other_ref[...].reshape(64, wide)], axis=0
    )
    facts = rows[:, width:].astype(F32)
    block, there = facts[:, 0:1], facts[:, 4:5]
    same_core = block - 2.0 * jnp.floor(block * 0.5) == place_ref[1].astype(F32)
    to = jnp.where(same_core & (there > 0.0), jnp.floor(block * 0.125), -1.0).astype(I32)
    source, target = iota((128, 128), 0), iota((128, 128), 1)
    chosen = (to == target // 16) & (source % 16 == target % 16)
    routed = dot(chosen.astype(BF), rows, (0, 0))
    routed_ref[...] = routed.astype(BF).reshape(8, 16, wide)


def own_kernel(
    place_ref, grid_ref, block_ref, offset_ref, picture_ref, share_ref, own_ref, facts_ref
):
    t, block = place_ref[2], block_ref[0]
    count = picture_ref.shape[0]
    row = iota((MERGED, count), 0) + t * MERGED
    chosen = (slot_of(row) == iota((MERGED, count), 1)).astype(BF)
    own_ref[...] = dot(chosen, picture_ref[...], (1, 0)) + share_ref[...].astype(F32)
    lane, line = iota((8, FACTS), 1), iota((8, FACTS), 0)
    facts = jnp.zeros((8, FACTS), I32)
    for index, fact in enumerate((block, offset_ref[0], grid_ref[0, 0], grid_ref[0, 1], 1)):
        facts = jnp.where((lane == index) & (t == 0), fact, facts)
    facts_ref[...] = jnp.where(line == 0, facts, block % 8 // 2).astype(F32)


def merge_kernel(facts_ref, own_ref, s1_ref, s2_ref, s3_ref, w0_ref, w1_ref, w2_ref, rows_ref):
    width = own_ref.shape[1]
    total = own_ref[...]
    for share in (s1_ref, s2_ref, s3_ref):
        total = total + share[...].astype(F32)
    normed = normalize(total)
    first, merged = 0, jnp.zeros((MERGED, width), F32)
    for weight in (w0_ref, w1_ref, w2_ref):
        deep = weight.shape[0]
        merged = merged + dot(normed[:, first : first + deep], weight[...], (1, 0))
        first = first + deep
    merged = merged.astype(BF)
    facts = jnp.broadcast_to(facts_ref[0:1, :], (MERGED, FACTS)).astype(BF)
    to_y = facts_ref[1:2, 0:1]
    for y in range(4):
        here = to_y == float(y)
        rows = jnp.where(here, merged, jnp.zeros_like(merged))
        ends = jnp.where(here, facts, jnp.zeros_like(facts))
        for t in range(4):
            rows_ref[t, y, :, :width] = rows[t * 16 : (t + 1) * 16]
            rows_ref[t, y, :, width:] = ends[t * 16 : (t + 1) * 16]


def placed_rows(place_ref, pieces_refs, tokens_ref):
    width = tokens_ref.shape[1]
    pieces, firsts = [], []
    for by, piece in enumerate(pieces_refs):
        pieces.append(piece[...])
        firsts.append(jnp.full((16, 1), 16 * lax.rem(place_ref[2] + 4 - by, 4), I32))
    rows = jnp.concatenate(pieces, axis=0)
    cell = jnp.concatenate(firsts, axis=0) + iota((MERGED, 1), 0) % 16
    facts = rows[:, width:].astype(F32)
    a, b = (cell // 8).astype(F32), (cell % 8).astype(F32)
    offset, high, wide, there = (facts[:, i : i + 1] for i in (1, 2, 3, 4))
    target = offset + a * wide + b
    usable = (a < high) & (b < wide) & (there > 0.0)
    target = jnp.where(usable, target, -1.0)
    table = (target == iota((MERGED, BLOCK), 1).astype(F32)).astype(BF)
    placed = dot(table, rows, (0, 0))
    covered = placed[:, width + 4 : width + 5] > 0.0
    return jnp.where(covered, placed[:, :width], tokens_ref[...].astype(F32))


def place_kernel(place_ref, r0_ref, r1_ref, r2_ref, r3_ref, tokens_ref, prompt_ref):
    pieces = (r0_ref, r1_ref, r2_ref, r3_ref)
    prompt_ref[...] = placed_rows(place_ref, pieces, tokens_ref).astype(BF)


def project_kernel(
    place_ref, r0_ref, r1_ref, r2_ref, r3_ref, tokens_ref, qkv_ref, heads_ref
):
    pieces = (r0_ref, r1_ref, r2_ref, r3_ref)
    normed = normalize(placed_rows(place_ref, pieces, tokens_ref))
    for part in range(3):
        projected = dot(qkv_ref[part], normed, (1, 1))
        for head in range(4):
            heads_ref[head, part] = projected[head * HEAD : (head + 1) * HEAD].astype(BF)


def attend_kernel(facts_ref, lengths_ref, own_ref, near_ref, far_ref,
                  own2_ref, near2_ref, far2_ref, sent_ref):
    z, c = facts_ref[0], facts_ref[1]
    blocks = []
    for mine, other, skip in (
        (far_ref, far2_ref, 0), (near_ref, near2_ref, 0), (own_ref, own2_ref, 1)
    ):
        blocks += [(mine, other, skip, y) for y in range(4)]

    def strip_of(strip, part):
        mine, other, skip, y = blocks[strip]
        return jnp.concatenate([mine[y, skip + part], other[y, part]], axis=1)

    row = iota((BLOCK, 1), 0)
    lane = iota((BLOCK, STRIP), 1)
    column = lane + jnp.where(lane < BLOCK, c * BLOCK, -c * BLOCK)
    base = (z - 2) * 1024
    for j in range(4):
        here = 2048 + j * 256 + c * BLOCK + row
        start = jnp.zeros((BLOCK, 1), I32)
        end = jnp.int32(0)
        for prompt in range(16):
            end = end + lengths_ref[prompt]
            start = jnp.where(end <= here + base, end, start)
        low = start - base
        query = own_ref[j, 0].T
        strips, top = [], None
        for strip in range(j, j + 9):
            scores = dot(query, strip_of(strip, 0), (1, 0))
            visible = column >= low - strip * STRIP
            if strip >= 8:
                visible = visible & (column <= here - strip * STRIP)
            scores = jnp.where(visible, scores, -jnp.inf)
            top = scores if top is None else jnp.maximum(top, scores)
            strips.append((strip, scores))
        top = jnp.max(top, axis=1, keepdims=True)
        total = jnp.zeros((BLOCK, STRIP), F32)
        summed = jnp.zeros((HEAD, BLOCK), F32)
        for strip, scores in strips:
            expons = jnp.exp2((scores - top) * SCALE2)
            total = total + expons
            summed = summed + dot(strip_of(strip, 1), expons.astype(BF), (1, 1))
        total = jnp.sum(total, axis=1, keepdims=True)
        total = jnp.transpose(jnp.broadcast_to(total, (BLOCK, BLOCK)))
        context = (summed / total[:HEAD]).astype(BF)
        for t in range(4):
            sent_ref[t, j] = context


def output_kernel(
    place_ref, context_ref, w0_ref, m2_ref, m1_ref, m3_ref, o2_ref, o1_ref, o3_ref,
    prompt_ref, out_ref,
):
    c, t = place_ref[1], place_ref[2]
    half = m1_ref.shape[0]
    width = out_ref.shape[1]
    pairs = [(context_ref[t, part].T, w0_ref.at[part * half : (part + 1) * half]) for part in (0, 1)]
    for by, mine, other in ((1, m1_ref, o1_ref), (2, m2_ref, o2_ref), (3, m3_ref, o3_ref)):
        source = lax.rem(t + 4 - by, 4)
        pairs.append((context_ref[source, c].T, mine))
        pairs.append((context_ref[source, 1 - c].T, other))
    for first in range(0, width, 256):
        strip = slice(first, min(first + 256, width))
        total = prompt_ref[:, strip].astype(F32)
        for context, weight in pairs:
            total = total + dot(context, weight[:, strip], (1, 0))
        out_ref[:, strip] = total.astype(BF)


def local(
    patches,
    picture_grid,
    vision_qkv,
    vision_out,
    merge_weight,
    picture_block,
    picture_offset,
    tokens,
    prompt_lengths,
    text_qkv,
    text_out,
):
    count, width = patches.shape[1:]
    local_width = vision_qkv.shape[2]
    wide = width + FACTS
    z = lax.axis_index("z")
    c = lax.axis_index("c")
    t = lax.axis_index("t")
    picture = patches[0]

    place = jnp.stack([z, c, t]).astype(I32)
    share = call(
        vision_kernel,
        [shape((MERGED, width))] * 4,
        [SMEM, HBM, HBM, HBM],
        [
            VMEM((count, width), BF),
            VMEM((3, local_width, width), BF),
            VMEM((local_width, width), BF),
            pltpu.SemaphoreType.DMA((5,)),
        ],
        limit=60,
    )(picture_grid, picture, vision_qkv.transpose(1, 2, 0), vision_out)
    shares = [around(share[by], "t", by) for by in range(1, 4)]
    own, facts = call(
        own_kernel,
        [shape((MERGED, width), F32), shape((8, FACTS), F32)],
        [SMEM] * 4 + [VMEM] * 2,
        flops=8 * 10**9,
    )(place, picture_grid, picture_block, picture_offset, picture, share[0])
    own, text_early = lax.optimization_barrier((own, text_out))
    half = local_width // 2
    near_half = lax.dynamic_slice_in_dim(text_early, c * half, half, 0)
    near_half, merge_weight = lax.optimization_barrier((near_half, merge_weight))
    merge_parts = jnp.split(merge_weight[0], [640, 1024], axis=0)
    routed = call(merge_kernel, shape((4, 4, 16, wide)), [VMEM] * 8)(
        facts, own, *shares, *merge_parts
    )

    got = lax.all_to_all(routed.reshape(16, 16, wide), ("t", "y"), 0, 0, tiled=True)
    got = call(sum_kernel, shape((4, 16, wide)), [VMEM])(got.reshape(4, 4, 16, wide))
    other = around(got, "c", 1)
    routed = call(select_kernel, shape((8, 16, wide)), [SMEM, VMEM, VMEM])(place, got, other)
    place, = call(order_kernel, [shape((3,), I32)], [SMEM, pl.ANY], tail=(SMEM,))(place, routed)
    place, near_half, tokens = lax.optimization_barrier((place, near_half, tokens))
    halves = [None] + [around(near_half, "t", by) for by in (1, 3)]
    pieces = [tokens] + [around(tokens, "t", by) for by in range(1, 4)]
    got = lax.all_to_all(routed, "z", 0, 0, tiled=True)
    got = call(join_kernel, shape((16, wide)), [VMEM])(got)
    rows = [got] + [around(got, "t", by) for by in range(1, 4)]
    own_tokens = jnp.zeros((4, BLOCK, local_width), BF)
    for by, piece in enumerate(pieces):
        own_tokens = lax.dynamic_update_index_in_dim(own_tokens, piece, (t - by) % 4, 0)
    own_tokens = own_tokens.transpose(1, 0, 2).reshape(BLOCK, width)
    heads = call(
        project_kernel,
        shape((4, 3, HEAD, BLOCK)),
        [SMEM] + [VMEM] * 6,
    )(place, *rows, own_tokens, text_qkv.transpose(1, 2, 0))
    heads, late_tokens, near_half = lax.optimization_barrier((heads, own_tokens, near_half))
    halves[0] = around(near_half, "t", 2)
    mine = lax.all_to_all(heads, "y", 0, 0, tiled=True)
    prompt_in = call(place_kernel, shape((BLOCK, width)), [SMEM] + [VMEM] * 5)(
        place, *rows, late_tokens
    )
    pair = mine[:, 1:]
    near, far = ahead(pair, "z", 1), ahead(pair, "z", 2)
    others = [around(x, "c", 1) for x in (pair, near, far)]
    halves = halves + [around(x, "c", 1) for x in halves]
    sent = call(
        attend_kernel,
        shape((4, 4, HEAD, BLOCK)),
        [SMEM, SMEM] + [VMEM] * 6,
        limit=16,
    )(place, prompt_lengths, mine, near, far, *others)
    context = lax.all_to_all(sent.reshape(16, HEAD, BLOCK), ("t", "y"), 0, 0, tiled=True)
    return call(output_kernel, shape((BLOCK, width)), [SMEM] + [VMEM] * 9)(
        place, context.reshape(4, 2, half, BLOCK), text_out, *halves, prompt_in
    )


def solution(mesh):
    split = Mesh(np.asarray(mesh.devices).reshape(8, 4, 2, 4), ("z", "y", "c", "t"))
    seq = ("z", "y", "c")
    placed = (
        P(seq, None, None),
        P(seq, None),
        P(None, None, "t"),
        P("t", None),
        P("t", None, None),
        P(seq),
        P(seq),
        P(seq, "t"),
        P(),
        P(None, None, "t"),
        P("t", None),
    )
    return jax.shard_map(
        local, mesh=split, in_specs=placed, out_specs=P(seq, None), check_vma=False
    )
```

```python
import jax
import jax.numpy as jnp
import numpy as np
from jax import lax
from jax.experimental import pallas as pl
from jax.experimental.pallas import tpu as pltpu
from jax.sharding import Mesh
from jax.sharding import PartitionSpec as P

HEAD = 88
MAXGRID = 16
BLOCK = 128
MERGED = 64
EPSILON = 1e-06
SCALE2 = HEAD ** (-0.5) / float(np.log(2.0))
BF = jnp.bfloat16
F32 = jnp.float32
I32 = jnp.int32
VMEM = pltpu.VMEM
SMEM = pltpu.SMEM
HBM = pltpu.HBM
FACTS = 128
STRIP = 256


def ahead(x, axis, by):
    count = lax.axis_size(axis)
    return lax.ppermute(x, axis, [(i, i + by) for i in range(count - by)])


def around(x, axis, by):
    count = lax.axis_size(axis)
    return lax.ppermute(x, axis, [(i, (i + by) % count) for i in range(count)])


def call(kernel, out_shape, spaces, scratch=(), limit=8, flops=None, tail=()):
    single = not isinstance(out_shape, (list, tuple))
    outs = pl.BlockSpec(memory_space=VMEM)
    cost = flops and pl.CostEstimate(flops=flops, transcendentals=0, bytes_accessed=flops // 400)
    return pl.pallas_call(
        kernel,
        out_shape=out_shape,
        in_specs=[pl.BlockSpec(memory_space=s) for s in spaces],
        out_specs=outs if single else [outs] * (len(out_shape) - len(tail)) + [pl.BlockSpec(memory_space=x) for x in tail],
        scratch_shapes=scratch,
        compiler_params=pltpu.CompilerParams(vmem_limit_bytes=limit << 20),
        cost_estimate=cost,
    )


def shape(dims, dtype=BF):
    return jax.ShapeDtypeStruct(dims, dtype)


def iota(dims, axis):
    return lax.broadcasted_iota(I32, dims, axis)


def dot(a, b, over):
    return lax.dot_general(
        a, b, (((over[0],), (over[1],)), ((), ())), preferred_element_type=F32
    )


def normalize(values):
    centre = jnp.mean(values, axis=-1, keepdims=True)
    shifted = values - centre
    spread = jnp.mean(shifted * shifted, axis=-1, keepdims=True)
    return (shifted * lax.rsqrt(spread + EPSILON)).astype(BF)


def slot_of(row):
    i, j = row // 128, (row // 64) % 2
    a, b = (row // 8) % 8, row % 8
    return (2 * a + i) * MAXGRID + 2 * b + j


def vision_kernel(
    grid_ref, picture_hbm, qkv_hbm, out_hbm, s0_ref, s1_ref, s2_ref, s3_ref,
    picture_ref, qkv_ref, out_ref, arrived,
):
    copies = [pltpu.make_async_copy(picture_hbm, picture_ref, arrived.at[0])]
    for part in range(3):
        copies.append(
            pltpu.make_async_copy(qkv_hbm.at[part], qkv_ref.at[part], arrived.at[1 + part])
        )
    copies.append(pltpu.make_async_copy(out_hbm, out_ref, arrived.at[4]))
    for copy in copies:
        copy.start()
    count = picture_ref.shape[0]
    local_width = qkv_ref.shape[1]
    copies[0].wait()
    normed = normalize(picture_ref[...].astype(F32))
    parts = []
    for part in range(3):
        copies[1 + part].wait()
        parts.append(dot(qkv_ref[part], normed, (1, 1)))
    slots = iota((count, 1), 0)
    usable = (slots // MAXGRID < 2 * grid_ref[0, 0]) & (slots % MAXGRID < 2 * grid_ref[0, 1])
    contexts = []
    for first in range(0, local_width, HEAD):
        q, k, v = (x[first : first + HEAD].astype(BF) for x in parts)
        scores = jnp.where(usable, dot(k, q, (0, 0)), -jnp.inf)
        expons = jnp.exp2((scores - jnp.max(scores, axis=0, keepdims=True)) * SCALE2)
        total = jnp.sum(expons, axis=0, keepdims=True)
        contexts.append(dot(v, expons.astype(BF), (1, 0)) / total)
    context = jnp.concatenate(contexts, axis=0).astype(BF)
    row = (iota((count, count), 0) + lax.axis_index("t") * MERGED) % count
    order = slot_of(row) == iota((count, count), 1)
    context = dot(order.astype(BF), context, (1, 1)).astype(BF)
    copies[4].wait()
    share = dot(context, out_ref[...], (1, 0)).astype(BF)
    for by, share_ref in enumerate((s0_ref, s1_ref, s2_ref, s3_ref)):
        share_ref[...] = share[by * MERGED : (by + 1) * MERGED]


def sum_kernel(parts_ref, rows_ref):
    for y in range(4):
        total = parts_ref[y, 0].astype(F32)
        for t in range(1, 4):
            total = total + parts_ref[y, t].astype(F32)
        rows_ref[y] = total.astype(BF)


def join_kernel(parts_ref, rows_ref):
    total = parts_ref[0].astype(F32)
    for part in range(1, 8):
        total = total + parts_ref[part].astype(F32)
    rows_ref[...] = total.astype(BF)


def order_kernel(place_ref, after_ref, same_ref):
    for index in range(3):
        same_ref[index] = place_ref[index]


def select_kernel(place_ref, mine_ref, other_ref, routed_ref):
    wide = mine_ref.shape[2]
    width = wide - FACTS
    rows = jnp.concatenate(
        [mine_ref[...].reshape(64, wide), other_ref[...].reshape(64, wide)], axis=0
    )
    facts = rows[:, width:].astype(F32)
    block, there = facts[:, 0:1], facts[:, 4:5]
    same_core = block - 2.0 * jnp.floor(block * 0.5) == place_ref[1].astype(F32)
    to = jnp.where(same_core & (there > 0.0), jnp.floor(block * 0.125), -1.0).astype(I32)
    source, target = iota((128, 128), 0), iota((128, 128), 1)
    chosen = (to == target // 16) & (source % 16 == target % 16)
    routed = dot(chosen.astype(BF), rows, (0, 0))
    routed_ref[...] = routed.astype(BF).reshape(8, 16, wide)


def own_kernel(
    place_ref, grid_ref, block_ref, offset_ref, picture_ref, share_ref, own_ref, facts_ref
):
    t, block = place_ref[2], block_ref[0]
    count = picture_ref.shape[0]
    row = iota((MERGED, count), 0) + t * MERGED
    chosen = (slot_of(row) == iota((MERGED, count), 1)).astype(BF)
    own_ref[...] = dot(chosen, picture_ref[...], (1, 0)) + share_ref[...].astype(F32)
    lane, line = iota((8, FACTS), 1), iota((8, FACTS), 0)
    facts = jnp.zeros((8, FACTS), I32)
    for index, fact in enumerate((block, offset_ref[0], grid_ref[0, 0], grid_ref[0, 1], 1)):
        facts = jnp.where((lane == index) & (t == 0), fact, facts)
    facts_ref[...] = jnp.where(line == 0, facts, block % 8 // 2).astype(F32)


def merge_kernel(facts_ref, own_ref, s1_ref, s2_ref, s3_ref, w0_ref, w1_ref, w2_ref, rows_ref):
    width = own_ref.shape[1]
    total = own_ref[...]
    for share in (s1_ref, s2_ref, s3_ref):
        total = total + share[...].astype(F32)
    normed = normalize(total)
    first, merged = 0, jnp.zeros((MERGED, width), F32)
    for weight in (w0_ref, w1_ref, w2_ref):
        deep = weight.shape[0]
        merged = merged + dot(normed[:, first : first + deep], weight[...], (1, 0))
        first = first + deep
    merged = merged.astype(BF)
    facts = jnp.broadcast_to(facts_ref[0:1, :], (MERGED, FACTS)).astype(BF)
    to_y = facts_ref[1:2, 0:1]
    for y in range(4):
        here = to_y == float(y)
        rows_ref[y, :, :width] = jnp.where(here, merged, jnp.zeros_like(merged))
        rows_ref[y, :, width:] = jnp.where(here, facts, jnp.zeros_like(facts))


def placed_rows(place_ref, pieces_refs, tokens_ref):
    width = tokens_ref.shape[1]
    pieces, firsts = [], []
    for by, piece in enumerate(pieces_refs):
        pieces.append(piece[...])
        firsts.append(jnp.full((16, 1), 16 * lax.rem(place_ref[2] + 4 - by, 4), I32))
    rows = jnp.concatenate(pieces, axis=0)
    cell = jnp.concatenate(firsts, axis=0) + iota((MERGED, 1), 0) % 16
    facts = rows[:, width:].astype(F32)
    a, b = (cell // 8).astype(F32), (cell % 8).astype(F32)
    offset, high, wide, there = (facts[:, i : i + 1] for i in (1, 2, 3, 4))
    target = offset + a * wide + b
    usable = (a < high) & (b < wide) & (there > 0.0)
    target = jnp.where(usable, target, -1.0)
    table = (target == iota((MERGED, BLOCK), 1).astype(F32)).astype(BF)
    placed = dot(table, rows, (0, 0))
    covered = placed[:, width + 4 : width + 5] > 0.0
    return jnp.where(covered, placed[:, :width], tokens_ref[...].astype(F32))


def place_kernel(place_ref, r0_ref, r1_ref, r2_ref, r3_ref, tokens_ref, prompt_ref):
    pieces = (r0_ref, r1_ref, r2_ref, r3_ref)
    prompt_ref[...] = placed_rows(place_ref, pieces, tokens_ref).astype(BF)


def project_kernel(
    place_ref, r0_ref, r1_ref, r2_ref, r3_ref, tokens_ref, qkv_ref, heads_ref
):
    pieces = (r0_ref, r1_ref, r2_ref, r3_ref)
    normed = normalize(placed_rows(place_ref, pieces, tokens_ref))
    for part in range(3):
        projected = dot(qkv_ref[part], normed, (1, 1))
        for head in range(4):
            heads_ref[head, part] = projected[head * HEAD : (head + 1) * HEAD].astype(BF)


def attend_kernel(facts_ref, lengths_ref, own_ref, near_ref, far_ref,
                  own2_ref, near2_ref, far2_ref, sent_ref):
    z, c = facts_ref[0], facts_ref[1]
    blocks = []
    for mine, other, skip in (
        (far_ref, far2_ref, 0), (near_ref, near2_ref, 0), (own_ref, own2_ref, 1)
    ):
        blocks += [(mine, other, skip, y) for y in range(4)]

    def strip_of(strip, part):
        mine, other, skip, y = blocks[strip]
        return jnp.concatenate([mine[y, skip + part], other[y, part]], axis=1)

    row = iota((BLOCK, 1), 0)
    lane = iota((BLOCK, STRIP), 1)
    column = lane + jnp.where(lane < BLOCK, c * BLOCK, -c * BLOCK)
    base = (z - 2) * 1024
    for j in range(4):
        here = 2048 + j * 256 + c * BLOCK + row
        start = jnp.zeros((BLOCK, 1), I32)
        end = jnp.int32(0)
        for prompt in range(16):
            end = end + lengths_ref[prompt]
            start = jnp.where(end <= here + base, end, start)
        low = start - base
        query = own_ref[j, 0].T
        strips, top = [], None
        for strip in range(j, j + 9):
            scores = dot(query, strip_of(strip, 0), (1, 0))
            visible = column >= low - strip * STRIP
            if strip >= 8:
                visible = visible & (column <= here - strip * STRIP)
            scores = jnp.where(visible, scores, -jnp.inf)
            top = scores if top is None else jnp.maximum(top, scores)
            strips.append((strip, scores))
        top = jnp.max(top, axis=1, keepdims=True)
        total = jnp.zeros((BLOCK, STRIP), F32)
        summed = jnp.zeros((HEAD, BLOCK), F32)
        for strip, scores in strips:
            expons = jnp.exp2((scores - top) * SCALE2)
            total = total + expons
            summed = summed + dot(strip_of(strip, 1), expons.astype(BF), (1, 1))
        total = jnp.sum(total, axis=1, keepdims=True)
        total = jnp.transpose(jnp.broadcast_to(total, (BLOCK, BLOCK)))
        context = (summed / total[:HEAD]).astype(BF)
        for t in range(4):
            sent_ref[t, j] = context


def output_kernel(
    place_ref, context_ref, w0_ref, m2_ref, m1_ref, m3_ref, o2_ref, o1_ref, o3_ref,
    prompt_ref, out_ref,
):
    c, t = place_ref[1], place_ref[2]
    half = m1_ref.shape[0]
    width = out_ref.shape[1]
    pairs = [(context_ref[t, part].T, w0_ref.at[part * half : (part + 1) * half]) for part in (0, 1)]
    for by, mine, other in ((1, m1_ref, o1_ref), (2, m2_ref, o2_ref), (3, m3_ref, o3_ref)):
        source = lax.rem(t + 4 - by, 4)
        pairs.append((context_ref[source, c].T, mine))
        pairs.append((context_ref[source, 1 - c].T, other))
    for first in range(0, width, 256):
        strip = slice(first, min(first + 256, width))
        total = prompt_ref[:, strip].astype(F32)
        for context, weight in pairs:
            total = total + dot(context, weight[:, strip], (1, 0))
        out_ref[:, strip] = total.astype(BF)


def local(
    patches,
    picture_grid,
    vision_qkv,
    vision_out,
    merge_weight,
    picture_block,
    picture_offset,
    tokens,
    prompt_lengths,
    text_qkv,
    text_out,
):
    count, width = patches.shape[1:]
    local_width = vision_qkv.shape[2]
    wide = width + FACTS
    z = lax.axis_index("z")
    c = lax.axis_index("c")
    t = lax.axis_index("t")
    picture = patches[0]

    place = jnp.stack([z, c, t]).astype(I32)
    share = call(
        vision_kernel,
        [shape((MERGED, width))] * 4,
        [SMEM, HBM, HBM, HBM],
        [
            VMEM((count, width), BF),
            VMEM((3, local_width, width), BF),
            VMEM((local_width, width), BF),
            pltpu.SemaphoreType.DMA((5,)),
        ],
        limit=60,
    )(picture_grid, picture, vision_qkv.transpose(1, 2, 0), vision_out)
    shares = [around(share[by], "t", by) for by in range(1, 4)]
    own, facts = call(
        own_kernel,
        [shape((MERGED, width), F32), shape((8, FACTS), F32)],
        [SMEM] * 4 + [VMEM] * 2,
        flops=8 * 10**9,
    )(place, picture_grid, picture_block, picture_offset, picture, share[0])
    own, text_early = lax.optimization_barrier((own, text_out))
    half = local_width // 2
    near_half = lax.dynamic_slice_in_dim(text_early, c * half, half, 0)
    near_half, merge_weight = lax.optimization_barrier((near_half, merge_weight))
    merge_parts = jnp.split(merge_weight[0], [640, 1024], axis=0)
    routed = call(merge_kernel, shape((4, MERGED, wide)), [VMEM] * 8)(
        facts, own, *shares, *merge_parts
    )

    got = lax.all_to_all(routed.reshape(16, 16, wide), ("y", "t"), 0, 0, tiled=True)
    got = call(sum_kernel, shape((4, 16, wide)), [VMEM])(got.reshape(4, 4, 16, wide))
    other = around(got, "c", 1)
    routed = call(select_kernel, shape((8, 16, wide)), [SMEM, VMEM, VMEM])(place, got, other)
    place, = call(order_kernel, [shape((3,), I32)], [SMEM, pl.ANY], tail=(SMEM,))(place, routed)
    place, near_half, tokens = lax.optimization_barrier((place, near_half, tokens))
    halves = [None] + [around(near_half, "t", by) for by in (1, 3)]
    pieces = [tokens] + [around(tokens, "t", by) for by in range(1, 4)]
    got = lax.all_to_all(routed, "z", 0, 0, tiled=True)
    got = call(join_kernel, shape((16, wide)), [VMEM])(got)
    rows = [got] + [around(got, "t", by) for by in range(1, 4)]
    own_tokens = jnp.zeros((4, BLOCK, local_width), BF)
    for by, piece in enumerate(pieces):
        own_tokens = lax.dynamic_update_index_in_dim(own_tokens, piece, (t - by) % 4, 0)
    own_tokens = own_tokens.transpose(1, 0, 2).reshape(BLOCK, width)
    heads = call(
        project_kernel,
        shape((4, 3, HEAD, BLOCK)),
        [SMEM] + [VMEM] * 6,
    )(place, *rows, own_tokens, text_qkv.transpose(1, 2, 0))
    heads, late_tokens, near_half = lax.optimization_barrier((heads, own_tokens, near_half))
    halves[0] = around(near_half, "t", 2)
    mine = lax.all_to_all(heads, "y", 0, 0, tiled=True)
    prompt_in = call(place_kernel, shape((BLOCK, width)), [SMEM] + [VMEM] * 5)(
        place, *rows, late_tokens
    )
    pair = mine[:, 1:]
    near, far = ahead(pair, "z", 1), ahead(pair, "z", 2)
    others = [around(x, "c", 1) for x in (pair, near, far)]
    halves = halves + [around(x, "c", 1) for x in halves]
    sent = call(
        attend_kernel,
        shape((4, 4, HEAD, BLOCK)),
        [SMEM, SMEM] + [VMEM] * 6,
        limit=16,
    )(place, prompt_lengths, mine, near, far, *others)
    context = lax.all_to_all(sent.reshape(16, HEAD, BLOCK), ("t", "y"), 0, 0, tiled=True)
    return call(output_kernel, shape((BLOCK, width)), [SMEM] + [VMEM] * 9)(
        place, context.reshape(4, 2, half, BLOCK), text_out, *halves, prompt_in
    )


def solution(mesh):
    split = Mesh(np.asarray(mesh.devices).reshape(8, 4, 2, 4), ("z", "y", "c", "t"))
    seq = ("z", "y", "c")
    placed = (
        P(seq, None, None),
        P(seq, None),
        P(None, None, "t"),
        P("t", None),
        P("t", None, None),
        P(seq),
        P(seq),
        P(seq, "t"),
        P(),
        P(None, None, "t"),
        P("t", None),
    )
    return jax.shard_map(
        local, mesh=split, in_specs=placed, out_specs=P(seq, None), check_vma=False
    )
```
